128 devices in a mesh: enc: 16 (over y, x), abs: 8 (over z, core).
Axes of the slice: x: 4, y: 4, z: 4, core: 2. Of those that a mesh axis runs over, the one named last changes fastest.
Arguments:
- tiles: bfloat16 [768, 24, 24, 1024], P('enc', None, None, 'abs'), may hold values from -6 to 6
- w_in: bfloat16 [1024, 1024], replicated, may hold values from -0.1875 to 0.1875
- w_out: bfloat16 [1024, 1024], replicated, may hold values from -0.1875 to 0.1875
- se_down: bfloat16 [1024, 256], replicated, may hold values from -0.1875 to 0.1875
- se_up: bfloat16 [256, 1024], replicated, may hold values from -0.375 to 0.375
- kernel: bfloat16 [9, 1024], replicated, may hold values from -2 to 2
- gain: bfloat16 [1024], replicated, may hold values from 0.5 to 1.5
- token_grads: bfloat16 [1280, 144, 1024], P(('enc', 'abs')), may hold values from -6 to 6
- tile_counts: int32 [16, 16], replicated, may hold values from 1 to 9, as said below
- sample_owner: int32 [16, 16], replicated, may hold values from 0 to 15, as said below
- sample_rank: int32 [16, 16], replicated, may hold values from 0 to 15, as said below
Outputs:
- visual: bfloat16 [1280, 144, 1024], P(('enc', 'abs'))
- tile_grads: bfloat16 [768, 24, 24, 1024], P('enc', None, None, 'abs')
- w_in_grad: float32 [1024, 1024], P(('enc', 'abs'))
- w_out_grad: float32 [1024, 1024], P(('enc', 'abs'))
- se_down_grad: float32 [1024, 256], P(('enc', 'abs'))
- se_up_grad: float32 [256, 1024], P(('enc', 'abs'))
- kernel_grad: float32 [9, 1024], P(None, ('enc', 'abs'))
- gain_grad: float32 [1024], P(('enc', 'abs'))
The draws below stay inside these ranges and needn't reach their ends.
Inputs may be any that keep to these rules, and one draw needn't show every extreme that they name: `tile_counts`: the samples of every encoder group hold 48 tiles together; the samples owned by one abstractor group hold at most 80 tiles together. `sample_owner`: every row names each abstractor group once. `sample_rank`: the 16 samples owned by one abstractor group have distinct ranks.
All inputs are finite; a program needn't handle non-finite values.
Results may differ from the reference program's by a relative error of at most 0.0066.
Values may be sent and summed in bfloat16 or wider, within the bound.
No kernel may reach another device: no remote copies, remote signals or barrier semaphores. Data moves between devices by JAX's collectives and lax.ppermute only.
A program may use at most 192 MiB of HBM per device.

```python
import math
import jax
import jax.numpy as jnp
from jax import lax

D = 1024
R = 256
GRID = 24
P_SIZE = 144
TILES_E = 48
TILES = 768
OWN_CAP = 80
SLOTS = 1280
N_ENC = 16


def routing_tables(key):
    groups = N_ENC
    half = groups // 2
    keys = jax.random.split(jax.random.fold_in(key, 31), 6)
    spread = jax.random.randint(keys[0], (half // 2,), 0, 5).astype(jnp.int32)
    spread = spread.at[0].set(4)
    heavy_counts = jnp.concatenate([5 + spread, 5 - spread])
    heavy_counts = heavy_counts[jax.random.permutation(keys[1], half)]
    owner_order = jax.random.permutation(keys[2], groups)
    heavy_index = jnp.argsort(owner_order).astype(jnp.int32)
    shifts = (jax.random.permutation(keys[3], groups) % half).astype(jnp.int32)
    owners = jax.vmap(lambda sub: jax.random.permutation(sub, groups))(jax.random.split(keys[4], groups)).astype(jnp.int32)
    place = heavy_index[owners]
    counts = jnp.where(place < half, heavy_counts[(shifts[:, None] + place) % half], 1).astype(jnp.int32)
    orders = jax.vmap(lambda sub: jax.random.permutation(sub, groups))(jax.random.split(keys[5], groups)).astype(jnp.int32)
    ranks = orders[owners, jnp.arange(groups, dtype=jnp.int32)[:, None]].astype(jnp.int32)
    return (counts, owners, ranks)


def draw_tile_counts(key, part):
    return routing_tables(key)[0]


def draw_sample_owner(key, part):
    return routing_tables(key)[1]


def draw_sample_rank(key, part):
    return routing_tables(key)[2]


def levels(rng, dims, pieces, low, top_value):
    level, own = 1.0, jax.random.fold_in(rng, 6)
    for dim, shards_of in pieces:
        heights = jnp.exp(jax.random.uniform(jax.random.fold_in(own, dim), (shards_of,), jnp.float32, low / len(pieces), top_value / len(pieces)))
        level = level * jnp.repeat(heights, dims[dim] // shards_of).reshape([-1 if axis == dim else 1 for axis in range(len(dims))])
    return level


def bell_draw(stream_key, shape, deviation, limit, cuts=(), held_as=jnp.bfloat16):
    drawn = jax.random.normal(stream_key, shape, jnp.float32) * deviation
    if len(cuts) > 0:
        drawn = levels(stream_key, shape, cuts, -0.22, 0.18) * drawn
    return jnp.clip(drawn, min=-limit, max=limit).astype(held_as)


def setup_inputs(seed: int = 0) -> dict:
    key_of = jax.random.split(jax.random.key(seed), 12)
    return {
        "tiles": bell_draw(key_of[0], (TILES, GRID, GRID, D), 1.0, 6.0, ((0, 16), (3, 8))),
        "w_in": bell_draw(key_of[1], (D, D), D ** -0.5, 0.1875),
        "w_out": bell_draw(key_of[2], (D, D), D ** -0.5, 0.1875),
        "se_down": bell_draw(key_of[3], (D, R), D ** -0.5, 0.1875),
        "se_up": bell_draw(key_of[4], (R, D), R ** -0.5, 0.375),
        "kernel": bell_draw(key_of[5], (9, D), 9 ** -0.5, 2.0),
        "gain": jnp.clip(1.0 + 0.1 * jax.random.normal(key_of[6], (D,), jnp.float32), 0.5, 1.5).astype(jnp.bfloat16),
        "token_grads": bell_draw(key_of[7], (SLOTS, P_SIZE, D), 1.0, 6.0, ((0, 128),)),
        "tile_counts": draw_tile_counts(jax.random.fold_in(key_of[11], 71), 0),
        "sample_owner": draw_sample_owner(jax.random.fold_in(key_of[11], 71), 0),
        "sample_rank": draw_sample_rank(jax.random.fold_in(key_of[11], 71), 0),
    }


NORM_EPS = 1e-06

def route_tables(counts, owners, ranks):
    groups = counts.shape[0]
    start = jnp.cumsum(counts, axis=1, dtype=jnp.int32) - counts
    flat_counts = counts.reshape(-1)
    flat_owners = owners.reshape(-1)
    flat_ranks = ranks.reshape(-1)
    ahead = (flat_owners[:, None] == flat_owners[None, :]) & (flat_ranks[None, :] < flat_ranks[:, None])
    offset = lax.optimization_barrier(jnp.sum(jnp.where(ahead, flat_counts[None, :], 0), axis=1, dtype=jnp.int32)).reshape(groups, groups)
    owner_axis = jnp.arange(groups, dtype=jnp.int32)
    filled = lax.optimization_barrier(jnp.sum(jnp.where(flat_owners[None, :] == owner_axis[:, None], flat_counts[None, :], 0), axis=1, dtype=jnp.int32))
    return (start, offset, filled)

def pool_tiles(raw):
    count, grid, channels = (raw.shape[0], raw.shape[1], raw.shape[3])
    side = grid // 2
    wide = raw.astype(jnp.float32).reshape(count, side, 2, side, 2, channels)
    pooled = (lax.optimization_barrier(jnp.sum(wide, axis=(2, 4))) * 0.25).astype(jnp.bfloat16)
    return pooled.reshape(count, side * side, channels)

def spread_back(grads, grid):
    count, cells, channels = grads.shape
    side = grid // 2
    quarter = (grads.astype(jnp.float32) * 0.25).reshape(count, side, 1, side, 1, channels)
    whole = jnp.broadcast_to(quarter, (count, side, 2, side, 2, channels))
    return whole.reshape(count, grid, grid, channels).astype(jnp.bfloat16)

def depthwise(field, taps, side):
    count, cells, channels = field.shape
    plane = field.reshape(count, side, side, channels)
    padded = jnp.pad(plane, ((0, 0), (1, 1), (1, 1), (0, 0)))
    result = jnp.zeros_like(plane)
    for row_tap in range(3):
        for col_tap in range(3):
            result = result + taps[3 * row_tap + col_tap] * padded[:, row_tap:row_tap + side, col_tap:col_tap + side, :]
    return result.reshape(count, cells, channels)

def depthwise_back(back, taps, side):
    count, cells, channels = back.shape
    plane = back.reshape(count, side, side, channels)
    padded = jnp.pad(plane, ((0, 0), (1, 1), (1, 1), (0, 0)))
    result = jnp.zeros_like(plane)
    for row_tap in range(3):
        for col_tap in range(3):
            result = result + taps[3 * row_tap + col_tap] * padded[:, 2 - row_tap:2 - row_tap + side, 2 - col_tap:2 - col_tap + side, :]
    return result.reshape(count, cells, channels)

def kernel_terms(back, activated, side):
    count, cells, channels = back.shape
    plane = back.reshape(count, side, side, channels)
    padded = jnp.pad(activated.reshape(count, side, side, channels), ((0, 0), (1, 1), (1, 1), (0, 0)))
    rows_out = []
    for row_tap in range(3):
        for col_tap in range(3):
            window = padded[:, row_tap:row_tap + side, col_tap:col_tap + side, :]
            rows_out.append(lax.optimization_barrier(jnp.sum(plane * window, axis=(0, 1, 2))))
    return jnp.stack(rows_out, axis=0)

def silu_slope(value):
    sig = jax.nn.sigmoid(value)
    return sig * (1.0 + value * (1.0 - sig))

def block_forward(pooled, w_in, w_out, se_down, se_up, kernel, gain):
    count, cells, width = pooled.shape
    side = math.isqrt(cells)
    wide = pooled.astype(jnp.float32)
    average = lax.optimization_barrier(jnp.mean(wide, axis=-1, keepdims=True))
    centred = wide - average
    variance = lax.optimization_barrier(jnp.mean(centred * centred, axis=-1, keepdims=True))
    inverse = lax.rsqrt(variance + NORM_EPS)
    standard = centred * inverse
    normed = (standard * gain.astype(jnp.float32)).astype(jnp.bfloat16)
    hidden = jnp.dot(normed.reshape(-1, width), w_in, preferred_element_type=jnp.float32).reshape(count, cells, width)
    activated = jax.nn.silu(hidden)
    spatial = depthwise(activated, kernel.astype(jnp.float32), side)
    mixed = jax.nn.silu(spatial)
    squeeze = lax.optimization_barrier(jnp.mean(mixed, axis=1))
    squeeze_pre = jnp.dot(squeeze, se_down.astype(jnp.float32), precision=lax.Precision.HIGHEST)
    squeeze_act = jax.nn.silu(squeeze_pre)
    excite = jax.nn.sigmoid(jnp.dot(squeeze_act, se_up.astype(jnp.float32), precision=lax.Precision.HIGHEST))
    scaled = (mixed * excite[:, None, :]).astype(jnp.bfloat16)
    output = jnp.dot(scaled.reshape(-1, width), w_out, preferred_element_type=jnp.float32).reshape(count, cells, width)
    block = (wide + output).astype(jnp.bfloat16)
    saved = (standard, inverse, normed, hidden, activated, spatial, mixed, squeeze, squeeze_pre, squeeze_act, excite, scaled)
    return (block, saved)

def block_backward(saved, upstream, w_in, w_out, se_down, se_up, kernel, gain):
    standard, inverse, normed, hidden, activated, spatial, mixed, squeeze, squeeze_pre, squeeze_act, excite, scaled = saved
    count, cells, width = upstream.shape
    side = math.isqrt(cells)
    flat_up = upstream.reshape(-1, width)
    w_out_term = jnp.dot(scaled.reshape(-1, width).T, flat_up, preferred_element_type=jnp.float32)
    back_scaled = jnp.dot(flat_up, w_out.T, preferred_element_type=jnp.float32).reshape(count, cells, width)
    back_excite = lax.optimization_barrier(jnp.sum(back_scaled * mixed, axis=1))
    back_pre = back_excite * excite * (1.0 - excite)
    se_up_term = jnp.dot(squeeze_act.T, back_pre, precision=lax.Precision.HIGHEST)
    back_squeeze_act = jnp.dot(back_pre, se_up.astype(jnp.float32).T, precision=lax.Precision.HIGHEST)
    back_squeeze_pre = back_squeeze_act * silu_slope(squeeze_pre)
    se_down_term = jnp.dot(squeeze.T, back_squeeze_pre, precision=lax.Precision.HIGHEST)
    back_squeeze = jnp.dot(back_squeeze_pre, se_down.astype(jnp.float32).T, precision=lax.Precision.HIGHEST)
    back_mixed = back_scaled * excite[:, None, :] + back_squeeze[:, None, :] / cells
    back_spatial = back_mixed * silu_slope(spatial)
    kernel_term = kernel_terms(back_spatial, activated, side)
    back_act = depthwise_back(back_spatial, kernel.astype(jnp.float32), side)
    back_hidden = (back_act * silu_slope(hidden)).astype(jnp.bfloat16)
    flat_hidden = back_hidden.reshape(-1, width)
    w_in_term = jnp.dot(normed.reshape(-1, width).T, flat_hidden, preferred_element_type=jnp.float32)
    back_normed = jnp.dot(flat_hidden, w_in.T, preferred_element_type=jnp.float32).reshape(count, cells, width)
    gain_term = lax.optimization_barrier(jnp.sum(back_normed * standard, axis=(0, 1)))
    back_x = back_normed * gain.astype(jnp.float32)
    centre_term = lax.optimization_barrier(jnp.mean(back_x, axis=-1, keepdims=True))
    along_term = lax.optimization_barrier(jnp.mean(back_x * standard, axis=-1, keepdims=True))
    back_pooled = upstream.astype(jnp.float32) + inverse * (back_x - centre_term - standard * along_term)
    terms = (w_in_term, w_out_term, se_down_term, se_up_term, kernel_term, gain_term)
    return (back_pooled.astype(jnp.bfloat16), terms)

def reference(tiles, w_in, w_out, se_down, se_up, kernel, gain, token_grads, tile_counts, sample_owner, sample_rank):
    groups = N_ENC
    start, offset, filled = route_tables(tile_counts, sample_owner, sample_rank)
    tile_index = jnp.arange(TILES_E, dtype=jnp.int32)
    sample_axis = jnp.arange(groups, dtype=jnp.int32)
    member = lax.optimization_barrier(jnp.sum((start[:, None, :] <= tile_index[None, :, None]).astype(jnp.int32), axis=2, dtype=jnp.int32)) - 1
    pick = member[:, :, None] == sample_axis[None, None, :]
    owner_of = lax.optimization_barrier(jnp.sum(jnp.where(pick, sample_owner[:, None, :], 0), axis=2, dtype=jnp.int32))
    start_of = lax.optimization_barrier(jnp.sum(jnp.where(pick, start[:, None, :], 0), axis=2, dtype=jnp.int32))
    offset_of = lax.optimization_barrier(jnp.sum(jnp.where(pick, offset[:, None, :], 0), axis=2, dtype=jnp.int32))
    slots = (owner_of * OWN_CAP + offset_of + tile_index[None, :] - start_of).astype(jnp.int32)
    raw = tiles.reshape(groups, TILES_E, GRID, GRID, D)
    init = (jnp.zeros((D, D), jnp.float32), jnp.zeros((D, D), jnp.float32), jnp.zeros((D, R), jnp.float32), jnp.zeros((R, D), jnp.float32), jnp.zeros((9, D), jnp.float32), jnp.zeros((D,), jnp.float32))

    def group_step(totals, inputs):
        raw_group, slot_group = inputs
        pooled = pool_tiles(raw_group)
        upstream = jnp.take(token_grads, slot_group, axis=0)
        block, saved = block_forward(pooled, w_in, w_out, se_down, se_up, kernel, gain)
        back_pooled, terms = block_backward(saved, upstream, w_in, w_out, se_down, se_up, kernel, gain)
        totals = jax.tree.map(lambda left, right: left + right, totals, terms)
        return (totals, (block, spread_back(back_pooled, GRID)))
    totals, (blocks, tile_back) = lax.scan(group_step, init, (raw, slots))
    visual = jnp.zeros((SLOTS, P_SIZE, D), jnp.bfloat16).at[slots.reshape(-1)].set(blocks.reshape(-1, P_SIZE, D))
    scale = 1.0 / math.sqrt(N_ENC * TILES_E * P_SIZE)
    return (visual, tile_back.reshape(TILES, GRID, GRID, D), totals[0] * scale, totals[1] * scale, totals[2] * scale, totals[3] * scale, totals[4] * scale, totals[5] * scale)
```

```python
import functools
import math

import jax
import jax.numpy as jnp
from jax import lax
from jax.experimental import pallas as pl
from jax.experimental.pallas import tpu as pltpu
from jax.sharding import PartitionSpec as P

F32 = jnp.float32
BF16 = jnp.bfloat16
NORM_EPS = 1e-06
LANES = 128
PAD = 16
CHUNKS = 2
VMEM_BYTES = 60 * 1024 * 1024
ANY = pl.BlockSpec(memory_space=pl.ANY)
SMEM = pl.BlockSpec(memory_space=pltpu.SMEM)
VMEM = pl.BlockSpec(memory_space=pltpu.VMEM)


def params(**more):
    return pltpu.CompilerParams(vmem_limit_bytes=VMEM_BYTES, **more)


def pool_kernel(steps, per, own_ref, pos_ref, tiles_ref, *rest):
    outs, (wide, pooled, sem) = rest[:CHUNKS], rest[CHUNKS:]
    step = pl.program_id(0)
    side = tiles_ref.shape[1] // 2
    width = 2 * side
    slots = outs[0].shape[1]
    for n in range(per):
        for row in range(side):
            pair = tiles_ref[n, 2 * row].astype(F32) + tiles_ref[n, 2 * row + 1].astype(F32)
            wide[pl.ds(row * width, width), :] = pair
        total = wide[pl.ds(0, side * side, stride=2), :] + wide[pl.ds(1, side * side, stride=2), :]
        j = step * per + n
        pooled[j] = (total * 0.25).astype(BF16)
        position = pos_ref[j]
        for h in range(CHUNKS):

            @pl.when(position // slots == h)
            def _(h=h):
                pltpu.make_async_copy(
                    pooled.at[j], outs[h].at[own_ref[j], position - h * slots], sem
                ).start()

    @pl.when(step == steps - 1)
    def _():
        @pl.loop(0, steps * per)
        def _(j):
            pltpu.make_async_copy(pooled.at[0], outs[0].at[0, 0], sem).wait()


def pool_and_pack(tiles, own, pos, groups, slots):
    count, grid, _, channels = tiles.shape
    cells = grid * grid // 4
    per = 4
    steps = count // per
    made = jax.ShapeDtypeStruct((groups, slots, cells, channels), BF16)
    return pl.pallas_call(
        functools.partial(pool_kernel, steps, per),
        grid=(steps,),
        in_specs=[SMEM, SMEM, pl.BlockSpec((per, grid, grid, channels), lambda i: (i, 0, 0, 0))],
        out_specs=[ANY] * CHUNKS,
        out_shape=[made] * CHUNKS,
        scratch_shapes=[
            pltpu.VMEM((grid * grid // 2, channels), F32),
            pltpu.VMEM((count, cells, channels), BF16),
            pltpu.SemaphoreType.DMA,
        ],
        compiler_params=params(),
        cost_estimate=pl.CostEstimate(flops=tiles.size, bytes_accessed=tiles.size * 3, transcendentals=0),
        name="pool_and_pack",
    )(own, pos, tiles)


def route_kernel(chunk, slots, per, columns, back, table_ref, filled_ref, src, dst, sem):
    filled = filled_ref[0]

    def copy(n):
        column, local = n // slots, n % slots
        q = column * per + chunk * slots + local
        group = table_ref[q]
        if back:
            one = pltpu.make_async_copy(src.at[column, local], dst.at[group, local], sem)
        else:
            one = pltpu.make_async_copy(src.at[group, local], dst.at[column, local], sem)
        return q, one

    @pl.loop(0, columns * slots)
    def _(n):
        q, one = copy(n)

        @pl.when(q < filled)
        def _():
            one.start()

    @pl.loop(0, columns * slots)
    def _(n):
        q, one = copy(n)

        @pl.when(q < filled)
        def _():
            one.wait()


def route(source, table, filled, chunk, per, columns, groups, back):
    slots, cells, channels = source.shape[1:]
    lead = groups if back else columns
    return pl.pallas_call(
        functools.partial(route_kernel, chunk, slots, per, columns, back),
        in_specs=[SMEM, SMEM, ANY],
        out_specs=ANY,
        out_shape=jax.ShapeDtypeStruct((lead, slots, cells, channels), BF16),
        scratch_shapes=[pltpu.SemaphoreType.DMA],
        compiler_params=params(),
        cost_estimate=pl.CostEstimate(
            flops=0, bytes_accessed=4 * columns * slots * cells * channels, transcendentals=0
        ),
        name="route_back" if back else "route_in",
    )(table, filled, source)


def exact_dot(left, weights):
    rows = left.shape[0]
    first = left.astype(BF16).astype(F32)
    rest = left - first
    second = rest.astype(BF16).astype(F32)
    third = rest - second
    stacked = jnp.concatenate([first, second, third, jnp.zeros_like(left)], axis=0).astype(BF16)
    made = jnp.dot(stacked, weights, preferred_element_type=F32)
    return made[:rows] + made[rows : 2 * rows] + made[2 * rows : 3 * rows]


def block_kernel(
    chunk,
    side,
    live_ref,
    x_hbm,
    up_hbm,
    w_in_hbm,
    w_out_hbm,
    w_in_t_hbm,
    w_out_t_hbm,
    se_down,
    se_up,
    se_down_t,
    se_up_t,
    taps,
    gain,
    *rest,
):
    (vis_hbm, normed_hbm, scaled_hbm, hidden_hbm, back_hbm, small_a, small_b, small_k) = rest[-25:-17]
    (
        x,
        up,
        w_in,
        w_out,
        w_in_t,
        w_out_t,
        standard,
        inverse,
        slope_h,
        act,
        mixed,
        slope_s,
        wide,
        tmp,
        masks,
        stage,
        sem,
    ) = rest[-17:]
    (rows_v, squeeze, excite, extra, kacc, gacc, normed, scaled, vis) = stage
    blocks, tiles, cells, lanes = x.shape
    width = blocks * lanes
    flat = tiles * cells
    loads = [
        pltpu.make_async_copy(a, b, sem.at[n])
        for n, (a, b) in enumerate(
            [
                (x_hbm, x),
                (w_in_hbm, w_in),
                (up_hbm.at[pl.ds(chunk * tiles, tiles)], up),
                (w_out_hbm, w_out),
                (w_out_t_hbm, w_out_t),
                (w_in_t_hbm, w_in_t),
            ]
        )
    ]
    for one in loads:
        one.start()

    column = lax.rem(lax.broadcasted_iota(jnp.int32, (cells, lanes), 0), side)
    masks[0] = jnp.where(column != 0, 1.0, 0.0).astype(F32)
    masks[1] = jnp.where(column != side - 1, 1.0, 0.0).astype(F32)
    edge = jnp.zeros((PAD, lanes), F32)
    tmp[pl.ds(0, PAD), :] = edge
    tmp[pl.ds(PAD + cells, PAD), :] = edge
    kacc[...] = jnp.zeros_like(kacc)
    gacc[...] = jnp.zeros_like(gacc)
    squeeze[...] = jnp.zeros_like(squeeze)
    extra[...] = jnp.zeros_like(extra)

    @pl.loop(0, blocks * tiles)
    def _(n):
        c, t = n % blocks, n // blocks
        act[c, t, pl.ds(0, PAD), :] = edge
        act[c, t, pl.ds(PAD + cells, PAD), :] = edge

    loads[0].wait()
    loads[2].wait()
    for t in range(tiles):

        @pl.when(chunk * tiles + t >= live_ref[0])
        def _(t=t):
            up[t] = jnp.zeros(up.shape[1:], BF16)
            for c in range(blocks):
                x[c, t] = jnp.zeros((cells, lanes), BF16)

    @pl.loop(0, tiles)
    def _(t):
        total = x[0, t].astype(F32)
        for c in range(1, blocks):
            total = total + x[c, t].astype(F32)
        average = jnp.sum(total, axis=1, keepdims=True) * (1.0 / width)
        square = jnp.zeros((cells, lanes), F32)
        for c in range(blocks):
            centred = x[c, t].astype(F32) - average
            square = square + centred * centred
        variance = jnp.sum(square, axis=1, keepdims=True) * (1.0 / width)
        inv = lax.rsqrt(variance + NORM_EPS)
        inverse[t] = jnp.broadcast_to(inv, (cells, lanes))
        for c in range(blocks):
            std = (x[c, t].astype(F32) - average) * inv
            standard[c, t] = std
            normed[t, :, c * lanes : (c + 1) * lanes] = (std * gain[c, 0:1, :]).astype(BF16)

    def product(left, right, put):
        wide_n = 256
        value = left[...].reshape(flat, width)
        for n in range(width // wide_n):
            made = jnp.dot(value, right[:, n * wide_n : (n + 1) * wide_n], preferred_element_type=F32)
            for half in range(wide_n // lanes):
                c = n * (wide_n // lanes) + half
                put(c, made[:, half * lanes : (half + 1) * lanes].reshape(tiles, cells, lanes))

    def put_hidden(c, value):
        slope_h[c] = value

    loads[1].wait()
    product(normed, w_in, put_hidden)
    save_normed = pltpu.make_async_copy(normed, normed_hbm.at[pl.ds(chunk * tiles, tiles)], sem.at[6])
    save_normed.start()

    @pl.loop(0, blocks * tiles)
    def _(n):
        c, t = n % blocks, n // blocks
        h = slope_h[c, t]
        sig = jax.nn.sigmoid(h)
        a = h * sig
        slope_h[c, t] = sig * (1.0 + h * (1.0 - sig))
        act[c, t, pl.ds(PAD, cells), :] = a

        def column_sum(b):
            made = None
            for r in range(3):
                term = taps[c, 3 * r + b : 3 * r + b + 1, :] * act[c, t, pl.ds(PAD + side * (r - 1) + b - 1, cells), :]
                made = term if made is None else made + term
            return made

        spatial = column_sum(1) + masks[0] * column_sum(0) + masks[1] * column_sum(2)
        sig = jax.nn.sigmoid(spatial)
        mix = spatial * sig
        mixed[c, t] = mix
        slope_s[c, t] = sig * (1.0 + spatial * (1.0 - sig))
        squeeze[c, pl.ds(t, 1), :] = jnp.sum(mix, axis=0, keepdims=True) * (1.0 / cells)

    def joined(ref):
        return jnp.concatenate([ref[c] for c in range(blocks)], axis=1)

    squeezed = joined(squeeze)
    squeeze_pre = exact_dot(squeezed, se_down[...])
    sig_pre = jax.nn.sigmoid(squeeze_pre)
    squeeze_act = squeeze_pre * sig_pre
    excited = jax.nn.sigmoid(exact_dot(squeeze_act, se_up[...]))
    for c in range(blocks):
        excite[c] = excited[:, c * lanes : (c + 1) * lanes]

    def put_back(c, value):
        wide[c] = value

    loads[4].wait()
    product(up, w_out_t, put_back)

    @pl.loop(0, tiles)
    def _(t):
        for c in range(blocks):
            mix = mixed[c, t]
            scaled[t, :, c * lanes : (c + 1) * lanes] = (mix * excite[c, pl.ds(t, 1), :]).astype(BF16)
            extra[c, pl.ds(t, 1), :] = jnp.sum(wide[c, t] * mix, axis=0, keepdims=True)

    back_pre = joined(extra) * excited * (1.0 - excited)
    back_squeeze_pre = exact_dot(back_pre, se_up_t[...]) * (
        sig_pre * (1.0 + squeeze_pre * (1.0 - sig_pre))
    )
    back_squeeze = exact_dot(back_squeeze_pre, se_down_t[...]) * (1.0 / cells)
    for c in range(blocks):
        extra[c] = back_squeeze[:, c * lanes : (c + 1) * lanes]
    small_a[0] = squeezed
    small_a[1] = back_pre
    small_b[0] = back_squeeze_pre
    small_b[1] = squeeze_act

    def put_visual(c, value):
        vis[:, :, c * lanes : (c + 1) * lanes] = (x[c].astype(F32) + value).astype(BF16)

    loads[3].wait()
    product(scaled, w_out, put_visual)
    save_scaled = pltpu.make_async_copy(scaled, scaled_hbm.at[pl.ds(chunk * tiles, tiles)], sem.at[7])
    save_scaled.start()
    save_vis = pltpu.make_async_copy(vis, vis_hbm.at[pl.ds(chunk * tiles, tiles)], sem.at[8])
    save_vis.start()
    save_normed.wait()

    @pl.loop(0, tiles)
    def _(t):
        for c in range(blocks):
            back = (wide[c, t] * excite[c, pl.ds(t, 1), :] + extra[c, pl.ds(t, 1), :]) * slope_s[c, t]
            tmp[pl.ds(PAD, cells), :] = back
            sides = (back * masks[0], back, back * masks[1])
            for r in range(3):
                for b in range(3):
                    term = sides[b] * act[c, t, pl.ds(PAD + side * (r - 1) + b - 1, cells), :]
                    kacc[c, 3 * r + b] += jnp.sum(term.reshape(cells // 8, 8, lanes), axis=0)

            def column_sum(b, c=c):
                made = None
                for r in range(3):
                    term = taps[c, 3 * r + b : 3 * r + b + 1, :] * tmp[pl.ds(PAD - side * (r - 1) - (b - 1), cells), :]
                    made = term if made is None else made + term
                return made

            back_act = column_sum(1) + masks[1] * column_sum(0) + masks[0] * column_sum(2)
            normed[t, :, c * lanes : (c + 1) * lanes] = (back_act * slope_h[c, t]).astype(BF16)

    loads[5].wait()
    product(normed, w_in_t, put_back)
    save_hidden = pltpu.make_async_copy(normed, hidden_hbm.at[pl.ds(chunk * tiles, tiles)], sem.at[9])
    save_hidden.start()

    @pl.loop(0, tiles)
    def _(t):
        centre = jnp.zeros((cells, lanes), F32)
        along = jnp.zeros((cells, lanes), F32)
        for c in range(blocks):
            along_n = wide[c, t] * standard[c, t]
            gacc[c] += jnp.sum(along_n.reshape(cells // 8, 8, lanes), axis=0)
            centre = centre + wide[c, t] * gain[c, 0:1, :]
            along = along + along_n * gain[c, 0:1, :]
        centre = jnp.sum(centre, axis=1, keepdims=True) * (1.0 / width)
        along = jnp.sum(along, axis=1, keepdims=True) * (1.0 / width)
        inv = inverse[t]
        for c in range(blocks):
            made = up[t, :, c * lanes : (c + 1) * lanes].astype(F32) + inv * (
                wide[c, t] * gain[c, 0:1, :] - centre - standard[c, t] * along
            )
            rows_v[c, t] = made.astype(BF16)

    save_back = pltpu.make_async_copy(rows_v, back_hbm, sem.at[10])
    save_back.start()
    small_k[...] = jnp.zeros_like(small_k)
    for c in range(blocks):
        for r in range(9):
            small_k[r : r + 1, c * lanes : (c + 1) * lanes] = jnp.sum(kacc[c, r], axis=0, keepdims=True)
        small_k[9:10, c * lanes : (c + 1) * lanes] = jnp.sum(gacc[c], axis=0, keepdims=True)
    save_scaled.wait()
    save_vis.wait()
    save_hidden.wait()
    save_back.wait()


def run_block(chunk, side, live, x, up, weights, carried):
    blocks, tiles, cells, lanes = x.shape
    width = blocks * lanes
    narrow = weights[4].shape[1]
    whole = jax.ShapeDtypeStruct(up.shape, BF16)
    fixed = [live, x, up, *weights]
    field = pltpu.VMEM((blocks, tiles, cells, lanes), F32)
    packed = pltpu.VMEM((tiles, cells, width), BF16)
    eight = pltpu.VMEM((blocks, 8, lanes), F32)
    square = pltpu.VMEM((width, width), BF16)
    flops = 8 * tiles * cells * width * width
    return pl.pallas_call(
        functools.partial(block_kernel, chunk, side),
        in_specs=[SMEM] + [ANY] * 6 + [VMEM] * 6 + [ANY] * len(carried),
        out_specs=[ANY] * 5 + [VMEM] * 3,
        out_shape=[whole] * 4
        + [
            jax.ShapeDtypeStruct((blocks, tiles, cells, lanes), BF16),
            jax.ShapeDtypeStruct((2, 8, width), F32),
            jax.ShapeDtypeStruct((2, 8, narrow), F32),
            jax.ShapeDtypeStruct((16, width), F32),
        ],
        input_output_aliases={len(fixed) + n: n for n in range(len(carried))},
        scratch_shapes=[
            pltpu.VMEM((blocks, tiles, cells, lanes), BF16),
            packed,
            square,
            square,
            square,
            square,
            field,
            pltpu.VMEM((tiles, cells, lanes), F32),
            field,
            pltpu.VMEM((blocks, tiles, cells + 2 * PAD, lanes), F32),
            field,
            field,
            field,
            pltpu.VMEM((cells + 2 * PAD, lanes), F32),
            pltpu.VMEM((2, cells, lanes), F32),
            [
                pltpu.VMEM((blocks, tiles, cells, lanes), BF16),
                eight,
                eight,
                eight,
                pltpu.VMEM((blocks, 9, 8, lanes), F32),
                eight,
                packed,
                packed,
                packed,
            ],
            pltpu.SemaphoreType.DMA((11,)),
        ],
        compiler_params=params(),
        cost_estimate=pl.CostEstimate(
            flops=flops, bytes_accessed=8 * x.size * 2 + 8 * width * width, transcendentals=2 * x.size
        ),
        name="block_%d" % chunk,
    )(*fixed, *carried)


def weights_kernel(normed, scaled, hidden, up, rest_ref, out):
    count, cells, columns = normed.shape
    flat = count * cells
    width = hidden.shape[2]

    def product(left, right):
        return lax.dot_general(
            left[...].reshape(flat, columns),
            right[...].reshape(flat, width),
            (((0,), (0,)), ((), ())),
            preferred_element_type=F32,
        )

    for place, (left, right) in enumerate(((normed, hidden), (scaled, up))):
        made = product(left, right).astype(BF16)
        for group in range(2):
            for z in range(4):
                for core in range(2):
                    row = 8 * (8 * group + 2 * z + core)
                    out[core, z, group, :, place * width : (place + 1) * width] = made[row : row + 8]
    out[:, :, :, :, 2 * width :] = rest_ref[...]


def weight_terms(normed, scaled, hidden, up, others):
    count, cells, width = normed.shape
    columns = 128
    lanes = 2 * width + others.shape[-1]
    left = pl.BlockSpec((count, cells, columns), lambda i: (0, 0, i))
    right = pl.BlockSpec((count, cells, width), lambda i: (0, 0, 0), pipeline_mode=pl.Buffered(1))
    return pl.pallas_call(
        weights_kernel,
        grid=(width // columns,),
        in_specs=[
            left,
            left,
            right,
            right,
            pl.BlockSpec((2, 4, 2, 8, others.shape[-1]), lambda i: (0, 0, i, 0, 0)),
        ],
        out_specs=pl.BlockSpec((2, 4, 2, 8, lanes), lambda i: (0, 0, i, 0, 0)),
        out_shape=jax.ShapeDtypeStruct((2, 4, 16, 8, lanes), BF16),
        compiler_params=params(),
        cost_estimate=pl.CostEstimate(
            flops=4 * count * cells * width * width, bytes_accessed=8 * count * cells * width, transcendentals=0
        ),
        name="weight_terms",
    )(normed, scaled, hidden, up, others)


def spread_kernel(per, own_ref, pos_ref, *rest):
    arrived, out, (held, wide, sem) = rest[:CHUNKS], rest[CHUNKS], rest[CHUNKS + 1 :]
    step = pl.program_id(0)
    slots = arrived[0].shape[1]
    count = held.shape[0]
    side = out.shape[1] // 2
    width = 2 * side

    @pl.when(step == 0)
    def _():
        @pl.loop(0, count)
        def _(j):
            position = pos_ref[j]
            for h in range(CHUNKS):

                @pl.when(position // slots == h)
                def _(h=h):
                    pltpu.make_async_copy(
                        arrived[h].at[own_ref[j], position - h * slots], held.at[j], sem
                    ).start()

        @pl.loop(0, count)
        def _(j):
            pltpu.make_async_copy(arrived[0].at[0, 0], held.at[0], sem).wait()

    for n in range(per):
        quarter = held[step * per + n].astype(F32) * 0.25
        wide[pl.ds(0, side * side, stride=2), :] = quarter
        wide[pl.ds(1, side * side, stride=2), :] = quarter
        for row in range(side):
            line = wide[pl.ds(row * width, width), :].astype(BF16)
            out[n, 2 * row] = line
            out[n, 2 * row + 1] = line


def unpack_and_spread(arrived, own, pos, count, grid):
    _, _, cells, channels = arrived[0].shape
    per = 4
    return pl.pallas_call(
        functools.partial(spread_kernel, per),
        grid=(count // per,),
        in_specs=[SMEM, SMEM] + [ANY] * CHUNKS,
        out_specs=pl.BlockSpec((per, grid, grid, channels), lambda i: (i, 0, 0, 0)),
        out_shape=jax.ShapeDtypeStruct((count, grid, grid, channels), BF16),
        scratch_shapes=[
            pltpu.VMEM((count, cells, channels), BF16),
            pltpu.VMEM((grid * grid // 2, channels), F32),
            pltpu.SemaphoreType.DMA,
        ],
        compiler_params=params(),
        cost_estimate=pl.CostEstimate(
            flops=0, bytes_accessed=10 * count * cells * channels, transcendentals=0
        ),
        name="unpack_and_spread",
    )(own, pos, *arrived)


def before(table):
    groups = table.shape[1]
    index = jnp.arange(groups, dtype=jnp.int32)
    lower = index[None, :] < index[:, None]
    return jnp.sum(jnp.where(lower[None], table[:, None, :], 0), axis=2, dtype=jnp.int32)


def routing(counts, owners, ranks, group_id, local_tiles, capacity):
    groups = counts.shape[0]
    start = before(counts)
    flat_counts, flat_owners, flat_ranks = counts.reshape(-1), owners.reshape(-1), ranks.reshape(-1)
    ahead = (flat_owners[:, None] == flat_owners[None, :]) & (flat_ranks[None, :] < flat_ranks[:, None])
    offset = jnp.sum(jnp.where(ahead, flat_counts[None, :], 0), axis=1, dtype=jnp.int32).reshape(groups, groups)
    sources = jnp.arange(groups, dtype=jnp.int32)
    mine = (sources == group_id)[:, None]

    def row(table):
        return jnp.sum(jnp.where(mine, table, 0), axis=0, dtype=jnp.int32)

    owner_row, start_row, offset_row = row(owners), row(start), row(offset)
    ids = jnp.arange(local_tiles, dtype=jnp.int32)
    member = jnp.sum((start_row[None, :] <= ids[:, None]).astype(jnp.int32), axis=1, dtype=jnp.int32) - 1
    which = member[:, None] == sources[None, :]
    own = jnp.sum(jnp.where(which, owner_row[None, :], 0), axis=1, dtype=jnp.int32)
    slot = jnp.sum(jnp.where(which, (offset_row - start_row)[None, :], 0), axis=1, dtype=jnp.int32) + ids
    arriving = owners == group_id
    recv_count = jnp.sum(jnp.where(arriving, counts, 0), axis=1, dtype=jnp.int32)
    recv_offset = jnp.sum(jnp.where(arriving, offset, 0), axis=1, dtype=jnp.int32)
    positions = jnp.arange(capacity, dtype=jnp.int32)
    inside = (positions[:, None] >= recv_offset[None, :]) & (
        positions[:, None] < (recv_offset + recv_count)[None, :]
    )
    table = jnp.sum(jnp.where(inside, sources[None, :], 0), axis=1, dtype=jnp.int32)
    filled = jnp.sum(recv_count, dtype=jnp.int32).reshape(1)
    return own, slot, table, filled


def local(
    tiles,
    w_in,
    w_out,
    se_down,
    se_up,
    kernel,
    gain,
    token_grads,
    tile_counts,
    sample_owner,
    sample_rank,
):
    groups = lax.axis_size("enc")
    columns = lax.axis_size("abs")
    group_id = lax.axis_index("enc")
    column_id = lax.axis_index("abs")
    local_tiles, grid = tiles.shape[0], tiles.shape[1]
    per, cells, width = token_grads.shape
    narrow = se_down.shape[1]
    capacity = per * columns
    side = grid // 2
    slots = per // CHUNKS
    blocks = width // LANES
    own, slot, table, filled = routing(
        tile_counts, sample_owner, sample_rank, group_id, local_tiles, capacity
    )
    pos = slot % per
    live = jnp.clip(filled - column_id * per, 0, per)
    sends = pool_and_pack(tiles, own, pos, groups, slots)

    taps = jnp.pad(kernel.astype(F32).reshape(9, blocks, LANES).transpose(1, 0, 2), ((0, 0), (0, 7), (0, 0)))
    gains = jnp.broadcast_to(gain.astype(F32).reshape(blocks, 1, LANES), (blocks, 8, LANES))
    weights = [w_in, w_out, w_in.T, w_out.T, se_down, se_up, se_down.T, se_up.T, taps, gains]

    inner = []
    for h in range(CHUNKS):
        send = sends[h]
        if h > 0:
            send, _ = lax.optimization_barrier((send, received))
        received = lax.all_to_all(send, "enc", split_axis=0, concat_axis=0, tiled=True)
        compact = route(received, table, filled, h, per, columns, groups, False)
        inner.append(lax.all_to_all(compact, "abs", split_axis=0, concat_axis=0, tiled=True))

    carried = []
    arrived, small = [], []
    for h in range(CHUNKS):
        made = run_block(h, side, live, inner[h], token_grads, weights, carried)
        carried = list(made[:4])
        small.append(made[5:])
        narrowed = lax.all_to_all(made[4], "abs", split_axis=0, concat_axis=0, tiled=True)
        back = route(narrowed, table, filled, h, per, columns, groups, True)
        arrived.append(lax.all_to_all(back, "enc", split_axis=0, concat_axis=0, tiled=True))
    visual, normed, scaled, hidden = carried
    tile_grads = unpack_and_spread(arrived, own, pos, local_tiles, grid)

    rows_a = jnp.concatenate([s[0] for s in small], axis=1)
    rows_b = jnp.concatenate([s[1] for s in small], axis=1)
    high = lax.Precision.HIGHEST
    down = jnp.dot(rows_a[0].T, rows_b[0], precision=high)
    up = jnp.dot(rows_b[1].T, rows_a[1], precision=high)
    both = sum(s[2] for s in small)[:10]
    devices = groups * columns
    down = down.reshape(devices, 8, narrow)
    up = up.reshape(devices, 8, narrow)
    both = both.reshape(10, devices, 8).transpose(1, 2, 0)
    both = jnp.pad(both, ((0, 0), (0, 0), (0, LANES - 10)))
    others = jnp.concatenate([down, up, both], axis=2).astype(BF16)
    others = others.reshape(groups, 4, 2, 8, -1).transpose(2, 1, 0, 3, 4)
    terms = weight_terms(normed, scaled, hidden, token_grads, others)

    core = column_id % 2
    away = jnp.where(core == 0, terms[1], terms[0])
    home = jnp.where(core == 0, terms[0], terms[1])
    near = lax.ppermute(away, "abs", [(n, n ^ 1) for n in range(columns)])
    pair = (home.astype(F32) + near.astype(F32)).astype(BF16)
    ring = [[2 * z + c for z in range(4)] for c in range(2)]
    column = lax.all_to_all(pair, "abs", split_axis=0, concat_axis=0, tiled=True, axis_index_groups=ring)
    column = jnp.sum(column.astype(F32), axis=0).astype(BF16)
    spread = lax.all_to_all(column, "enc", split_axis=0, concat_axis=0, tiled=True)
    scale = 1.0 / math.sqrt(groups * local_tiles * cells)
    total = jnp.sum(spread.astype(F32), axis=0) * scale
    w_in_grad = total[:, :width]
    w_out_grad = total[:, width : 2 * width]
    down_grad = total[:, 2 * width : 2 * width + narrow]
    up_grad = total[:, 2 * width + narrow : 2 * width + 2 * narrow].reshape(2, width)
    last = total[:, 2 * width + 2 * narrow : 2 * width + 2 * narrow + 10]
    return (
        visual,
        tile_grads,
        w_in_grad,
        w_out_grad,
        down_grad,
        up_grad,
        last[:, :9].T,
        last[:, 9],
    )


def solution(mesh):
    return jax.shard_map(
        local,
        mesh=mesh,
        in_specs=(
            P("enc", None, None, "abs"),
            P(),
            P(),
            P(),
            P(),
            P(),
            P(),
            P(("enc", "abs"), None, None),
            P(),
            P(),
            P(),
        ),
        out_specs=(
            P(("enc", "abs"), None, None),
            P("enc", None, None, "abs"),
            P(("enc", "abs"), None),
            P(("enc", "abs"), None),
            P(("enc", "abs"), None),
            P(("enc", "abs"), None),
            P(None, ("enc", "abs")),
            P(("enc", "abs")),
        ),
        check_vma=False,
    )
```

```python
import functools
import math

import jax
import jax.numpy as jnp
from jax import lax
from jax.experimental import pallas as pl
from jax.experimental.pallas import tpu as pltpu
from jax.sharding import PartitionSpec as P

F32 = jnp.float32
BF16 = jnp.bfloat16
NORM_EPS = 1e-06
LANES = 128
PAD = 16
CHUNKS = 2
VMEM_BYTES = 60 * 1024 * 1024
ANY = pl.BlockSpec(memory_space=pl.ANY)
SMEM = pl.BlockSpec(memory_space=pltpu.SMEM)
VMEM = pl.BlockSpec(memory_space=pltpu.VMEM)


def params(**more):
    return pltpu.CompilerParams(vmem_limit_bytes=VMEM_BYTES, **more)


def pool_kernel(steps, per, own_ref, pos_ref, tiles_ref, *rest):
    outs, (wide, pooled, sem) = rest[:CHUNKS], rest[CHUNKS:]
    step = pl.program_id(0)
    side = tiles_ref.shape[1] // 2
    width = 2 * side
    slots = outs[0].shape[1]
    for n in range(per):
        for row in range(side):
            pair = tiles_ref[n, 2 * row].astype(F32) + tiles_ref[n, 2 * row + 1].astype(F32)
            wide[pl.ds(row * width, width), :] = pair
        total = wide[pl.ds(0, side * side, stride=2), :] + wide[pl.ds(1, side * side, stride=2), :]
        j = step * per + n
        pooled[j] = (total * 0.25).astype(BF16)
        position = pos_ref[j]
        for h in range(CHUNKS):

            @pl.when(position // slots == h)
            def _(h=h):
                pltpu.make_async_copy(
                    pooled.at[j], outs[h].at[own_ref[j], position - h * slots], sem
                ).start()

    @pl.when(step == steps - 1)
    def _():
        @pl.loop(0, steps * per)
        def _(j):
            pltpu.make_async_copy(pooled.at[0], outs[0].at[0, 0], sem).wait()


def pool_and_pack(tiles, own, pos, groups, slots):
    count, grid, _, channels = tiles.shape
    cells = grid * grid // 4
    per = 4
    steps = count // per
    made = jax.ShapeDtypeStruct((groups, slots, cells, channels), BF16)
    return pl.pallas_call(
        functools.partial(pool_kernel, steps, per),
        grid=(steps,),
        in_specs=[SMEM, SMEM, pl.BlockSpec((per, grid, grid, channels), lambda i: (i, 0, 0, 0))],
        out_specs=[ANY] * CHUNKS,
        out_shape=[made] * CHUNKS,
        scratch_shapes=[
            pltpu.VMEM((grid * grid // 2, channels), F32),
            pltpu.VMEM((count, cells, channels), BF16),
            pltpu.SemaphoreType.DMA,
        ],
        compiler_params=params(),
        cost_estimate=pl.CostEstimate(flops=tiles.size, bytes_accessed=tiles.size * 3, transcendentals=0),
        name="pool_and_pack",
    )(own, pos, tiles)


def partner(me, step, columns, sign):
    ring = columns // 2
    z = lax.rem(me // 2 + sign * (step // 2) + ring, ring)
    return 2 * z + lax.rem(lax.rem(me, 2) + step % 2, 2)


def partner_pairs(step, columns):
    ring = columns // 2
    return [(n, 2 * ((n // 2 + step // 2) % ring) + (n % 2 + step) % 2) for n in range(columns)]


def exchange(parts):
    columns = len(parts)
    return [parts[0]] + [lax.ppermute(parts[k], "abs", partner_pairs(k, columns)) for k in range(1, columns)]


def route_in_kernel(chunk, slots, per, columns, table_ref, info_ref, src, *rest):
    outs, (held, sem, out_sem) = rest[:columns], rest[columns:]
    filled, me = info_ref[0], info_ref[1]

    def each(act):
        for k in range(columns):
            first = partner(me, k, columns, 1) * per + chunk * slots

            @pl.loop(0, slots)
            def _(local, k=k, first=first):
                q = first + local

                @pl.when(q < filled)
                def _():
                    act(pltpu.make_async_copy(src.at[table_ref[q], local], held.at[k, local], sem))

    each(lambda one: one.start())
    each(lambda one: one.wait())
    saves = [pltpu.make_async_copy(held.at[k], outs[k], out_sem.at[k]) for k in range(columns)]
    for one in saves:
        one.start()
    for one in saves:
        one.wait()


def route_back_kernel(chunk, slots, per, columns, table_ref, info_ref, *rest):
    srcs, (dst, held, sem, in_sem) = rest[:columns], rest[columns:]
    filled, me = info_ref[0], info_ref[1]
    loads = [pltpu.make_async_copy(srcs[k], held.at[k], in_sem.at[k]) for k in range(columns)]
    for one in loads:
        one.start()

    def each(act, ready):
        for k in range(columns):
            first = partner(me, k, columns, -1) * per + chunk * slots
            if ready:
                loads[k].wait()

            @pl.loop(0, slots)
            def _(local, k=k, first=first):
                q = first + local

                @pl.when(q < filled)
                def _():
                    act(pltpu.make_async_copy(held.at[k, local], dst.at[table_ref[q], local], sem))

    each(lambda one: one.start(), True)
    each(lambda one: one.wait(), False)


def route(sources, table, info, chunk, per, columns, groups, back):
    slots, cells, channels = sources[0].shape[-3:]
    part = jax.ShapeDtypeStruct((slots, cells, channels), BF16)
    whole = jax.ShapeDtypeStruct((groups, slots, cells, channels), BF16)
    body = route_back_kernel if back else route_in_kernel
    return pl.pallas_call(
        functools.partial(body, chunk, slots, per, columns),
        in_specs=[SMEM, SMEM] + [ANY] * len(sources),
        out_specs=ANY if back else [ANY] * columns,
        out_shape=whole if back else [part] * columns,
        scratch_shapes=[
            pltpu.VMEM((columns, slots, cells, channels), BF16),
            pltpu.SemaphoreType.DMA,
            pltpu.SemaphoreType.DMA((columns,)),
        ],
        compiler_params=pltpu.CompilerParams(vmem_limit_bytes=8 * 1024 * 1024),
        cost_estimate=pl.CostEstimate(
            flops=0, bytes_accessed=8 * columns * slots * cells * channels, transcendentals=0
        ),
        name="route_back" if back else "route_in",
    )(table, info, *sources)


def exact_dot(left, weights):
    rows = left.shape[0]
    first = left.astype(BF16).astype(F32)
    rest = left - first
    second = rest.astype(BF16).astype(F32)
    third = rest - second
    stacked = jnp.concatenate([first, second, third, jnp.zeros_like(left)], axis=0).astype(BF16)
    made = jnp.dot(stacked, weights, preferred_element_type=F32)
    return made[:rows] + made[rows : 2 * rows] + made[2 * rows : 3 * rows]


def block_kernel(
    chunk,
    side,
    columns,
    info_ref,
    *rest,
):
    x_hbm, rest = rest[:columns], rest[columns:]
    up_hbm, w_in_hbm, w_out_hbm, w_in_t_hbm, w_out_t_hbm = rest[:5]
    se_down, se_up, se_down_t, se_up_t, taps, gain = rest[5:11]
    outs = rest[-24 - columns : -17]
    (vis_hbm, normed_hbm, scaled_hbm, hidden_hbm), back_hbm = outs[:4], outs[4 : 4 + columns]
    small_a, small_b, small_k = outs[4 + columns :]
    filled, me = info_ref[0], info_ref[1]
    live = filled - me * info_ref[2]
    (
        x,
        up,
        w_in,
        w_out,
        w_in_t,
        w_out_t,
        standard,
        inverse,
        slope_h,
        act,
        mixed,
        slope_s,
        wide,
        tmp,
        masks,
        stage,
        sem,
    ) = rest[-17:]
    (rows_v, squeeze, excite, extra, kacc, gacc, normed, scaled, vis) = stage
    blocks, tiles, cells, lanes = x.shape
    width = blocks * lanes
    flat = tiles * cells
    loads = [
        pltpu.make_async_copy(a, b, sem.at[n])
        for n, (a, b) in enumerate(
            [
                (w_in_hbm, w_in),
                (up_hbm.at[pl.ds(chunk * tiles, tiles)], up),
                (w_out_hbm, w_out),
                (w_out_t_hbm, w_out_t),
                (w_in_t_hbm, w_in_t),
            ]
        )
    ]
    x_loads = [
        pltpu.make_async_copy(x_hbm[k], x.at[partner(me, k, columns, -1)], sem.at[10 + k]) for k in range(columns)
    ]
    for one in x_loads + loads:
        one.start()

    column = lax.rem(lax.broadcasted_iota(jnp.int32, (cells, lanes), 0), side)
    masks[0] = jnp.where(column != 0, 1.0, 0.0).astype(F32)
    masks[1] = jnp.where(column != side - 1, 1.0, 0.0).astype(F32)
    edge = jnp.zeros((PAD, lanes), F32)
    tmp[pl.ds(0, PAD), :] = edge
    tmp[pl.ds(PAD + cells, PAD), :] = edge
    kacc[...] = jnp.zeros_like(kacc)
    gacc[...] = jnp.zeros_like(gacc)
    squeeze[...] = jnp.zeros_like(squeeze)
    extra[...] = jnp.zeros_like(extra)

    @pl.loop(0, blocks * tiles)
    def _(n):
        c, t = n % blocks, n // blocks
        act[c, t, pl.ds(0, PAD), :] = edge
        act[c, t, pl.ds(PAD + cells, PAD), :] = edge

    for one in x_loads:
        one.wait()
    loads[1].wait()
    for t in range(tiles):

        @pl.when(chunk * tiles + t >= live)
        def _(t=t):
            up[t] = jnp.zeros(up.shape[1:], BF16)
            for c in range(blocks):
                x[c, t] = jnp.zeros((cells, lanes), BF16)

    @pl.loop(0, tiles)
    def _(t):
        total = x[0, t].astype(F32)
        for c in range(1, blocks):
            total = total + x[c, t].astype(F32)
        average = jnp.sum(total, axis=1, keepdims=True) * (1.0 / width)
        square = jnp.zeros((cells, lanes), F32)
        for c in range(blocks):
            centred = x[c, t].astype(F32) - average
            square = square + centred * centred
        variance = jnp.sum(square, axis=1, keepdims=True) * (1.0 / width)
        inv = lax.rsqrt(variance + NORM_EPS)
        inverse[t] = jnp.broadcast_to(inv, (cells, lanes))
        for c in range(blocks):
            std = (x[c, t].astype(F32) - average) * inv
            standard[c, t] = std
            normed[t, :, c * lanes : (c + 1) * lanes] = (std * gain[c, 0:1, :]).astype(BF16)

    def product(left, right, put):
        wide_n = 256
        value = left[...].reshape(flat, width)
        for n in range(width // wide_n):
            made = jnp.dot(value, right[:, n * wide_n : (n + 1) * wide_n], preferred_element_type=F32)
            for half in range(wide_n // lanes):
                c = n * (wide_n // lanes) + half
                put(c, made[:, half * lanes : (half + 1) * lanes].reshape(tiles, cells, lanes))

    def put_hidden(c, value):
        slope_h[c] = value

    loads[0].wait()
    product(normed, w_in, put_hidden)
    save_normed = pltpu.make_async_copy(normed, normed_hbm.at[pl.ds(chunk * tiles, tiles)], sem.at[6])
    save_normed.start()

    @pl.loop(0, blocks * tiles)
    def _(n):
        c, t = n % blocks, n // blocks
        h = slope_h[c, t]
        sig = jax.nn.sigmoid(h)
        a = h * sig
        slope_h[c, t] = sig * (1.0 + h * (1.0 - sig))
        act[c, t, pl.ds(PAD, cells), :] = a

        def column_sum(b):
            made = None
            for r in range(3):
                term = taps[c, 3 * r + b : 3 * r + b + 1, :] * act[c, t, pl.ds(PAD + side * (r - 1) + b - 1, cells), :]
                made = term if made is None else made + term
            return made

        spatial = column_sum(1) + masks[0] * column_sum(0) + masks[1] * column_sum(2)
        sig = jax.nn.sigmoid(spatial)
        mix = spatial * sig
        mixed[c, t] = mix
        slope_s[c, t] = sig * (1.0 + spatial * (1.0 - sig))
        squeeze[c, pl.ds(t, 1), :] = jnp.sum(mix, axis=0, keepdims=True) * (1.0 / cells)

    def joined(ref):
        return jnp.concatenate([ref[c] for c in range(blocks)], axis=1)

    squeezed = joined(squeeze)
    squeeze_pre = exact_dot(squeezed, se_down[...])
    sig_pre = jax.nn.sigmoid(squeeze_pre)
    squeeze_act = squeeze_pre * sig_pre
    excited = jax.nn.sigmoid(exact_dot(squeeze_act, se_up[...]))
    for c in range(blocks):
        excite[c] = excited[:, c * lanes : (c + 1) * lanes]

    def put_back(c, value):
        wide[c] = value

    loads[3].wait()
    product(up, w_out_t, put_back)

    @pl.loop(0, tiles)
    def _(t):
        for c in range(blocks):
            mix = mixed[c, t]
            scaled[t, :, c * lanes : (c + 1) * lanes] = (mix * excite[c, pl.ds(t, 1), :]).astype(BF16)
            extra[c, pl.ds(t, 1), :] = jnp.sum(wide[c, t] * mix, axis=0, keepdims=True)

    back_pre = joined(extra) * excited * (1.0 - excited)
    back_squeeze_pre = exact_dot(back_pre, se_up_t[...]) * (
        sig_pre * (1.0 + squeeze_pre * (1.0 - sig_pre))
    )
    back_squeeze = exact_dot(back_squeeze_pre, se_down_t[...]) * (1.0 / cells)
    for c in range(blocks):
        extra[c] = back_squeeze[:, c * lanes : (c + 1) * lanes]
    small_a[0] = squeezed
    small_a[1] = back_pre
    small_b[0] = back_squeeze_pre
    small_b[1] = squeeze_act

    def put_visual(c, value):
        vis[:, :, c * lanes : (c + 1) * lanes] = (x[c].astype(F32) + value).astype(BF16)

    loads[2].wait()
    product(scaled, w_out, put_visual)
    save_scaled = pltpu.make_async_copy(scaled, scaled_hbm.at[pl.ds(chunk * tiles, tiles)], sem.at[7])
    save_scaled.start()
    save_vis = pltpu.make_async_copy(vis, vis_hbm.at[pl.ds(chunk * tiles, tiles)], sem.at[8])
    save_vis.start()
    save_normed.wait()

    @pl.loop(0, tiles)
    def _(t):
        for c in range(blocks):
            back = (wide[c, t] * excite[c, pl.ds(t, 1), :] + extra[c, pl.ds(t, 1), :]) * slope_s[c, t]
            tmp[pl.ds(PAD, cells), :] = back
            sides = (back * masks[0], back, back * masks[1])
            for r in range(3):
                for b in range(3):
                    term = sides[b] * act[c, t, pl.ds(PAD + side * (r - 1) + b - 1, cells), :]
                    kacc[c, 3 * r + b] += jnp.sum(term.reshape(cells // 8, 8, lanes), axis=0)

            def column_sum(b, c=c):
                made = None
                for r in range(3):
                    term = taps[c, 3 * r + b : 3 * r + b + 1, :] * tmp[pl.ds(PAD - side * (r - 1) - (b - 1), cells), :]
                    made = term if made is None else made + term
                return made

            back_act = column_sum(1) + masks[1] * column_sum(0) + masks[0] * column_sum(2)
            normed[t, :, c * lanes : (c + 1) * lanes] = (back_act * slope_h[c, t]).astype(BF16)

    loads[4].wait()
    product(normed, w_in_t, put_back)
    save_hidden = pltpu.make_async_copy(normed, hidden_hbm.at[pl.ds(chunk * tiles, tiles)], sem.at[9])
    save_hidden.start()

    @pl.loop(0, tiles)
    def _(t):
        centre = jnp.zeros((cells, lanes), F32)
        along = jnp.zeros((cells, lanes), F32)
        for c in range(blocks):
            along_n = wide[c, t] * standard[c, t]
            gacc[c] += jnp.sum(along_n.reshape(cells // 8, 8, lanes), axis=0)
            centre = centre + wide[c, t] * gain[c, 0:1, :]
            along = along + along_n * gain[c, 0:1, :]
        centre = jnp.sum(centre, axis=1, keepdims=True) * (1.0 / width)
        along = jnp.sum(along, axis=1, keepdims=True) * (1.0 / width)
        inv = inverse[t]
        for c in range(blocks):
            made = up[t, :, c * lanes : (c + 1) * lanes].astype(F32) + inv * (
                wide[c, t] * gain[c, 0:1, :] - centre - standard[c, t] * along
            )
            rows_v[c, t] = made.astype(BF16)

    save_back = [
        pltpu.make_async_copy(rows_v.at[partner(me, k, columns, 1)], back_hbm[k], sem.at[10 + columns + k])
        for k in range(columns)
    ]
    for one in save_back:
        one.start()
    small_k[...] = jnp.zeros_like(small_k)
    for c in range(blocks):
        for r in range(9):
            small_k[r : r + 1, c * lanes : (c + 1) * lanes] = jnp.sum(kacc[c, r], axis=0, keepdims=True)
        small_k[9:10, c * lanes : (c + 1) * lanes] = jnp.sum(gacc[c], axis=0, keepdims=True)
    save_scaled.wait()
    save_vis.wait()
    save_hidden.wait()
    for one in save_back:
        one.wait()


def run_block(chunk, side, info, x, up, weights, carried):
    columns = len(x)
    tiles, cells, lanes = x[0].shape
    blocks = columns
    size = blocks * tiles * cells * lanes
    width = blocks * lanes
    narrow = weights[4].shape[1]
    whole = jax.ShapeDtypeStruct(up.shape, BF16)
    fixed = [info, *x, up, *weights]
    field = pltpu.VMEM((blocks, tiles, cells, lanes), F32)
    packed = pltpu.VMEM((tiles, cells, width), BF16)
    eight = pltpu.VMEM((blocks, 8, lanes), F32)
    square = pltpu.VMEM((width, width), BF16)
    flops = 8 * tiles * cells * width * width
    return pl.pallas_call(
        functools.partial(block_kernel, chunk, side, columns),
        in_specs=[SMEM] + [ANY] * (columns + 5) + [VMEM] * 6 + [ANY] * len(carried),
        out_specs=[ANY] * (4 + columns) + [VMEM] * 3,
        out_shape=[whole] * 4
        + [jax.ShapeDtypeStruct((tiles, cells, lanes), BF16)] * columns
        + [
            jax.ShapeDtypeStruct((2, 8, width), F32),
            jax.ShapeDtypeStruct((2, 8, narrow), F32),
            jax.ShapeDtypeStruct((16, width), F32),
        ],
        input_output_aliases={len(fixed) + n: n for n in range(len(carried))},
        scratch_shapes=[
            pltpu.VMEM((blocks, tiles, cells, lanes), BF16),
            packed,
            square,
            square,
            square,
            square,
            field,
            pltpu.VMEM((tiles, cells, lanes), F32),
            field,
            pltpu.VMEM((blocks, tiles, cells + 2 * PAD, lanes), F32),
            field,
            field,
            field,
            pltpu.VMEM((cells + 2 * PAD, lanes), F32),
            pltpu.VMEM((2, cells, lanes), F32),
            [
                pltpu.VMEM((blocks, tiles, cells, lanes), BF16),
                eight,
                eight,
                eight,
                pltpu.VMEM((blocks, 9, 8, lanes), F32),
                eight,
                packed,
                packed,
                packed,
            ],
            pltpu.SemaphoreType.DMA((10 + 2 * columns,)),
        ],
        compiler_params=params(),
        cost_estimate=pl.CostEstimate(
            flops=flops, bytes_accessed=16 * size + 8 * width * width, transcendentals=2 * size
        ),
        name="block_%d" % chunk,
    )(*fixed, *carried)


def weights_kernel(chunks, columns, info_ref, normed, scaled, hidden, up, *rest):
    smalls, (home, away, held) = rest[: 5 * chunks], rest[5 * chunks :]
    count, cells, wide = normed.shape
    flat = count * cells
    width = hidden.shape[2]
    me = info_ref[1]
    ring = columns // 2
    made = []
    for left, right in ((normed, hidden), (scaled, up)):
        made.append(
            lax.dot_general(
                left[...].reshape(flat, wide),
                right[...].reshape(flat, width),
                (((0,), (0,)), ((), ())),
                preferred_element_type=F32,
            )
        )

    def outer(left, right):
        return lax.dot_general(
            left, right, (((0,), (0,)), ((), ())), preferred_element_type=F32, precision=lax.Precision.HIGHEST
        )

    quarter = lax.rem(lax.broadcasted_iota(jnp.int32, (8, wide), 1), 4)
    same = jnp.where(
        lax.broadcasted_iota(jnp.int32, (16, wide), 0) == lax.broadcasted_iota(jnp.int32, (16, wide), 1), 1.0, 0.0
    ).astype(F32)
    down = lift = taps = None
    for h in range(chunks):
        squeeze, back_pre, back_squeeze_pre, act, terms = smalls[5 * h : 5 * h + 5]
        narrow = back_squeeze_pre.shape[2]
        one = outer(squeeze[0], back_squeeze_pre[0])
        down = one if down is None else down + one
        for m in range(4):
            one = outer(
                jnp.where(quarter == m, act[...], 0.0), back_pre[0, :, m * narrow : (m + 1) * narrow]
            )
            lift = one if lift is None else lift + one
        one = outer(terms[...], same)
        taps = one if taps is None else taps + one
    place = 0
    for value in (*made, down, lift, taps):
        held[:, place : place + value.shape[1]] = value
        place += value.shape[1]
    for group in range(wide // (8 * columns)):
        for k in range(columns):
            row = pl.multiple_of(8 * (columns * group + partner(me, k, columns, 1)), 8)
            target = home if k % 2 == 0 else away
            target[k // 2, group] = held[pl.ds(row, 8), :].astype(BF16)


def weight_terms(info, normed, scaled, hidden, up, small, columns):
    count, cells, width = normed.shape
    narrow = small[0][1].shape[2]
    wide = LANES
    lanes = 2 * width + 2 * narrow + wide
    groups = width // (8 * columns)
    per = wide // (8 * columns)
    left = pl.BlockSpec((count, cells, wide), lambda i: (0, 0, i))
    right = pl.BlockSpec((count, cells, width), lambda i: (0, 0, 0), pipeline_mode=pl.Buffered(1))
    args, specs = [], []
    for a, b, k in small:
        args += [a, a, b, jnp.repeat(b[1], 4, axis=1), k]
        specs += [
            pl.BlockSpec((1, 8, wide), lambda i: (0, 0, i)),
            pl.BlockSpec((1, 8, width), lambda i: (1, 0, 0)),
            pl.BlockSpec((1, 8, narrow), lambda i: (0, 0, 0)),
            pl.BlockSpec((8, wide), lambda i: (0, i)),
            pl.BlockSpec((16, wide), lambda i: (0, i)),
        ]
    part = jax.ShapeDtypeStruct((columns // 2, groups, 8, lanes), BF16)
    return pl.pallas_call(
        functools.partial(weights_kernel, len(small), columns),
        grid=(width // wide,),
        in_specs=[SMEM, left, left, right, right] + specs,
        out_specs=[pl.BlockSpec((columns // 2, per, 8, lanes), lambda i: (0, i, 0, 0))] * 2,
        out_shape=[part] * 2,
        scratch_shapes=[pltpu.VMEM((wide, lanes), F32)],
        compiler_params=params(),
        cost_estimate=pl.CostEstimate(
            flops=4 * count * cells * width * width, bytes_accessed=8 * count * cells * width, transcendentals=0
        ),
        name="weight_terms",
    )(info, normed, scaled, hidden, up, *args)


def spread_kernel(per, own_ref, pos_ref, *rest):
    arrived, out, (held, wide, sem) = rest[:CHUNKS], rest[CHUNKS], rest[CHUNKS + 1 :]
    step = pl.program_id(0)
    slots = arrived[0].shape[1]
    count = held.shape[0]
    side = out.shape[1] // 2
    width = 2 * side

    @pl.when(step == 0)
    def _():
        @pl.loop(0, count)
        def _(j):
            position = pos_ref[j]
            for h in range(CHUNKS):

                @pl.when(position // slots == h)
                def _(h=h):
                    pltpu.make_async_copy(
                        arrived[h].at[own_ref[j], position - h * slots], held.at[j], sem
                    ).start()

        @pl.loop(0, count)
        def _(j):
            pltpu.make_async_copy(arrived[0].at[0, 0], held.at[0], sem).wait()

    for n in range(per):
        quarter = held[step * per + n].astype(F32) * 0.25
        wide[pl.ds(0, side * side, stride=2), :] = quarter
        wide[pl.ds(1, side * side, stride=2), :] = quarter
        for row in range(side):
            line = wide[pl.ds(row * width, width), :].astype(BF16)
            out[n, 2 * row] = line
            out[n, 2 * row + 1] = line


def unpack_and_spread(arrived, own, pos, count, grid):
    _, _, cells, channels = arrived[0].shape
    per = 4
    return pl.pallas_call(
        functools.partial(spread_kernel, per),
        grid=(count // per,),
        in_specs=[SMEM, SMEM] + [ANY] * CHUNKS,
        out_specs=pl.BlockSpec((per, grid, grid, channels), lambda i: (i, 0, 0, 0)),
        out_shape=jax.ShapeDtypeStruct((count, grid, grid, channels), BF16),
        scratch_shapes=[
            pltpu.VMEM((count, cells, channels), BF16),
            pltpu.VMEM((grid * grid // 2, channels), F32),
            pltpu.SemaphoreType.DMA,
        ],
        compiler_params=params(),
        cost_estimate=pl.CostEstimate(
            flops=0, bytes_accessed=10 * count * cells * channels, transcendentals=0
        ),
        name="unpack_and_spread",
    )(own, pos, *arrived)


def before(table):
    groups = table.shape[1]
    index = jnp.arange(groups, dtype=jnp.int32)
    lower = index[None, :] < index[:, None]
    return jnp.sum(jnp.where(lower[None], table[:, None, :], 0), axis=2, dtype=jnp.int32)


def routing(counts, owners, ranks, group_id, local_tiles, capacity):
    groups = counts.shape[0]
    start = before(counts)
    flat_counts, flat_owners, flat_ranks = counts.reshape(-1), owners.reshape(-1), ranks.reshape(-1)
    ahead = (flat_owners[:, None] == flat_owners[None, :]) & (flat_ranks[None, :] < flat_ranks[:, None])
    offset = jnp.sum(jnp.where(ahead, flat_counts[None, :], 0), axis=1, dtype=jnp.int32).reshape(groups, groups)
    sources = jnp.arange(groups, dtype=jnp.int32)
    mine = (sources == group_id)[:, None]

    def row(table):
        return jnp.sum(jnp.where(mine, table, 0), axis=0, dtype=jnp.int32)

    owner_row, start_row, offset_row = row(owners), row(start), row(offset)
    ids = jnp.arange(local_tiles, dtype=jnp.int32)
    member = jnp.sum((start_row[None, :] <= ids[:, None]).astype(jnp.int32), axis=1, dtype=jnp.int32) - 1
    which = member[:, None] == sources[None, :]
    own = jnp.sum(jnp.where(which, owner_row[None, :], 0), axis=1, dtype=jnp.int32)
    slot = jnp.sum(jnp.where(which, (offset_row - start_row)[None, :], 0), axis=1, dtype=jnp.int32) + ids
    arriving = owners == group_id
    recv_count = jnp.sum(jnp.where(arriving, counts, 0), axis=1, dtype=jnp.int32)
    recv_offset = jnp.sum(jnp.where(arriving, offset, 0), axis=1, dtype=jnp.int32)
    positions = jnp.arange(capacity, dtype=jnp.int32)
    inside = (positions[:, None] >= recv_offset[None, :]) & (
        positions[:, None] < (recv_offset + recv_count)[None, :]
    )
    table = jnp.sum(jnp.where(inside, sources[None, :], 0), axis=1, dtype=jnp.int32)
    filled = jnp.sum(recv_count, dtype=jnp.int32).reshape(1)
    return own, slot, table, filled


def local(
    tiles,
    w_in,
    w_out,
    se_down,
    se_up,
    kernel,
    gain,
    token_grads,
    tile_counts,
    sample_owner,
    sample_rank,
):
    groups = lax.axis_size("enc")
    columns = lax.axis_size("abs")
    group_id = lax.axis_index("enc")
    column_id = lax.axis_index("abs")
    local_tiles, grid = tiles.shape[0], tiles.shape[1]
    per, cells, width = token_grads.shape
    capacity = per * columns
    side = grid // 2
    slots = per // CHUNKS
    blocks = width // LANES
    own, slot, table, filled = routing(
        tile_counts, sample_owner, sample_rank, group_id, local_tiles, capacity
    )
    pos = slot % per
    info = jnp.stack([filled[0], column_id.astype(jnp.int32), jnp.int32(per)])
    sends = pool_and_pack(tiles, own, pos, groups, slots)

    taps = jnp.pad(kernel.astype(F32).reshape(9, blocks, LANES).transpose(1, 0, 2), ((0, 0), (0, 7), (0, 0)))
    gains = jnp.broadcast_to(gain.astype(F32).reshape(blocks, 1, LANES), (blocks, 8, LANES))
    weights = [w_in, w_out, w_in.T, w_out.T, se_down, se_up, se_down.T, se_up.T, taps, gains]

    inner = []
    for h in range(CHUNKS):
        send = sends[h]
        if h > 0:
            send, _ = lax.optimization_barrier((send, received))
        received = lax.all_to_all(send, "enc", split_axis=0, concat_axis=0, tiled=True)
        if h == 0:
            received, *weights = lax.optimization_barrier((received, *weights))
        parts = route([received], table, info, h, per, columns, groups, False)
        inner.append(exchange(parts))

    carried = []
    arrived, small = [], []
    for h in range(CHUNKS):
        made = run_block(h, side, info, inner[h], token_grads, weights, carried)
        carried = list(made[:4])
        small.append(made[4 + columns :])
        narrowed = exchange(made[4 : 4 + columns])
        back = route(narrowed, table, info, h, per, columns, groups, True)
        arrived.append(lax.all_to_all(back, "enc", split_axis=0, concat_axis=0, tiled=True))
    visual, normed, scaled, hidden = carried
    tile_grads = unpack_and_spread(arrived, own, pos, local_tiles, grid)

    home, away = weight_terms(info, normed, scaled, hidden, token_grads, small, columns)
    near = lax.ppermute(away, "abs", partner_pairs(1, columns))
    pair = [(home[k].astype(F32) + near[k].astype(F32)).astype(BF16) for k in range(columns // 2)]
    rows = [pair[0]] + [
        lax.ppermute(pair[k], "abs", partner_pairs(2 * k, columns)) for k in range(1, columns // 2)
    ]
    column = sum(r.astype(F32) for r in rows).astype(BF16)
    spread = lax.all_to_all(column, "enc", split_axis=0, concat_axis=0, tiled=True)
    scale = 1.0 / math.sqrt(groups * local_tiles * cells)
    total = jnp.sum(spread.astype(F32), axis=0) * scale
    narrow = se_down.shape[1]
    ends = [width, 2 * width, 2 * width + narrow, 2 * width + 2 * narrow]
    last = total[:, ends[3] : ends[3] + 10]
    return (
        visual,
        tile_grads,
        total[:, : ends[0]],
        total[:, ends[0] : ends[1]],
        total[:, ends[1] : ends[2]],
        total[:, ends[2] : ends[3]].reshape(2, width),
        last[:, :9].T,
        last[:, 9],
    )


def solution(mesh):
    return jax.shard_map(
        local,
        mesh=mesh,
        in_specs=(
            P("enc", None, None, "abs"),
            P(),
            P(),
            P(),
            P(),
            P(),
            P(),
            P(("enc", "abs"), None, None),
            P(),
            P(),
            P(),
        ),
        out_specs=(
            P(("enc", "abs"), None, None),
            P("enc", None, None, "abs"),
            P(("enc", "abs"), None),
            P(("enc", "abs"), None),
            P(("enc", "abs"), None),
            P(("enc", "abs"), None),
            P(None, ("enc", "abs")),
            P(("enc", "abs")),
        ),
        check_vma=False,
    )
```

```python
import functools
import math

import jax
import jax.numpy as jnp
from jax import lax
from jax.experimental import pallas as pl
from jax.experimental.pallas import tpu as pltpu
from jax.sharding import PartitionSpec as P

F32 = jnp.float32
BF16 = jnp.bfloat16
NORM_EPS = 1e-06
LANES = 128
PAD = 16
CHUNKS = 2
VMEM_BYTES = 60 * 1024 * 1024
ANY = pl.BlockSpec(memory_space=pl.ANY)
SMEM = pl.BlockSpec(memory_space=pltpu.SMEM)
VMEM = pl.BlockSpec(memory_space=pltpu.VMEM)


def params(**more):
    return pltpu.CompilerParams(vmem_limit_bytes=VMEM_BYTES, **more)


def pool_kernel(steps, per, own_ref, pos_ref, tiles_ref, *rest):
    outs, (wide, pooled, sem) = rest[:CHUNKS], rest[CHUNKS:]
    step = pl.program_id(0)
    side = tiles_ref.shape[1] // 2
    width = 2 * side
    slots = outs[0].shape[1]
    for n in range(per):
        for row in range(side):
            pair = tiles_ref[n, 2 * row].astype(F32) + tiles_ref[n, 2 * row + 1].astype(F32)
            wide[pl.ds(row * width, width), :] = pair
        total = wide[pl.ds(0, side * side, stride=2), :] + wide[pl.ds(1, side * side, stride=2), :]
        j = step * per + n
        pooled[j] = (total * 0.25).astype(BF16)
        position = pos_ref[j]
        for h in range(CHUNKS):

            @pl.when(position // slots == h)
            def _(h=h):
                pltpu.make_async_copy(
                    pooled.at[j], outs[h].at[own_ref[j], position - h * slots], sem
                ).start()

    @pl.when(step == steps - 1)
    def _():
        @pl.loop(0, steps * per)
        def _(j):
            pltpu.make_async_copy(pooled.at[0], outs[0].at[0, 0], sem).wait()


def pool_and_pack(tiles, own, pos, groups, slots):
    count, grid, _, channels = tiles.shape
    cells = grid * grid // 4
    per = 4
    steps = count // per
    made = jax.ShapeDtypeStruct((groups, slots, cells, channels), BF16)
    return pl.pallas_call(
        functools.partial(pool_kernel, steps, per),
        grid=(steps,),
        in_specs=[SMEM, SMEM, pl.BlockSpec((per, grid, grid, channels), lambda i: (i, 0, 0, 0))],
        out_specs=[ANY] * CHUNKS,
        out_shape=[made] * CHUNKS,
        scratch_shapes=[
            pltpu.VMEM((grid * grid // 2, channels), F32),
            pltpu.VMEM((count, cells, channels), BF16),
            pltpu.SemaphoreType.DMA,
        ],
        compiler_params=params(),
        cost_estimate=pl.CostEstimate(flops=tiles.size, bytes_accessed=tiles.size * 3, transcendentals=0),
        name="pool_and_pack",
    )(own, pos, tiles)


def partner(me, step, columns, sign):
    ring = columns // 2
    z = lax.rem(me // 2 + sign * (step // 2) + ring, ring)
    return 2 * z + lax.rem(lax.rem(me, 2) + step % 2, 2)


def partner_pairs(step, columns):
    ring = columns // 2
    return [(n, 2 * ((n // 2 + step // 2) % ring) + (n % 2 + step) % 2) for n in range(columns)]


def exchange(parts):
    columns = len(parts)
    if columns == 1:
        return [lax.all_to_all(parts[0], "abs", split_axis=0, concat_axis=0, tiled=True)]
    return [parts[0]] + [lax.ppermute(parts[k], "abs", partner_pairs(k, columns)) for k in range(1, columns)]


def pick(refs, me, step, sign):
    if len(refs) > 1:
        return refs[step]
    return refs[0].at[partner(me, step, refs[0].shape[0], sign)]


def route_in_kernel(chunk, slots, per, columns, table_ref, info_ref, src, *rest):
    outs, (held, sem, out_sem) = rest[:-3], rest[-3:]
    filled, me = info_ref[0], info_ref[1]

    def each(act):
        for k in range(columns):
            first = partner(me, k, columns, 1) * per + chunk * slots

            @pl.loop(0, slots)
            def _(local, k=k, first=first):
                q = first + local

                @pl.when(q < filled)
                def _():
                    act(pltpu.make_async_copy(src.at[table_ref[q], local], held.at[k, local], sem))

    each(lambda one: one.start())
    each(lambda one: one.wait())
    saves = [pltpu.make_async_copy(held.at[k], pick(outs, me, k, 1), out_sem.at[k]) for k in range(columns)]
    for one in saves:
        one.start()
    for one in saves:
        one.wait()


def route_back_kernel(chunk, slots, per, columns, table_ref, info_ref, *rest):
    srcs, (dst, held, sem, in_sem) = rest[:-4], rest[-4:]
    filled, me = info_ref[0], info_ref[1]
    loads = [pltpu.make_async_copy(pick(srcs, me, k, -1), held.at[k], in_sem.at[k]) for k in range(columns)]
    for one in loads:
        one.start()

    def each(act, ready):
        for k in range(columns):
            first = partner(me, k, columns, -1) * per + chunk * slots
            if ready:
                loads[k].wait()

            @pl.loop(0, slots)
            def _(local, k=k, first=first):
                q = first + local

                @pl.when(q < filled)
                def _():
                    act(pltpu.make_async_copy(held.at[k, local], dst.at[table_ref[q], local], sem))

    each(lambda one: one.start(), True)
    each(lambda one: one.wait(), False)


def parts_of(columns, shape, joined):
    if joined:
        return [jax.ShapeDtypeStruct((columns, *shape), BF16)]
    return [jax.ShapeDtypeStruct(shape, BF16)] * columns


def route(sources, table, info, chunk, per, columns, groups, back, joined=False):
    slots, cells, channels = sources[0].shape[-3:]
    parts = parts_of(columns, (slots, cells, channels), joined)
    whole = jax.ShapeDtypeStruct((groups, slots, cells, channels), BF16)
    body = route_back_kernel if back else route_in_kernel
    return pl.pallas_call(
        functools.partial(body, chunk, slots, per, columns),
        in_specs=[SMEM, SMEM] + [ANY] * len(sources),
        out_specs=ANY if back else [ANY] * len(parts),
        out_shape=whole if back else parts,
        scratch_shapes=[
            pltpu.VMEM((columns, slots, cells, channels), BF16),
            pltpu.SemaphoreType.DMA,
            pltpu.SemaphoreType.DMA((columns,)),
        ],
        compiler_params=pltpu.CompilerParams(vmem_limit_bytes=8 * 1024 * 1024),
        cost_estimate=pl.CostEstimate(
            flops=0, bytes_accessed=8 * columns * slots * cells * channels, transcendentals=0
        ),
        name="route_back" if back else "route_in",
    )(table, info, *sources)


def exact_dot(left, weights):
    rows = left.shape[0]
    first = left.astype(BF16).astype(F32)
    rest = left - first
    second = rest.astype(BF16).astype(F32)
    third = rest - second
    stacked = jnp.concatenate([first, second, third, jnp.zeros_like(left)], axis=0).astype(BF16)
    made = jnp.dot(stacked, weights, preferred_element_type=F32)
    return made[:rows] + made[rows : 2 * rows] + made[2 * rows : 3 * rows]


def block_kernel(
    chunk,
    side,
    columns,
    parts_in,
    parts_out,
    info_ref,
    *rest,
):
    x_hbm, rest = rest[:parts_in], rest[parts_in:]
    up_hbm, w_in_hbm, w_out_hbm, w_in_t_hbm, w_out_t_hbm = rest[:5]
    se_down, se_up, se_down_t, se_up_t, taps, gain = rest[5:11]
    outs = rest[-24 - parts_out : -17]
    (vis_hbm, normed_hbm, scaled_hbm, hidden_hbm), back_hbm = outs[:4], outs[4 : 4 + parts_out]
    small_a, small_b, small_k = outs[4 + parts_out :]
    filled, me = info_ref[0], info_ref[1]
    live = filled - me * info_ref[2]
    (
        x,
        up,
        w_in,
        w_out,
        w_in_t,
        w_out_t,
        standard,
        inverse,
        slope_h,
        act,
        mixed,
        slope_s,
        wide,
        tmp,
        masks,
        stage,
        sem,
    ) = rest[-17:]
    (rows_v, squeeze, excite, extra, kacc, gacc, normed, scaled, vis) = stage
    blocks, tiles, cells, lanes = x.shape
    width = blocks * lanes
    flat = tiles * cells
    loads = [
        pltpu.make_async_copy(a, b, sem.at[n])
        for n, (a, b) in enumerate(
            [
                (w_in_hbm, w_in),
                (up_hbm.at[pl.ds(chunk * tiles, tiles)], up),
                (w_out_hbm, w_out),
                (w_out_t_hbm, w_out_t),
                (w_in_t_hbm, w_in_t),
            ]
        )
    ]
    x_loads = [
        pltpu.make_async_copy(pick(x_hbm, me, k, -1), x.at[partner(me, k, columns, -1)], sem.at[10 + k])
        for k in range(columns)
    ]
    for one in x_loads + loads:
        one.start()

    column = lax.rem(lax.broadcasted_iota(jnp.int32, (cells, lanes), 0), side)
    masks[0] = jnp.where(column != 0, 1.0, 0.0).astype(F32)
    masks[1] = jnp.where(column != side - 1, 1.0, 0.0).astype(F32)
    edge = jnp.zeros((PAD, lanes), F32)
    tmp[pl.ds(0, PAD), :] = edge
    tmp[pl.ds(PAD + cells, PAD), :] = edge
    kacc[...] = jnp.zeros_like(kacc)
    gacc[...] = jnp.zeros_like(gacc)
    squeeze[...] = jnp.zeros_like(squeeze)
    extra[...] = jnp.zeros_like(extra)

    @pl.loop(0, blocks * tiles)
    def _(n):
        c, t = n % blocks, n // blocks
        act[c, t, pl.ds(0, PAD), :] = edge
        act[c, t, pl.ds(PAD + cells, PAD), :] = edge

    for one in x_loads:
        one.wait()
    loads[1].wait()
    for t in range(tiles):

        @pl.when(chunk * tiles + t >= live)
        def _(t=t):
            up[t] = jnp.zeros(up.shape[1:], BF16)
            for c in range(blocks):
                x[c, t] = jnp.zeros((cells, lanes), BF16)

    @pl.loop(0, tiles)
    def _(t):
        total = x[0, t].astype(F32)
        for c in range(1, blocks):
            total = total + x[c, t].astype(F32)
        average = jnp.sum(total, axis=1, keepdims=True) * (1.0 / width)
        square = jnp.zeros((cells, lanes), F32)
        for c in range(blocks):
            centred = x[c, t].astype(F32) - average
            square = square + centred * centred
        variance = jnp.sum(square, axis=1, keepdims=True) * (1.0 / width)
        inv = lax.rsqrt(variance + NORM_EPS)
        inverse[t] = jnp.broadcast_to(inv, (cells, lanes))
        for c in range(blocks):
            std = (x[c, t].astype(F32) - average) * inv
            standard[c, t] = std
            normed[t, :, c * lanes : (c + 1) * lanes] = (std * gain[c, 0:1, :]).astype(BF16)

    def product(left, right, put):
        wide_n = 256
        value = left[...].reshape(flat, width)
        for n in range(width // wide_n):
            made = jnp.dot(value, right[:, n * wide_n : (n + 1) * wide_n], preferred_element_type=F32)
            for half in range(wide_n // lanes):
                c = n * (wide_n // lanes) + half
                put(c, made[:, half * lanes : (half + 1) * lanes].reshape(tiles, cells, lanes))

    def put_hidden(c, value):
        slope_h[c] = value

    loads[0].wait()
    product(normed, w_in, put_hidden)
    save_normed = pltpu.make_async_copy(normed, normed_hbm.at[pl.ds(chunk * tiles, tiles)], sem.at[6])
    save_normed.start()

    @pl.loop(0, blocks * tiles)
    def _(n):
        c, t = n % blocks, n // blocks
        h = slope_h[c, t]
        sig = jax.nn.sigmoid(h)
        a = h * sig
        slope_h[c, t] = sig * (1.0 + h * (1.0 - sig))
        act[c, t, pl.ds(PAD, cells), :] = a

        def column_sum(b):
            made = None
            for r in range(3):
                term = taps[c, 3 * r + b : 3 * r + b + 1, :] * act[c, t, pl.ds(PAD + side * (r - 1) + b - 1, cells), :]
                made = term if made is None else made + term
            return made

        spatial = column_sum(1) + masks[0] * column_sum(0) + masks[1] * column_sum(2)
        sig = jax.nn.sigmoid(spatial)
        mix = spatial * sig
        mixed[c, t] = mix
        slope_s[c, t] = sig * (1.0 + spatial * (1.0 - sig))
        squeeze[c, pl.ds(t, 1), :] = jnp.sum(mix, axis=0, keepdims=True) * (1.0 / cells)

    def joined(ref):
        return jnp.concatenate([ref[c] for c in range(blocks)], axis=1)

    squeezed = joined(squeeze)
    squeeze_pre = exact_dot(squeezed, se_down[...])
    sig_pre = jax.nn.sigmoid(squeeze_pre)
    squeeze_act = squeeze_pre * sig_pre
    excited = jax.nn.sigmoid(exact_dot(squeeze_act, se_up[...]))
    for c in range(blocks):
        excite[c] = excited[:, c * lanes : (c + 1) * lanes]

    def put_back(c, value):
        wide[c] = value

    loads[3].wait()
    product(up, w_out_t, put_back)

    @pl.loop(0, tiles)
    def _(t):
        for c in range(blocks):
            mix = mixed[c, t]
            scaled[t, :, c * lanes : (c + 1) * lanes] = (mix * excite[c, pl.ds(t, 1), :]).astype(BF16)
            extra[c, pl.ds(t, 1), :] = jnp.sum(wide[c, t] * mix, axis=0, keepdims=True)

    back_pre = joined(extra) * excited * (1.0 - excited)
    back_squeeze_pre = exact_dot(back_pre, se_up_t[...]) * (
        sig_pre * (1.0 + squeeze_pre * (1.0 - sig_pre))
    )
    back_squeeze = exact_dot(back_squeeze_pre, se_down_t[...]) * (1.0 / cells)
    for c in range(blocks):
        extra[c] = back_squeeze[:, c * lanes : (c + 1) * lanes]
    small_a[0] = squeezed
    small_a[1] = back_pre
    small_b[0] = back_squeeze_pre
    small_b[1] = squeeze_act

    def put_visual(c, value):
        vis[:, :, c * lanes : (c + 1) * lanes] = (x[c].astype(F32) + value).astype(BF16)

    loads[2].wait()
    product(scaled, w_out, put_visual)
    save_scaled = pltpu.make_async_copy(scaled, scaled_hbm.at[pl.ds(chunk * tiles, tiles)], sem.at[7])
    save_scaled.start()
    save_vis = pltpu.make_async_copy(vis, vis_hbm.at[pl.ds(chunk * tiles, tiles)], sem.at[8])
    save_vis.start()
    save_normed.wait()

    @pl.loop(0, tiles)
    def _(t):
        for c in range(blocks):
            back = (wide[c, t] * excite[c, pl.ds(t, 1), :] + extra[c, pl.ds(t, 1), :]) * slope_s[c, t]
            tmp[pl.ds(PAD, cells), :] = back
            sides = (back * masks[0], back, back * masks[1])
            for r in range(3):
                for b in range(3):
                    term = sides[b] * act[c, t, pl.ds(PAD + side * (r - 1) + b - 1, cells), :]
                    kacc[c, 3 * r + b] += jnp.sum(term.reshape(cells // 8, 8, lanes), axis=0)

            def column_sum(b, c=c):
                made = None
                for r in range(3):
                    term = taps[c, 3 * r + b : 3 * r + b + 1, :] * tmp[pl.ds(PAD - side * (r - 1) - (b - 1), cells), :]
                    made = term if made is None else made + term
                return made

            back_act = column_sum(1) + masks[1] * column_sum(0) + masks[0] * column_sum(2)
            normed[t, :, c * lanes : (c + 1) * lanes] = (back_act * slope_h[c, t]).astype(BF16)

    loads[4].wait()
    product(normed, w_in_t, put_back)
    save_hidden = pltpu.make_async_copy(normed, hidden_hbm.at[pl.ds(chunk * tiles, tiles)], sem.at[9])
    save_hidden.start()

    @pl.loop(0, tiles)
    def _(t):
        centre = jnp.zeros((cells, lanes), F32)
        along = jnp.zeros((cells, lanes), F32)
        for c in range(blocks):
            along_n = wide[c, t] * standard[c, t]
            gacc[c] += jnp.sum(along_n.reshape(cells // 8, 8, lanes), axis=0)
            centre = centre + wide[c, t] * gain[c, 0:1, :]
            along = along + along_n * gain[c, 0:1, :]
        centre = jnp.sum(centre, axis=1, keepdims=True) * (1.0 / width)
        along = jnp.sum(along, axis=1, keepdims=True) * (1.0 / width)
        inv = inverse[t]
        for c in range(blocks):
            made = up[t, :, c * lanes : (c + 1) * lanes].astype(F32) + inv * (
                wide[c, t] * gain[c, 0:1, :] - centre - standard[c, t] * along
            )
            rows_v[c, t] = made.astype(BF16)

    save_back = [
        pltpu.make_async_copy(rows_v.at[partner(me, k, columns, 1)], pick(back_hbm, me, k, 1), sem.at[10 + columns + k])
        for k in range(columns)
    ]
    for one in save_back:
        one.start()
    small_k[...] = jnp.zeros_like(small_k)
    for c in range(blocks):
        for r in range(9):
            small_k[r : r + 1, c * lanes : (c + 1) * lanes] = jnp.sum(kacc[c, r], axis=0, keepdims=True)
        small_k[9:10, c * lanes : (c + 1) * lanes] = jnp.sum(gacc[c], axis=0, keepdims=True)
    save_scaled.wait()
    save_vis.wait()
    save_hidden.wait()
    for one in save_back:
        one.wait()


def run_block(chunk, side, info, x, up, weights, carried, joined):
    tiles, cells, lanes = x[0].shape[-3:]
    blocks = columns = up.shape[-1] // lanes
    backs = parts_of(columns, (tiles, cells, lanes), joined)
    size = blocks * tiles * cells * lanes
    width = blocks * lanes
    narrow = weights[4].shape[1]
    whole = jax.ShapeDtypeStruct(up.shape, BF16)
    fixed = [info, *x, up, *weights]
    field = pltpu.VMEM((blocks, tiles, cells, lanes), F32)
    packed = pltpu.VMEM((tiles, cells, width), BF16)
    eight = pltpu.VMEM((blocks, 8, lanes), F32)
    square = pltpu.VMEM((width, width), BF16)
    flops = 8 * tiles * cells * width * width
    return pl.pallas_call(
        functools.partial(block_kernel, chunk, side, columns, len(x), len(backs)),
        in_specs=[SMEM] + [ANY] * (len(x) + 5) + [VMEM] * 6 + [ANY] * len(carried),
        out_specs=[ANY] * (4 + len(backs)) + [VMEM] * 3,
        out_shape=[whole] * 4
        + backs
        + [
            jax.ShapeDtypeStruct((2, 8, width), F32),
            jax.ShapeDtypeStruct((2, 8, narrow), F32),
            jax.ShapeDtypeStruct((16, width), F32),
        ],
        input_output_aliases={len(fixed) + n: n for n in range(len(carried))},
        scratch_shapes=[
            pltpu.VMEM((blocks, tiles, cells, lanes), BF16),
            packed,
            square,
            square,
            square,
            square,
            field,
            pltpu.VMEM((tiles, cells, lanes), F32),
            field,
            pltpu.VMEM((blocks, tiles, cells + 2 * PAD, lanes), F32),
            field,
            field,
            field,
            pltpu.VMEM((cells + 2 * PAD, lanes), F32),
            pltpu.VMEM((2, cells, lanes), F32),
            [
                pltpu.VMEM((blocks, tiles, cells, lanes), BF16),
                eight,
                eight,
                eight,
                pltpu.VMEM((blocks, 9, 8, lanes), F32),
                eight,
                packed,
                packed,
                packed,
            ],
            pltpu.SemaphoreType.DMA((10 + 2 * columns,)),
        ],
        compiler_params=params(),
        cost_estimate=pl.CostEstimate(
            flops=flops, bytes_accessed=16 * size + 8 * width * width, transcendentals=2 * size
        ),
        name="block_%d" % chunk,
    )(*fixed, *carried)


def weights_kernel(chunks, columns, info_ref, normed, scaled, hidden, up, *rest):
    smalls, (home, away, held) = rest[: 5 * chunks], rest[5 * chunks :]
    count, cells, wide = normed.shape
    flat = count * cells
    width = hidden.shape[2]
    me = info_ref[1]
    ring = columns // 2
    made = []
    for left, right in ((normed, hidden), (scaled, up)):
        made.append(
            lax.dot_general(
                left[...].reshape(flat, wide),
                right[...].reshape(flat, width),
                (((0,), (0,)), ((), ())),
                preferred_element_type=F32,
            )
        )

    def outer(left, right):
        return lax.dot_general(
            jnp.concatenate(left, axis=0),
            jnp.concatenate(right, axis=0),
            (((0,), (0,)), ((), ())),
            preferred_element_type=F32,
            precision=lax.Precision.HIGHEST,
        )

    quarter = lax.rem(lax.broadcasted_iota(jnp.int32, (8, wide), 1), 4)
    pair = [lax.broadcasted_iota(jnp.int32, (16, LANES), n) for n in range(2)]
    same = jnp.where(pair[0] == pair[1], 1.0, 0.0).astype(F32)
    each = [smalls[5 * h : 5 * h + 5] for h in range(chunks)]
    narrow = each[0][2].shape[2]
    down = outer([e[0][0] for e in each], [e[2][0] for e in each])
    lift = outer(
        [jnp.where(quarter == m, e[3][...], 0.0) for e in each for m in range(4)],
        [e[1][0, :, m * narrow : (m + 1) * narrow] for e in each for m in range(4)],
    )
    taps = outer([sum(e[4][...] for e in each)], [same])
    place = 0
    for value in (*made, down, lift, taps):
        held[:, place : place + value.shape[1]] = value
        place += value.shape[1]
    line = home.shape[1]
    for step in range(line):
        group = lax.rem(info_ref[4] + step, line)
        for k in range(columns):
            row = pl.multiple_of(8 * (columns * group + partner(me, k, columns, 1)), 8)
            target = home if k % 2 == 0 else away
            target[k // 2, step, 0] = held[pl.ds(row, 8), :].astype(BF16)


def weight_terms(info, normed, scaled, hidden, up, small, columns):
    count, cells, width = normed.shape
    narrow = small[0][1].shape[2]
    lanes = 2 * width + 2 * narrow + LANES
    line = math.isqrt(width // (8 * columns))
    wide = width // line
    left = pl.BlockSpec((count, cells, wide), lambda i, s: (0, 0, i))
    right = pl.BlockSpec((count, cells, width), lambda i, s: (0, 0, 0), pipeline_mode=pl.Buffered(1))
    args, specs = [], []
    for a, b, k in small:
        args += [a, a, b, jnp.repeat(b[1], 4, axis=1), k]
        specs += [
            pl.BlockSpec((1, 8, wide), lambda i, s: (0, 0, i)),
            pl.BlockSpec((1, 8, width), lambda i, s: (1, 0, 0)),
            pl.BlockSpec((1, 8, narrow), lambda i, s: (0, 0, 0)),
            pl.BlockSpec((8, wide), lambda i, s: (0, i)),
            pl.BlockSpec((16, wide), lambda i, s: (0, i)),
        ]
    part = jax.ShapeDtypeStruct((columns // 2, line, line, 8, lanes), BF16)
    out = pl.BlockSpec((columns // 2, line, 1, 8, lanes), lambda i, s: (0, 0, lax.rem(i - s[3] + line, line), 0, 0))
    return pl.pallas_call(
        functools.partial(weights_kernel, len(small), columns),
        grid_spec=pltpu.PrefetchScalarGridSpec(
            num_scalar_prefetch=1,
            grid=(line,),
            in_specs=[left, left, right, right] + specs,
            out_specs=[out] * 2,
            scratch_shapes=[pltpu.VMEM((wide, lanes), F32)],
        ),
        out_shape=[part] * 2,
        compiler_params=params(),
        cost_estimate=pl.CostEstimate(
            flops=4 * count * cells * width * width, bytes_accessed=8 * count * cells * width, transcendentals=0
        ),
        name="weight_terms",
    )(info, normed, scaled, hidden, up, *args)


def spread_kernel(per, own_ref, pos_ref, *rest):
    arrived, out, (held, wide, sem) = rest[:CHUNKS], rest[CHUNKS], rest[CHUNKS + 1 :]
    step = pl.program_id(0)
    slots = arrived[0].shape[1]
    count = held.shape[0]
    side = out.shape[1] // 2
    width = 2 * side

    @pl.when(step == 0)
    def _():
        @pl.loop(0, count)
        def _(j):
            position = pos_ref[j]
            for h in range(CHUNKS):

                @pl.when(position // slots == h)
                def _(h=h):
                    pltpu.make_async_copy(
                        arrived[h].at[own_ref[j], position - h * slots], held.at[j], sem
                    ).start()

        @pl.loop(0, count)
        def _(j):
            pltpu.make_async_copy(arrived[0].at[0, 0], held.at[0], sem).wait()

    for n in range(per):
        quarter = held[step * per + n].astype(F32) * 0.25
        wide[pl.ds(0, side * side, stride=2), :] = quarter
        wide[pl.ds(1, side * side, stride=2), :] = quarter
        for row in range(side):
            line = wide[pl.ds(row * width, width), :].astype(BF16)
            out[n, 2 * row] = line
            out[n, 2 * row + 1] = line


def unpack_and_spread(arrived, own, pos, count, grid):
    _, _, cells, channels = arrived[0].shape
    per = 4
    return pl.pallas_call(
        functools.partial(spread_kernel, per),
        grid=(count // per,),
        in_specs=[SMEM, SMEM] + [ANY] * CHUNKS,
        out_specs=pl.BlockSpec((per, grid, grid, channels), lambda i: (i, 0, 0, 0)),
        out_shape=jax.ShapeDtypeStruct((count, grid, grid, channels), BF16),
        scratch_shapes=[
            pltpu.VMEM((count, cells, channels), BF16),
            pltpu.VMEM((grid * grid // 2, channels), F32),
            pltpu.SemaphoreType.DMA,
        ],
        compiler_params=params(),
        cost_estimate=pl.CostEstimate(
            flops=0, bytes_accessed=10 * count * cells * channels, transcendentals=0
        ),
        name="unpack_and_spread",
    )(own, pos, *arrived)


def before(table):
    groups = table.shape[1]
    index = jnp.arange(groups, dtype=jnp.int32)
    lower = index[None, :] < index[:, None]
    return jnp.sum(jnp.where(lower[None], table[:, None, :], 0), axis=2, dtype=jnp.int32)


def routing(counts, owners, ranks, group_id, local_tiles, capacity):
    groups = counts.shape[0]
    start = before(counts)
    flat_counts, flat_owners, flat_ranks = counts.reshape(-1), owners.reshape(-1), ranks.reshape(-1)
    ahead = (flat_owners[:, None] == flat_owners[None, :]) & (flat_ranks[None, :] < flat_ranks[:, None])
    offset = jnp.sum(jnp.where(ahead, flat_counts[None, :], 0), axis=1, dtype=jnp.int32).reshape(groups, groups)
    sources = jnp.arange(groups, dtype=jnp.int32)
    mine = (sources == group_id)[:, None]

    def row(table):
        return jnp.sum(jnp.where(mine, table, 0), axis=0, dtype=jnp.int32)

    owner_row, start_row, offset_row = row(owners), row(start), row(offset)
    ids = jnp.arange(local_tiles, dtype=jnp.int32)
    member = jnp.sum((start_row[None, :] <= ids[:, None]).astype(jnp.int32), axis=1, dtype=jnp.int32) - 1
    which = member[:, None] == sources[None, :]
    own = jnp.sum(jnp.where(which, owner_row[None, :], 0), axis=1, dtype=jnp.int32)
    slot = jnp.sum(jnp.where(which, (offset_row - start_row)[None, :], 0), axis=1, dtype=jnp.int32) + ids
    arriving = owners == group_id
    recv_count = jnp.sum(jnp.where(arriving, counts, 0), axis=1, dtype=jnp.int32)
    recv_offset = jnp.sum(jnp.where(arriving, offset, 0), axis=1, dtype=jnp.int32)
    positions = jnp.arange(capacity, dtype=jnp.int32)
    inside = (positions[:, None] >= recv_offset[None, :]) & (
        positions[:, None] < (recv_offset + recv_count)[None, :]
    )
    table = jnp.sum(jnp.where(inside, sources[None, :], 0), axis=1, dtype=jnp.int32)
    filled = jnp.sum(recv_count, dtype=jnp.int32).reshape(1)
    return own, slot, table, filled


def local(
    tiles,
    w_in,
    w_out,
    se_down,
    se_up,
    kernel,
    gain,
    token_grads,
    tile_counts,
    sample_owner,
    sample_rank,
):
    groups = lax.axis_size("enc")
    columns = lax.axis_size("abs")
    group_id = lax.axis_index("enc")
    column_id = lax.axis_index("abs")
    local_tiles, grid = tiles.shape[0], tiles.shape[1]
    per, cells, width = token_grads.shape
    capacity = per * columns
    side = grid // 2
    slots = per // CHUNKS
    blocks = width // LANES
    own, slot, table, filled = routing(
        tile_counts, sample_owner, sample_rank, group_id, local_tiles, capacity
    )
    pos = slot % per
    line = math.isqrt(groups)
    info = jnp.stack(
        [filled[0], column_id.astype(jnp.int32), jnp.int32(per), group_id // line, lax.rem(group_id, line)]
    )
    sends = pool_and_pack(tiles, own, pos, groups, slots)

    taps = jnp.pad(kernel.astype(F32).reshape(9, blocks, LANES).transpose(1, 0, 2), ((0, 0), (0, 7), (0, 0)))
    gains = jnp.broadcast_to(gain.astype(F32).reshape(blocks, 1, LANES), (blocks, 8, LANES))
    weights = [w_in, w_out, w_in.T, w_out.T, se_down, se_up, se_down.T, se_up.T, taps, gains]

    inner = []
    for h in range(CHUNKS):
        send = sends[h]
        if h > 0:
            send, _ = lax.optimization_barrier((send, received))
        received = lax.all_to_all(send, "enc", split_axis=0, concat_axis=0, tiled=True)
        if h == 0:
            received, *weights = lax.optimization_barrier((received, *weights))
        parts = route([received], table, info, h, per, columns, groups, False, h > 0)
        if h > 0:
            inner[-1], parts = lax.optimization_barrier((inner[-1], parts))
        inner.append(exchange(parts))

    carried = []
    arrived, small, narrowed, backs = [], [], [], []
    for h in range(CHUNKS):
        made = run_block(h, side, info, inner[h], token_grads, weights, carried, h == 0)
        carried = list(made[:4])
        small.append(made[-3:])
        narrowed.append(exchange(made[4:-3]))
    narrowed[0], carried = lax.optimization_barrier((narrowed[0], carried))
    for h in range(CHUNKS):
        back = route(narrowed[h], table, info, h, per, columns, groups, True)
        if h == 0:
            _, carried, narrowed[-1][1:4] = lax.optimization_barrier((back, carried, narrowed[-1][1:4]))
        arrived.append(lax.all_to_all(back, "enc", split_axis=0, concat_axis=0, tiled=True))
    last = (back, arrived[0])
    visual, normed, scaled, hidden = carried

    home, away = weight_terms(info, normed, scaled, hidden, token_grads, small, columns)
    home, (_, arrived[0]) = lax.optimization_barrier((home, last))
    near = lax.ppermute(away, "abs", partner_pairs(1, columns))
    pair = [(home[k].astype(F32) + near[k].astype(F32)).astype(BF16) for k in range(columns // 2)]
    rows = [pair[0]] + [
        lax.ppermute(pair[k], "abs", partner_pairs(2 * k, columns)) for k in range(1, columns // 2)
    ]

    def along(parts, pairs):
        sent = [parts[0]] + [lax.ppermute(parts[k], "enc", pairs(k)) for k in range(1, line)]
        return sum(r.astype(F32) for r in sent)

    parts = [sum(r[k].astype(F32) for r in rows).astype(BF16) for k in range(line)]
    row = along(parts, lambda k: [(n, n // line * line + (n + k) % line) for n in range(groups)])
    parts = [row[k].astype(BF16) for k in range(line)]
    total = along(parts, lambda k: [(n, (n + k * line) % groups) for n in range(groups)])
    total = total * (1.0 / math.sqrt(groups * local_tiles * cells))
    tile_grads = unpack_and_spread(arrived, own, pos, local_tiles, grid)
    narrow = se_down.shape[1]
    ends = [width, 2 * width, 2 * width + narrow, 2 * width + 2 * narrow]
    last = total[:, ends[3] : ends[3] + 10]
    return (
        visual,
        tile_grads,
        total[:, : ends[0]],
        total[:, ends[0] : ends[1]],
        total[:, ends[1] : ends[2]],
        total[:, ends[2] : ends[3]].reshape(2, width),
        last[:, :9].T,
        last[:, 9],
    )


def solution(mesh):
    return jax.shard_map(
        local,
        mesh=mesh,
        in_specs=(
            P("enc", None, None, "abs"),
            P(),
            P(),
            P(),
            P(),
            P(),
            P(),
            P(("enc", "abs"), None, None),
            P(),
            P(),
            P(),
        ),
        out_specs=(
            P(("enc", "abs"), None, None),
            P("enc", None, None, "abs"),
            P(("enc", "abs"), None),
            P(("enc", "abs"), None),
            P(("enc", "abs"), None),
            P(("enc", "abs"), None),
            P(None, ("enc", "abs")),
            P(("enc", "abs")),
        ),
        check_vma=False,
    )
```

```python
import functools
import math

import jax
import jax.numpy as jnp
from jax import lax
from jax.experimental import pallas as pl
from jax.experimental.pallas import tpu as pltpu
from jax.sharding import PartitionSpec as P

F32 = jnp.float32
BF16 = jnp.bfloat16
NORM_EPS = 1e-06
LANES = 128
PAD = 16
CHUNKS = 2
VMEM_BYTES = 60 * 1024 * 1024
ANY = pl.BlockSpec(memory_space=pl.ANY)
SMEM = pl.BlockSpec(memory_space=pltpu.SMEM)
VMEM = pl.BlockSpec(memory_space=pltpu.VMEM)


def params(**more):
    return pltpu.CompilerParams(vmem_limit_bytes=VMEM_BYTES, **more)


def pool_kernel(steps, per, own_ref, pos_ref, tiles_ref, *rest):
    outs, (wide, pooled, sem) = rest[:CHUNKS], rest[CHUNKS:]
    step = pl.program_id(0)
    side = tiles_ref.shape[1] // 2
    width = 2 * side
    slots = outs[0].shape[1]
    for n in range(per):
        for row in range(side):
            pair = tiles_ref[n, 2 * row].astype(F32) + tiles_ref[n, 2 * row + 1].astype(F32)
            wide[pl.ds(row * width, width), :] = pair
        total = wide[pl.ds(0, side * side, stride=2), :] + wide[pl.ds(1, side * side, stride=2), :]
        j = step * per + n
        pooled[j] = (total * 0.25).astype(BF16)
        position = pos_ref[j]
        for h in range(CHUNKS):

            @pl.when(position // slots == h)
            def _(h=h):
                pltpu.make_async_copy(
                    pooled.at[j], outs[h].at[own_ref[j], position - h * slots], sem
                ).start()

    @pl.when(step == steps - 1)
    def _():
        @pl.loop(0, steps * per)
        def _(j):
            pltpu.make_async_copy(pooled.at[0], outs[0].at[0, 0], sem).wait()


def pool_and_pack(tiles, own, pos, groups, slots):
    count, grid, _, channels = tiles.shape
    cells = grid * grid // 4
    per = 4
    steps = count // per
    made = jax.ShapeDtypeStruct((groups, slots, cells, channels), BF16)
    return pl.pallas_call(
        functools.partial(pool_kernel, steps, per),
        grid=(steps,),
        in_specs=[SMEM, SMEM, pl.BlockSpec((per, grid, grid, channels), lambda i: (i, 0, 0, 0))],
        out_specs=[ANY] * CHUNKS,
        out_shape=[made] * CHUNKS,
        scratch_shapes=[
            pltpu.VMEM((grid * grid // 2, channels), F32),
            pltpu.VMEM((count, cells, channels), BF16),
            pltpu.SemaphoreType.DMA,
        ],
        compiler_params=params(),
        cost_estimate=pl.CostEstimate(flops=tiles.size, bytes_accessed=tiles.size * 3, transcendentals=0),
        name="pool_and_pack",
    )(own, pos, tiles)


def partner(me, step, columns, sign):
    ring = columns // 2
    z = lax.rem(me // 2 + sign * (step // 2) + ring, ring)
    return 2 * z + lax.rem(lax.rem(me, 2) + step % 2, 2)


def partner_pairs(step, columns):
    ring = columns // 2
    return [(n, 2 * ((n // 2 + step // 2) % ring) + (n % 2 + step) % 2) for n in range(columns)]


def exchange(parts):
    columns = len(parts)
    if columns == 1:
        return [lax.all_to_all(parts[0], "abs", split_axis=0, concat_axis=0, tiled=True)]
    return [parts[0]] + [lax.ppermute(parts[k], "abs", partner_pairs(k, columns)) for k in range(1, columns)]


def pick(refs, me, step, sign):
    if len(refs) > 1:
        return refs[step]
    return refs[0].at[partner(me, step, refs[0].shape[0], sign)]


def route_kernel(chunk, per, columns, back, table_ref, info_ref, *rest):
    (srcs, outs) = (rest[:-2], rest[-2:-1]) if back else (rest[:1], rest[1:-1])
    sem = rest[-1]
    filled, me = info_ref[0], info_ref[1]
    whole = outs[0] if back else srcs[0]
    slots = whole.shape[1]

    def each(act):
        for k in range(columns):
            first = partner(me, k, columns, -1 if back else 1) * per + chunk * slots
            part = pick(srcs, me, k, -1) if back else pick(outs, me, k, 1)

            @pl.loop(0, slots)
            def _(local, part=part, first=first):
                q = first + local

                @pl.when(q < filled)
                def _():
                    there = whole.at[table_ref[q], local]
                    here = part.at[local]
                    act(pltpu.make_async_copy(*((here, there) if back else (there, here)), sem))

    each(lambda one: one.start())
    each(lambda one: one.wait())


def parts_of(columns, shape, joined):
    if joined:
        return [jax.ShapeDtypeStruct((columns, *shape), BF16)]
    return [jax.ShapeDtypeStruct(shape, BF16)] * columns


def route(sources, table, info, chunk, per, columns, groups, back, joined=False):
    slots, cells, channels = sources[0].shape[-3:]
    parts = parts_of(columns, (slots, cells, channels), joined)
    whole = jax.ShapeDtypeStruct((groups, slots, cells, channels), BF16)
    return pl.pallas_call(
        functools.partial(route_kernel, chunk, per, columns, back),
        in_specs=[SMEM, SMEM] + [VMEM] * len(sources),
        out_specs=ANY if back else [ANY] * len(parts),
        out_shape=whole if back else parts,
        scratch_shapes=[pltpu.SemaphoreType.DMA],
        compiler_params=pltpu.CompilerParams(vmem_limit_bytes=16 * 1024 * 1024),
        cost_estimate=pl.CostEstimate(
            flops=0, bytes_accessed=8 * columns * slots * cells * channels, transcendentals=0
        ),
        name="route_back" if back else "route_in",
    )(table, info, *sources)


def exact_dot(left, weights):
    rows = left.shape[0]
    first = left.astype(BF16).astype(F32)
    rest = left - first
    second = rest.astype(BF16).astype(F32)
    third = rest - second
    stacked = jnp.concatenate([first, second, third, jnp.zeros_like(left)], axis=0).astype(BF16)
    made = jnp.dot(stacked, weights, preferred_element_type=F32)
    return made[:rows] + made[rows : 2 * rows] + made[2 * rows : 3 * rows]


def block_kernel(
    chunk,
    side,
    columns,
    parts_in,
    parts_out,
    info_ref,
    *rest,
):
    x_hbm, rest = rest[:parts_in], rest[parts_in:]
    up_hbm, w_in_hbm, w_out_hbm, w_in_t_hbm, w_out_t_hbm = rest[:5]
    se_down, se_up, se_down_t, se_up_t, taps, gain = rest[5:11]
    outs = rest[-24 - parts_out : -17]
    (vis_hbm, normed_hbm, scaled_hbm, hidden_hbm), back_hbm = outs[:4], outs[4 : 4 + parts_out]
    small_a, small_b, small_k = outs[4 + parts_out :]
    filled, me = info_ref[0], info_ref[1]
    live = filled - me * info_ref[2]
    (
        x,
        up,
        w_in,
        w_out,
        w_in_t,
        w_out_t,
        standard,
        inverse,
        slope_h,
        act,
        mixed,
        slope_s,
        wide,
        tmp,
        masks,
        stage,
        sem,
    ) = rest[-17:]
    (rows_v, squeeze, excite, extra, kacc, gacc, normed, scaled, vis) = stage
    blocks, tiles, cells, lanes = x.shape
    width = blocks * lanes
    flat = tiles * cells
    loads = [
        pltpu.make_async_copy(a, b, sem.at[n])
        for n, (a, b) in enumerate(
            [
                (w_in_hbm, w_in),
                (up_hbm.at[pl.ds(chunk * tiles, tiles)], up),
                (w_out_hbm, w_out),
                (w_out_t_hbm, w_out_t),
                (w_in_t_hbm, w_in_t),
            ]
        )
    ]
    x_loads = [
        pltpu.make_async_copy(pick(x_hbm, me, k, -1), x.at[partner(me, k, columns, -1)], sem.at[10 + k])
        for k in range(columns)
    ]
    for one in x_loads + loads:
        one.start()

    column = lax.rem(lax.broadcasted_iota(jnp.int32, (cells, lanes), 0), side)
    masks[0] = jnp.where(column != 0, 1.0, 0.0).astype(F32)
    masks[1] = jnp.where(column != side - 1, 1.0, 0.0).astype(F32)
    edge = jnp.zeros((PAD, lanes), F32)
    tmp[pl.ds(0, PAD), :] = edge
    tmp[pl.ds(PAD + cells, PAD), :] = edge
    kacc[...] = jnp.zeros_like(kacc)
    gacc[...] = jnp.zeros_like(gacc)
    squeeze[...] = jnp.zeros_like(squeeze)
    extra[...] = jnp.zeros_like(extra)

    @pl.loop(0, blocks * tiles)
    def _(n):
        c, t = n % blocks, n // blocks
        act[c, t, pl.ds(0, PAD), :] = edge
        act[c, t, pl.ds(PAD + cells, PAD), :] = edge

    for one in x_loads:
        one.wait()
    loads[1].wait()
    for t in range(tiles):

        @pl.when(chunk * tiles + t >= live)
        def _(t=t):
            up[t] = jnp.zeros(up.shape[1:], BF16)
            for c in range(blocks):
                x[c, t] = jnp.zeros((cells, lanes), BF16)

    @pl.loop(0, tiles)
    def _(t):
        total = x[0, t].astype(F32)
        for c in range(1, blocks):
            total = total + x[c, t].astype(F32)
        average = jnp.sum(total, axis=1, keepdims=True) * (1.0 / width)
        square = jnp.zeros((cells, lanes), F32)
        for c in range(blocks):
            centred = x[c, t].astype(F32) - average
            square = square + centred * centred
        variance = jnp.sum(square, axis=1, keepdims=True) * (1.0 / width)
        inv = lax.rsqrt(variance + NORM_EPS)
        inverse[t] = jnp.broadcast_to(inv, (cells, lanes))
        for c in range(blocks):
            std = (x[c, t].astype(F32) - average) * inv
            standard[c, t] = std
            normed[t, :, c * lanes : (c + 1) * lanes] = (std * gain[c, 0:1, :]).astype(BF16)

    def product(left, right, put):
        wide_n = 256
        value = left[...].reshape(flat, width)
        for n in range(width // wide_n):
            made = jnp.dot(value, right[:, n * wide_n : (n + 1) * wide_n], preferred_element_type=F32)
            for half in range(wide_n // lanes):
                c = n * (wide_n // lanes) + half
                put(c, made[:, half * lanes : (half + 1) * lanes].reshape(tiles, cells, lanes))

    def put_hidden(c, value):
        slope_h[c] = value

    loads[0].wait()
    product(normed, w_in, put_hidden)
    save_normed = pltpu.make_async_copy(normed, normed_hbm.at[pl.ds(chunk * tiles, tiles)], sem.at[6])
    save_normed.start()

    @pl.loop(0, blocks * tiles)
    def _(n):
        c, t = n % blocks, n // blocks
        h = slope_h[c, t]
        sig = jax.nn.sigmoid(h)
        a = h * sig
        slope_h[c, t] = sig * (1.0 + h * (1.0 - sig))
        act[c, t, pl.ds(PAD, cells), :] = a

        def column_sum(b):
            made = None
            for r in range(3):
                term = taps[c, 3 * r + b : 3 * r + b + 1, :] * act[c, t, pl.ds(PAD + side * (r - 1) + b - 1, cells), :]
                made = term if made is None else made + term
            return made

        spatial = column_sum(1) + masks[0] * column_sum(0) + masks[1] * column_sum(2)
        sig = jax.nn.sigmoid(spatial)
        mix = spatial * sig
        mixed[c, t] = mix
        slope_s[c, t] = sig * (1.0 + spatial * (1.0 - sig))
        squeeze[c, pl.ds(t, 1), :] = jnp.sum(mix, axis=0, keepdims=True) * (1.0 / cells)

    def joined(ref):
        return jnp.concatenate([ref[c] for c in range(blocks)], axis=1)

    squeezed = joined(squeeze)
    squeeze_pre = exact_dot(squeezed, se_down[...])
    sig_pre = jax.nn.sigmoid(squeeze_pre)
    squeeze_act = squeeze_pre * sig_pre
    excited = jax.nn.sigmoid(exact_dot(squeeze_act, se_up[...]))
    for c in range(blocks):
        excite[c] = excited[:, c * lanes : (c + 1) * lanes]

    def put_back(c, value):
        wide[c] = value

    loads[3].wait()
    product(up, w_out_t, put_back)

    @pl.loop(0, tiles)
    def _(t):
        for c in range(blocks):
            mix = mixed[c, t]
            scaled[t, :, c * lanes : (c + 1) * lanes] = (mix * excite[c, pl.ds(t, 1), :]).astype(BF16)
            extra[c, pl.ds(t, 1), :] = jnp.sum(wide[c, t] * mix, axis=0, keepdims=True)

    back_pre = joined(extra) * excited * (1.0 - excited)
    back_squeeze_pre = exact_dot(back_pre, se_up_t[...]) * (
        sig_pre * (1.0 + squeeze_pre * (1.0 - sig_pre))
    )
    back_squeeze = exact_dot(back_squeeze_pre, se_down_t[...]) * (1.0 / cells)
    for c in range(blocks):
        extra[c] = back_squeeze[:, c * lanes : (c + 1) * lanes]
    small_a[0] = squeezed
    small_a[1] = back_pre
    small_b[0] = back_squeeze_pre
    small_b[1] = squeeze_act

    def put_visual(c, value):
        vis[:, :, c * lanes : (c + 1) * lanes] = (x[c].astype(F32) + value).astype(BF16)

    loads[2].wait()
    product(scaled, w_out, put_visual)
    save_scaled = pltpu.make_async_copy(scaled, scaled_hbm.at[pl.ds(chunk * tiles, tiles)], sem.at[7])
    save_scaled.start()
    save_vis = pltpu.make_async_copy(vis, vis_hbm.at[pl.ds(chunk * tiles, tiles)], sem.at[8])
    save_vis.start()
    save_normed.wait()

    @pl.loop(0, tiles)
    def _(t):
        for c in range(blocks):
            back = (wide[c, t] * excite[c, pl.ds(t, 1), :] + extra[c, pl.ds(t, 1), :]) * slope_s[c, t]
            tmp[pl.ds(PAD, cells), :] = back
            sides = (back * masks[0], back, back * masks[1])
            for r in range(3):
                for b in range(3):
                    term = sides[b] * act[c, t, pl.ds(PAD + side * (r - 1) + b - 1, cells), :]
                    kacc[c, 3 * r + b] += jnp.sum(term.reshape(cells // 8, 8, lanes), axis=0)

            def column_sum(b, c=c):
                made = None
                for r in range(3):
                    term = taps[c, 3 * r + b : 3 * r + b + 1, :] * tmp[pl.ds(PAD - side * (r - 1) - (b - 1), cells), :]
                    made = term if made is None else made + term
                return made

            back_act = column_sum(1) + masks[1] * column_sum(0) + masks[0] * column_sum(2)
            normed[t, :, c * lanes : (c + 1) * lanes] = (back_act * slope_h[c, t]).astype(BF16)

    loads[4].wait()
    product(normed, w_in_t, put_back)
    save_hidden = pltpu.make_async_copy(normed, hidden_hbm.at[pl.ds(chunk * tiles, tiles)], sem.at[9])
    save_hidden.start()

    @pl.loop(0, tiles)
    def _(t):
        centre = jnp.zeros((cells, lanes), F32)
        along = jnp.zeros((cells, lanes), F32)
        for c in range(blocks):
            along_n = wide[c, t] * standard[c, t]
            gacc[c] += jnp.sum(along_n.reshape(cells // 8, 8, lanes), axis=0)
            centre = centre + wide[c, t] * gain[c, 0:1, :]
            along = along + along_n * gain[c, 0:1, :]
        centre = jnp.sum(centre, axis=1, keepdims=True) * (1.0 / width)
        along = jnp.sum(along, axis=1, keepdims=True) * (1.0 / width)
        inv = inverse[t]
        for c in range(blocks):
            made = up[t, :, c * lanes : (c + 1) * lanes].astype(F32) + inv * (
                wide[c, t] * gain[c, 0:1, :] - centre - standard[c, t] * along
            )
            rows_v[c, t] = made.astype(BF16)

    save_back = [
        pltpu.make_async_copy(rows_v.at[partner(me, k, columns, 1)], pick(back_hbm, me, k, 1), sem.at[10 + columns + k])
        for k in range(columns)
    ]
    for one in save_back:
        one.start()
    small_k[...] = jnp.zeros_like(small_k)
    for c in range(blocks):
        for r in range(9):
            small_k[r : r + 1, c * lanes : (c + 1) * lanes] = jnp.sum(kacc[c, r], axis=0, keepdims=True)
        small_k[9:10, c * lanes : (c + 1) * lanes] = jnp.sum(gacc[c], axis=0, keepdims=True)
    save_scaled.wait()
    save_vis.wait()
    save_hidden.wait()
    for one in save_back:
        one.wait()


def run_block(chunk, side, info, x, up, weights, carried, joined):
    tiles, cells, lanes = x[0].shape[-3:]
    blocks = columns = up.shape[-1] // lanes
    backs = parts_of(columns, (tiles, cells, lanes), joined)
    size = blocks * tiles * cells * lanes
    width = blocks * lanes
    narrow = weights[4].shape[1]
    whole = jax.ShapeDtypeStruct(up.shape, BF16)
    fixed = [info, *x, up, *weights]
    field = pltpu.VMEM((blocks, tiles, cells, lanes), F32)
    packed = pltpu.VMEM((tiles, cells, width), BF16)
    eight = pltpu.VMEM((blocks, 8, lanes), F32)
    square = pltpu.VMEM((width, width), BF16)
    flops = 8 * tiles * cells * width * width
    return pl.pallas_call(
        functools.partial(block_kernel, chunk, side, columns, len(x), len(backs)),
        in_specs=[SMEM] + [ANY] * (len(x) + 5) + [VMEM] * 6 + [ANY] * len(carried),
        out_specs=[ANY] * (4 + len(backs)) + [VMEM] * 3,
        out_shape=[whole] * 4
        + backs
        + [
            jax.ShapeDtypeStruct((2, 8, width), F32),
            jax.ShapeDtypeStruct((2, 8, narrow), F32),
            jax.ShapeDtypeStruct((16, width), F32),
        ],
        input_output_aliases={len(fixed) + n: n for n in range(len(carried))},
        scratch_shapes=[
            pltpu.VMEM((blocks, tiles, cells, lanes), BF16),
            packed,
            square,
            square,
            square,
            square,
            field,
            pltpu.VMEM((tiles, cells, lanes), F32),
            field,
            pltpu.VMEM((blocks, tiles, cells + 2 * PAD, lanes), F32),
            field,
            field,
            field,
            pltpu.VMEM((cells + 2 * PAD, lanes), F32),
            pltpu.VMEM((2, cells, lanes), F32),
            [
                pltpu.VMEM((blocks, tiles, cells, lanes), BF16),
                eight,
                eight,
                eight,
                pltpu.VMEM((blocks, 9, 8, lanes), F32),
                eight,
                packed,
                packed,
                packed,
            ],
            pltpu.SemaphoreType.DMA((10 + 2 * columns,)),
        ],
        compiler_params=params(),
        cost_estimate=pl.CostEstimate(
            flops=flops, bytes_accessed=16 * size + 8 * width * width, transcendentals=2 * size
        ),
        name="block_%d" % chunk,
    )(*fixed, *carried)


def weights_kernel(chunks, columns, info_ref, normed, scaled, hidden, up, *rest):
    smalls, (home, away, held) = rest[: 5 * chunks], rest[5 * chunks :]
    count, cells, wide = normed.shape
    flat = count * cells
    width = hidden.shape[2]
    me = info_ref[1]
    ring = columns // 2
    made = []
    for left, right in ((normed, hidden), (scaled, up)):
        made.append(
            lax.dot_general(
                left[...].reshape(flat, wide),
                right[...].reshape(flat, width),
                (((0,), (0,)), ((), ())),
                preferred_element_type=F32,
            )
        )

    def outer(left, right):
        return lax.dot_general(
            jnp.concatenate(left, axis=0),
            jnp.concatenate(right, axis=0),
            (((0,), (0,)), ((), ())),
            preferred_element_type=F32,
            precision=lax.Precision.HIGHEST,
        )

    quarter = lax.rem(lax.broadcasted_iota(jnp.int32, (8, wide), 1), 4)
    pair = [lax.broadcasted_iota(jnp.int32, (16, LANES), n) for n in range(2)]
    same = jnp.where(pair[0] == pair[1], 1.0, 0.0).astype(F32)
    each = [smalls[5 * h : 5 * h + 5] for h in range(chunks)]
    narrow = each[0][2].shape[2]
    down = outer([e[0][0] for e in each], [e[2][0] for e in each])
    lift = outer(
        [jnp.where(quarter == m, e[3][...], 0.0) for e in each for m in range(4)],
        [e[1][0, :, m * narrow : (m + 1) * narrow] for e in each for m in range(4)],
    )
    taps = outer([sum(e[4][...] for e in each)], [same])
    place = 0
    for value in (*made, down, lift, taps):
        held[:, place : place + value.shape[1]] = value
        place += value.shape[1]
    for group in range(wide // (8 * columns)):
        for k in range(columns):
            row = pl.multiple_of(8 * (columns * group + partner(me, k, columns, 1)), 8)
            target = home if k % 2 == 0 else away
            target[k // 2, group] = held[pl.ds(row, 8), :].astype(BF16)


def weight_terms(info, normed, scaled, hidden, up, small, columns):
    count, cells, width = normed.shape
    narrow = small[0][1].shape[2]
    wide = 2 * LANES
    lanes = 2 * width + 2 * narrow + LANES
    groups = width // (8 * columns)
    per = wide // (8 * columns)
    left = pl.BlockSpec((count, cells, wide), lambda i: (0, 0, i))
    right = pl.BlockSpec((count, cells, width), lambda i: (0, 0, 0), pipeline_mode=pl.Buffered(1))
    args, specs = [], []
    for a, b, k in small:
        args += [a, a, b, jnp.repeat(b[1], 4, axis=1), k]
        specs += [
            pl.BlockSpec((1, 8, wide), lambda i: (0, 0, i)),
            pl.BlockSpec((1, 8, width), lambda i: (1, 0, 0)),
            pl.BlockSpec((1, 8, narrow), lambda i: (0, 0, 0)),
            pl.BlockSpec((8, wide), lambda i: (0, i)),
            pl.BlockSpec((16, wide), lambda i: (0, i)),
        ]
    part = jax.ShapeDtypeStruct((columns // 2, groups, 8, lanes), BF16)
    return pl.pallas_call(
        functools.partial(weights_kernel, len(small), columns),
        grid=(width // wide,),
        in_specs=[SMEM, left, left, right, right] + specs,
        out_specs=[pl.BlockSpec((columns // 2, per, 8, lanes), lambda i: (0, i, 0, 0))] * 2,
        out_shape=[part] * 2,
        scratch_shapes=[pltpu.VMEM((wide, lanes), F32)],
        compiler_params=params(),
        cost_estimate=pl.CostEstimate(
            flops=4 * count * cells * width * width, bytes_accessed=8 * count * cells * width, transcendentals=0
        ),
        name="weight_terms",
    )(info, normed, scaled, hidden, up, *args)


def spread_kernel(per, own_ref, pos_ref, *rest):
    arrived, (out, wide) = rest[:CHUNKS], rest[CHUNKS:]
    step = pl.program_id(0)
    slots = arrived[0].shape[1]
    side = out.shape[1] // 2
    width = 2 * side
    for n in range(per):
        group, position = own_ref[step * per + n], pos_ref[step * per + n]
        for h in range(CHUNKS):

            @pl.when(position // slots == h)
            def _(h=h):
                quarter = arrived[h][group, position - h * slots].astype(F32) * 0.25
                wide[n, pl.ds(0, side * side, stride=2), :] = quarter
                wide[n, pl.ds(1, side * side, stride=2), :] = quarter

        for row in range(side):
            line = wide[n, pl.ds(row * width, width), :].astype(BF16)
            out[n, 2 * row] = line
            out[n, 2 * row + 1] = line


def unpack_and_spread(arrived, own, pos, count, grid):
    _, _, cells, channels = arrived[0].shape
    per = 4
    return pl.pallas_call(
        functools.partial(spread_kernel, per),
        grid=(count // per,),
        in_specs=[SMEM, SMEM]
        + [pl.BlockSpec(a.shape, lambda i: (0, 0, 0, 0), pipeline_mode=pl.Buffered(1)) for a in arrived],
        out_specs=pl.BlockSpec((per, grid, grid, channels), lambda i: (i, 0, 0, 0)),
        out_shape=jax.ShapeDtypeStruct((count, grid, grid, channels), BF16),
        scratch_shapes=[pltpu.VMEM((per, grid * grid // 2, channels), F32)],
        compiler_params=pltpu.CompilerParams(vmem_limit_bytes=24 * 1024 * 1024),
        cost_estimate=pl.CostEstimate(
            flops=0, bytes_accessed=10 * count * cells * channels, transcendentals=0
        ),
        name="unpack_and_spread",
    )(own, pos, *arrived)


def before(table):
    groups = table.shape[1]
    index = jnp.arange(groups, dtype=jnp.int32)
    lower = index[None, :] < index[:, None]
    return jnp.sum(jnp.where(lower[None], table[:, None, :], 0), axis=2, dtype=jnp.int32)


def routing(counts, owners, ranks, group_id, local_tiles, capacity):
    groups = counts.shape[0]
    start = before(counts)
    flat_counts, flat_owners, flat_ranks = counts.reshape(-1), owners.reshape(-1), ranks.reshape(-1)
    ahead = (flat_owners[:, None] == flat_owners[None, :]) & (flat_ranks[None, :] < flat_ranks[:, None])
    offset = jnp.sum(jnp.where(ahead, flat_counts[None, :], 0), axis=1, dtype=jnp.int32).reshape(groups, groups)
    sources = jnp.arange(groups, dtype=jnp.int32)
    mine = (sources == group_id)[:, None]

    def row(table):
        return jnp.sum(jnp.where(mine, table, 0), axis=0, dtype=jnp.int32)

    owner_row, start_row, offset_row = row(owners), row(start), row(offset)
    ids = jnp.arange(local_tiles, dtype=jnp.int32)
    member = jnp.sum((start_row[None, :] <= ids[:, None]).astype(jnp.int32), axis=1, dtype=jnp.int32) - 1
    which = member[:, None] == sources[None, :]
    own = jnp.sum(jnp.where(which, owner_row[None, :], 0), axis=1, dtype=jnp.int32)
    slot = jnp.sum(jnp.where(which, (offset_row - start_row)[None, :], 0), axis=1, dtype=jnp.int32) + ids
    arriving = owners == group_id
    recv_count = jnp.sum(jnp.where(arriving, counts, 0), axis=1, dtype=jnp.int32)
    recv_offset = jnp.sum(jnp.where(arriving, offset, 0), axis=1, dtype=jnp.int32)
    positions = jnp.arange(capacity, dtype=jnp.int32)
    inside = (positions[:, None] >= recv_offset[None, :]) & (
        positions[:, None] < (recv_offset + recv_count)[None, :]
    )
    table = jnp.sum(jnp.where(inside, sources[None, :], 0), axis=1, dtype=jnp.int32)
    filled = jnp.sum(recv_count, dtype=jnp.int32).reshape(1)
    return own, slot, table, filled


def local(
    tiles,
    w_in,
    w_out,
    se_down,
    se_up,
    kernel,
    gain,
    token_grads,
    tile_counts,
    sample_owner,
    sample_rank,
):
    groups = lax.axis_size("enc")
    columns = lax.axis_size("abs")
    group_id = lax.axis_index("enc")
    column_id = lax.axis_index("abs")
    local_tiles, grid = tiles.shape[0], tiles.shape[1]
    per, cells, width = token_grads.shape
    capacity = per * columns
    side = grid // 2
    slots = per // CHUNKS
    blocks = width // LANES
    own, slot, table, filled = routing(
        tile_counts, sample_owner, sample_rank, group_id, local_tiles, capacity
    )
    pos = slot % per
    info = jnp.stack([filled[0], column_id.astype(jnp.int32), jnp.int32(per)])
    sends = pool_and_pack(tiles, own, pos, groups, slots)

    taps = jnp.pad(kernel.astype(F32).reshape(9, blocks, LANES).transpose(1, 0, 2), ((0, 0), (0, 7), (0, 0)))
    gains = jnp.broadcast_to(gain.astype(F32).reshape(blocks, 1, LANES), (blocks, 8, LANES))
    weights = [w_in, w_out, w_in.T, w_out.T, se_down, se_up, se_down.T, se_up.T, taps, gains]

    received = []
    for h in range(CHUNKS):
        send = sends[h]
        if h > 0:
            send, received[-1] = lax.optimization_barrier((send, received[-1]))
        received.append(lax.all_to_all(send, "enc", split_axis=0, concat_axis=0, tiled=True))
        if h == 0:
            received[0], *weights = lax.optimization_barrier((received[0], *weights))

    carried = []
    arrived, small = [], []
    for h in range(CHUNKS):
        if h > 0:
            received[h], carried = lax.optimization_barrier((received[h], carried))
        parts = route([received[h]], table, info, h, per, columns, groups, False, h > 0)
        parts = exchange(parts)
        made = run_block(h, side, info, parts, token_grads, weights, carried, False)
        carried = list(made[:4])
        small.append(made[-3:])
        back = route(exchange(made[4:-3]), table, info, h, per, columns, groups, True)
        arrived.append(lax.all_to_all(back, "enc", split_axis=0, concat_axis=0, tiled=True))
    visual, normed, scaled, hidden = carried
    tile_grads = unpack_and_spread(arrived, own, pos, local_tiles, grid)

    home, away = weight_terms(info, normed, scaled, hidden, token_grads, small, columns)
    near = lax.ppermute(away, "abs", partner_pairs(1, columns))
    pair = [(home[k].astype(F32) + near[k].astype(F32)).astype(BF16) for k in range(columns // 2)]
    rows = [pair[0]] + [
        lax.ppermute(pair[k], "abs", partner_pairs(2 * k, columns)) for k in range(1, columns // 2)
    ]
    column = sum(r.astype(F32) for r in rows).astype(BF16)
    spread = lax.all_to_all(column, "enc", split_axis=0, concat_axis=0, tiled=True)
    scale = 1.0 / math.sqrt(groups * local_tiles * cells)
    total = jnp.sum(spread.astype(F32), axis=0) * scale
    narrow = se_down.shape[1]
    ends = [width, 2 * width, 2 * width + narrow, 2 * width + 2 * narrow]
    last = total[:, ends[3] : ends[3] + 10]
    return (
        visual,
        tile_grads,
        total[:, : ends[0]],
        total[:, ends[0] : ends[1]],
        total[:, ends[1] : ends[2]],
        total[:, ends[2] : ends[3]].reshape(2, width),
        last[:, :9].T,
        last[:, 9],
    )


def solution(mesh):
    return jax.shard_map(
        local,
        mesh=mesh,
        in_specs=(
            P("enc", None, None, "abs"),
            P(),
            P(),
            P(),
            P(),
            P(),
            P(),
            P(("enc", "abs"), None, None),
            P(),
            P(),
            P(),
        ),
        out_specs=(
            P(("enc", "abs"), None, None),
            P("enc", None, None, "abs"),
            P(("enc", "abs"), None),
            P(("enc", "abs"), None),
            P(("enc", "abs"), None),
            P(("enc", "abs"), None),
            P(None, ("enc", "abs")),
            P(("enc", "abs")),
        ),
        check_vma=False,
    )
```

```python
import functools
import math

import jax
import jax.numpy as jnp
from jax import lax
from jax.experimental import pallas as pl
from jax.experimental.pallas import tpu as pltpu
from jax.sharding import PartitionSpec as P

F32 = jnp.float32
BF16 = jnp.bfloat16
NORM_EPS = 1e-06
LANES = 128
PAD = 16
CHUNKS = 2
VMEM_BYTES = 60 * 1024 * 1024
ANY = pl.BlockSpec(memory_space=pl.ANY)
SMEM = pl.BlockSpec(memory_space=pltpu.SMEM)
VMEM = pl.BlockSpec(memory_space=pltpu.VMEM)


def params(**more):
    return pltpu.CompilerParams(vmem_limit_bytes=VMEM_BYTES, **more)


def pool_kernel(steps, per, own_ref, pos_ref, tiles_ref, *rest):
    outs, (wide, pooled, sem) = rest[:CHUNKS], rest[CHUNKS:]
    step = pl.program_id(0)
    side = tiles_ref.shape[1] // 2
    width = 2 * side
    slots = outs[0].shape[1]
    for n in range(per):
        for row in range(side):
            pair = tiles_ref[n, 2 * row].astype(F32) + tiles_ref[n, 2 * row + 1].astype(F32)
            wide[pl.ds(row * width, width), :] = pair
        total = wide[pl.ds(0, side * side, stride=2), :] + wide[pl.ds(1, side * side, stride=2), :]
        j = step * per + n
        pooled[j] = (total * 0.25).astype(BF16)
        position = pos_ref[j]
        for h in range(CHUNKS):

            @pl.when(position // slots == h)
            def _(h=h):
                pltpu.make_async_copy(
                    pooled.at[j], outs[h].at[own_ref[j], position - h * slots], sem
                ).start()

    @pl.when(step == steps - 1)
    def _():
        @pl.loop(0, steps * per)
        def _(j):
            pltpu.make_async_copy(pooled.at[0], outs[0].at[0, 0], sem).wait()


def pool_and_pack(tiles, own, pos, groups, slots):
    count, grid, _, channels = tiles.shape
    cells = grid * grid // 4
    per = 4
    steps = count // per
    made = jax.ShapeDtypeStruct((groups, slots, cells, channels), BF16)
    return pl.pallas_call(
        functools.partial(pool_kernel, steps, per),
        grid=(steps,),
        in_specs=[SMEM, SMEM, pl.BlockSpec((per, grid, grid, channels), lambda i: (i, 0, 0, 0))],
        out_specs=[ANY] * CHUNKS,
        out_shape=[made] * CHUNKS,
        scratch_shapes=[
            pltpu.VMEM((grid * grid // 2, channels), F32),
            pltpu.VMEM((count, cells, channels), BF16),
            pltpu.SemaphoreType.DMA,
        ],
        compiler_params=params(),
        cost_estimate=pl.CostEstimate(flops=tiles.size, bytes_accessed=tiles.size * 3, transcendentals=0),
        name="pool_and_pack",
    )(own, pos, tiles)


def partner(me, step, columns, sign):
    ring = columns // 2
    z = lax.rem(me // 2 + sign * (step // 2) + ring, ring)
    return 2 * z + lax.rem(lax.rem(me, 2) + step % 2, 2)


def partner_pairs(step, columns):
    ring = columns // 2
    return [(n, 2 * ((n // 2 + step // 2) % ring) + (n % 2 + step) % 2) for n in range(columns)]


def exchange(parts):
    columns = len(parts)
    if columns == 1:
        return [lax.all_to_all(parts[0], "abs", split_axis=0, concat_axis=0, tiled=True)]
    return [parts[0]] + [lax.ppermute(parts[k], "abs", partner_pairs(k, columns)) for k in range(1, columns)]


def pick(refs, me, step, sign):
    if len(refs) > 1:
        return refs[step]
    return refs[0].at[partner(me, step, refs[0].shape[0], sign)]


def route_kernel(chunk, per, columns, back, table_ref, info_ref, *rest):
    (srcs, outs) = (rest[:-2], rest[-2:-1]) if back else (rest[:1], rest[1:-1])
    sem = rest[-1]
    filled, me = info_ref[0], info_ref[1]
    whole = outs[0] if back else srcs[0]
    slots = whole.shape[1]

    def each(act):
        for k in range(columns):
            first = partner(me, k, columns, -1 if back else 1) * per + chunk * slots
            part = pick(srcs, me, k, -1) if back else pick(outs, me, k, 1)

            @pl.loop(0, slots)
            def _(local, part=part, first=first):
                q = first + local

                @pl.when(q < filled)
                def _():
                    there = whole.at[table_ref[q], local]
                    here = part.at[local]
                    act(pltpu.make_async_copy(*((here, there) if back else (there, here)), sem))

    each(lambda one: one.start())
    each(lambda one: one.wait())


def parts_of(columns, shape, joined):
    if joined:
        return [jax.ShapeDtypeStruct((columns, *shape), BF16)]
    return [jax.ShapeDtypeStruct(shape, BF16)] * columns


def route(sources, table, info, chunk, per, columns, groups, back, joined=False):
    slots, cells, channels = sources[0].shape[-3:]
    parts = parts_of(columns, (slots, cells, channels), joined)
    whole = jax.ShapeDtypeStruct((groups, slots, cells, channels), BF16)
    return pl.pallas_call(
        functools.partial(route_kernel, chunk, per, columns, back),
        in_specs=[SMEM, SMEM] + [VMEM] * len(sources),
        out_specs=ANY if back else [ANY] * len(parts),
        out_shape=whole if back else parts,
        scratch_shapes=[pltpu.SemaphoreType.DMA],
        compiler_params=pltpu.CompilerParams(vmem_limit_bytes=16 * 1024 * 1024),
        cost_estimate=pl.CostEstimate(
            flops=0, bytes_accessed=8 * columns * slots * cells * channels, transcendentals=0
        ),
        name="route_back" if back else "route_in",
    )(table, info, *sources)


def exact_dot(left, weights):
    rows = left.shape[0]
    first = left.astype(BF16).astype(F32)
    rest = left - first
    second = rest.astype(BF16).astype(F32)
    third = rest - second
    stacked = jnp.concatenate([first, second, third, jnp.zeros_like(left)], axis=0).astype(BF16)
    made = jnp.dot(stacked, weights, preferred_element_type=F32)
    return made[:rows] + made[rows : 2 * rows] + made[2 * rows : 3 * rows]


def block_kernel(
    chunk,
    side,
    columns,
    parts_in,
    parts_out,
    info_ref,
    *rest,
):
    x_hbm, rest = rest[:parts_in], rest[parts_in:]
    up_hbm, w_in_hbm, w_out_hbm, w_in_t_hbm, w_out_t_hbm = rest[:5]
    se_down, se_up, se_down_t, se_up_t, taps, gain = rest[5:11]
    outs = rest[-24 - parts_out : -17]
    (vis_hbm, normed_hbm, scaled_hbm, hidden_hbm), back_hbm = outs[:4], outs[4 : 4 + parts_out]
    small_a, small_b, small_k = outs[4 + parts_out :]
    filled, me = info_ref[0], info_ref[1]
    live = filled - me * info_ref[2]
    (
        x,
        up,
        w_in,
        w_out,
        w_in_t,
        w_out_t,
        standard,
        inverse,
        slope_h,
        act,
        mixed,
        slope_s,
        wide,
        tmp,
        masks,
        stage,
        sem,
    ) = rest[-17:]
    (rows_v, squeeze, excite, extra, kacc, gacc, normed, scaled, vis) = stage
    blocks, tiles, cells, lanes = x.shape
    width = blocks * lanes
    flat = tiles * cells
    loads = [
        pltpu.make_async_copy(a, b, sem.at[n])
        for n, (a, b) in enumerate(
            [
                (w_in_hbm, w_in),
                (up_hbm.at[pl.ds(chunk * tiles, tiles)], up),
                (w_out_hbm, w_out),
                (w_out_t_hbm, w_out_t),
                (w_in_t_hbm, w_in_t),
            ]
        )
    ]
    x_loads = [
        pltpu.make_async_copy(pick(x_hbm, me, k, -1), x.at[partner(me, k, columns, -1)], sem.at[10 + k])
        for k in range(columns)
    ]
    for one in x_loads + loads:
        one.start()

    column = lax.rem(lax.broadcasted_iota(jnp.int32, (cells, lanes), 0), side)
    masks[0] = jnp.where(column != 0, 1.0, 0.0).astype(F32)
    masks[1] = jnp.where(column != side - 1, 1.0, 0.0).astype(F32)
    edge = jnp.zeros((PAD, lanes), F32)
    tmp[pl.ds(0, PAD), :] = edge
    tmp[pl.ds(PAD + cells, PAD), :] = edge
    kacc[...] = jnp.zeros_like(kacc)
    gacc[...] = jnp.zeros_like(gacc)
    squeeze[...] = jnp.zeros_like(squeeze)
    extra[...] = jnp.zeros_like(extra)

    @pl.loop(0, blocks * tiles)
    def _(n):
        c, t = n % blocks, n // blocks
        act[c, t, pl.ds(0, PAD), :] = edge
        act[c, t, pl.ds(PAD + cells, PAD), :] = edge

    for one in x_loads:
        one.wait()
    for t in range(tiles):

        @pl.when(chunk * tiles + t >= live)
        def _(t=t):
            for c in range(blocks):
                x[c, t] = jnp.zeros((cells, lanes), BF16)

    @pl.loop(0, tiles)
    def _(t):
        total = x[0, t].astype(F32)
        for c in range(1, blocks):
            total = total + x[c, t].astype(F32)
        average = jnp.sum(total, axis=1, keepdims=True) * (1.0 / width)
        square = jnp.zeros((cells, lanes), F32)
        for c in range(blocks):
            centred = x[c, t].astype(F32) - average
            square = square + centred * centred
        variance = jnp.sum(square, axis=1, keepdims=True) * (1.0 / width)
        inv = lax.rsqrt(variance + NORM_EPS)
        inverse[t] = jnp.broadcast_to(inv, (cells, lanes))
        for c in range(blocks):
            std = (x[c, t].astype(F32) - average) * inv
            standard[c, t] = std
            normed[t, :, c * lanes : (c + 1) * lanes] = (std * gain[c, 0:1, :]).astype(BF16)

    def product(left, right, put):
        wide_n = 256
        value = left[...].reshape(flat, width)
        for n in range(width // wide_n):
            made = jnp.dot(value, right[:, n * wide_n : (n + 1) * wide_n], preferred_element_type=F32)
            for half in range(wide_n // lanes):
                c = n * (wide_n // lanes) + half
                put(c, made[:, half * lanes : (half + 1) * lanes].reshape(tiles, cells, lanes))

    def put_hidden(c, value):
        slope_h[c] = value

    loads[0].wait()
    product(normed, w_in, put_hidden)
    save_normed = pltpu.make_async_copy(normed, normed_hbm.at[pl.ds(chunk * tiles, tiles)], sem.at[6])
    save_normed.start()

    @pl.loop(0, blocks * tiles)
    def _(n):
        c, t = n % blocks, n // blocks
        h = slope_h[c, t]
        sig = jax.nn.sigmoid(h)
        a = h * sig
        slope_h[c, t] = sig * (1.0 + h * (1.0 - sig))
        act[c, t, pl.ds(PAD, cells), :] = a

        def column_sum(b):
            made = None
            for r in range(3):
                term = taps[c, 3 * r + b : 3 * r + b + 1, :] * act[c, t, pl.ds(PAD + side * (r - 1) + b - 1, cells), :]
                made = term if made is None else made + term
            return made

        spatial = column_sum(1) + masks[0] * column_sum(0) + masks[1] * column_sum(2)
        sig = jax.nn.sigmoid(spatial)
        mix = spatial * sig
        mixed[c, t] = mix
        slope_s[c, t] = sig * (1.0 + spatial * (1.0 - sig))
        squeeze[c, pl.ds(t, 1), :] = jnp.sum(mix, axis=0, keepdims=True) * (1.0 / cells)

    def joined(ref):
        return jnp.concatenate([ref[c] for c in range(blocks)], axis=1)

    squeezed = joined(squeeze)
    squeeze_pre = exact_dot(squeezed, se_down[...])
    sig_pre = jax.nn.sigmoid(squeeze_pre)
    squeeze_act = squeeze_pre * sig_pre
    excited = jax.nn.sigmoid(exact_dot(squeeze_act, se_up[...]))
    for c in range(blocks):
        excite[c] = excited[:, c * lanes : (c + 1) * lanes]

    def put_back(c, value):
        wide[c] = value

    loads[1].wait()
    for t in range(tiles):

        @pl.when(chunk * tiles + t >= live)
        def _(t=t):
            up[t] = jnp.zeros(up.shape[1:], BF16)

    loads[3].wait()
    product(up, w_out_t, put_back)

    @pl.loop(0, tiles)
    def _(t):
        for c in range(blocks):
            mix = mixed[c, t]
            scaled[t, :, c * lanes : (c + 1) * lanes] = (mix * excite[c, pl.ds(t, 1), :]).astype(BF16)
            extra[c, pl.ds(t, 1), :] = jnp.sum(wide[c, t] * mix, axis=0, keepdims=True)

    back_pre = joined(extra) * excited * (1.0 - excited)
    back_squeeze_pre = exact_dot(back_pre, se_up_t[...]) * (
        sig_pre * (1.0 + squeeze_pre * (1.0 - sig_pre))
    )
    back_squeeze = exact_dot(back_squeeze_pre, se_down_t[...]) * (1.0 / cells)
    for c in range(blocks):
        extra[c] = back_squeeze[:, c * lanes : (c + 1) * lanes]
    small_a[0] = squeezed
    small_a[1] = back_pre
    small_b[0] = back_squeeze_pre
    small_b[1] = squeeze_act

    def put_visual(c, value):
        vis[:, :, c * lanes : (c + 1) * lanes] = (x[c].astype(F32) + value).astype(BF16)

    loads[2].wait()
    product(scaled, w_out, put_visual)
    save_scaled = pltpu.make_async_copy(scaled, scaled_hbm.at[pl.ds(chunk * tiles, tiles)], sem.at[7])
    save_scaled.start()
    save_vis = pltpu.make_async_copy(vis, vis_hbm.at[pl.ds(chunk * tiles, tiles)], sem.at[8])
    save_vis.start()
    save_normed.wait()

    @pl.loop(0, tiles)
    def _(t):
        for c in range(blocks):
            back = (wide[c, t] * excite[c, pl.ds(t, 1), :] + extra[c, pl.ds(t, 1), :]) * slope_s[c, t]
            tmp[pl.ds(PAD, cells), :] = back
            sides = (back * masks[0], back, back * masks[1])
            for r in range(3):
                for b in range(3):
                    term = sides[b] * act[c, t, pl.ds(PAD + side * (r - 1) + b - 1, cells), :]
                    kacc[c, 3 * r + b] += jnp.sum(term.reshape(cells // 8, 8, lanes), axis=0)

            def column_sum(b, c=c):
                made = None
                for r in range(3):
                    term = taps[c, 3 * r + b : 3 * r + b + 1, :] * tmp[pl.ds(PAD - side * (r - 1) - (b - 1), cells), :]
                    made = term if made is None else made + term
                return made

            back_act = column_sum(1) + masks[1] * column_sum(0) + masks[0] * column_sum(2)
            normed[t, :, c * lanes : (c + 1) * lanes] = (back_act * slope_h[c, t]).astype(BF16)

    loads[4].wait()
    product(normed, w_in_t, put_back)
    save_hidden = pltpu.make_async_copy(normed, hidden_hbm.at[pl.ds(chunk * tiles, tiles)], sem.at[9])
    save_hidden.start()

    @pl.loop(0, tiles)
    def _(t):
        centre = jnp.zeros((cells, lanes), F32)
        along = jnp.zeros((cells, lanes), F32)
        for c in range(blocks):
            along_n = wide[c, t] * standard[c, t]
            gacc[c] += jnp.sum(along_n.reshape(cells // 8, 8, lanes), axis=0)
            centre = centre + wide[c, t] * gain[c, 0:1, :]
            along = along + along_n * gain[c, 0:1, :]
        centre = jnp.sum(centre, axis=1, keepdims=True) * (1.0 / width)
        along = jnp.sum(along, axis=1, keepdims=True) * (1.0 / width)
        inv = inverse[t]
        for c in range(blocks):
            made = up[t, :, c * lanes : (c + 1) * lanes].astype(F32) + inv * (
                wide[c, t] * gain[c, 0:1, :] - centre - standard[c, t] * along
            )
            rows_v[c, t] = made.astype(BF16)

    save_back = [
        pltpu.make_async_copy(rows_v.at[partner(me, k, columns, 1)], pick(back_hbm, me, k, 1), sem.at[10 + columns + k])
        for k in range(columns)
    ]
    for one in save_back:
        one.start()
    small_k[...] = jnp.zeros_like(small_k)
    for c in range(blocks):
        for r in range(9):
            small_k[r : r + 1, c * lanes : (c + 1) * lanes] = jnp.sum(kacc[c, r], axis=0, keepdims=True)
        small_k[9:10, c * lanes : (c + 1) * lanes] = jnp.sum(gacc[c], axis=0, keepdims=True)
    save_scaled.wait()
    save_vis.wait()
    save_hidden.wait()
    for one in save_back:
        one.wait()


def run_block(chunk, side, info, x, up, weights, carried, joined):
    tiles, cells, lanes = x[0].shape[-3:]
    blocks = columns = up.shape[-1] // lanes
    backs = parts_of(columns, (tiles, cells, lanes), joined)
    size = blocks * tiles * cells * lanes
    width = blocks * lanes
    narrow = weights[4].shape[1]
    whole = jax.ShapeDtypeStruct(up.shape, BF16)
    fixed = [info, *x, up, *weights]
    field = pltpu.VMEM((blocks, tiles, cells, lanes), F32)
    packed = pltpu.VMEM((tiles, cells, width), BF16)
    eight = pltpu.VMEM((blocks, 8, lanes), F32)
    square = pltpu.VMEM((width, width), BF16)
    flops = 8 * tiles * cells * width * width
    return pl.pallas_call(
        functools.partial(block_kernel, chunk, side, columns, len(x), len(backs)),
        in_specs=[SMEM] + [ANY] * (len(x) + 5) + [VMEM] * 6 + [ANY] * len(carried),
        out_specs=[ANY] * (4 + len(backs)) + [VMEM] * 3,
        out_shape=[whole] * 4
        + backs
        + [
            jax.ShapeDtypeStruct((2, 8, width), F32),
            jax.ShapeDtypeStruct((2, 8, narrow), F32),
            jax.ShapeDtypeStruct((16, width), F32),
        ],
        input_output_aliases={len(fixed) + n: n for n in range(len(carried))},
        scratch_shapes=[
            pltpu.VMEM((blocks, tiles, cells, lanes), BF16),
            packed,
            square,
            square,
            square,
            square,
            field,
            pltpu.VMEM((tiles, cells, lanes), F32),
            field,
            pltpu.VMEM((blocks, tiles, cells + 2 * PAD, lanes), F32),
            field,
            field,
            field,
            pltpu.VMEM((cells + 2 * PAD, lanes), F32),
            pltpu.VMEM((2, cells, lanes), F32),
            [
                pltpu.VMEM((blocks, tiles, cells, lanes), BF16),
                eight,
                eight,
                eight,
                pltpu.VMEM((blocks, 9, 8, lanes), F32),
                eight,
                packed,
                packed,
                packed,
            ],
            pltpu.SemaphoreType.DMA((10 + 2 * columns,)),
        ],
        compiler_params=params(),
        cost_estimate=pl.CostEstimate(
            flops=flops, bytes_accessed=16 * size + 8 * width * width, transcendentals=2 * size
        ),
        name="block_%d" % chunk,
    )(*fixed, *carried)


def weights_kernel(chunks, columns, info_ref, normed, scaled, hidden, up, *rest):
    smalls, (home, away, held) = rest[: 5 * chunks], rest[5 * chunks :]
    count, cells, wide = normed.shape
    flat = count * cells
    width = hidden.shape[2]
    me = info_ref[1]
    ring = columns // 2
    made = []
    for left, right in ((normed, hidden), (scaled, up)):
        made.append(
            lax.dot_general(
                left[...].reshape(flat, wide),
                right[...].reshape(flat, width),
                (((0,), (0,)), ((), ())),
                preferred_element_type=F32,
            )
        )

    def outer(left, right):
        return lax.dot_general(
            jnp.concatenate(left, axis=0),
            jnp.concatenate(right, axis=0),
            (((0,), (0,)), ((), ())),
            preferred_element_type=F32,
            precision=lax.Precision.HIGHEST,
        )

    quarter = lax.rem(lax.broadcasted_iota(jnp.int32, (8, wide), 1), 4)
    pair = [lax.broadcasted_iota(jnp.int32, (16, LANES), n) for n in range(2)]
    same = jnp.where(pair[0] == pair[1], 1.0, 0.0).astype(F32)
    each = [smalls[5 * h : 5 * h + 5] for h in range(chunks)]
    narrow = each[0][2].shape[2]
    down = outer([e[0][0] for e in each], [e[2][0] for e in each])
    lift = outer(
        [jnp.where(quarter == m, e[3][...], 0.0) for e in each for m in range(4)],
        [e[1][0, :, m * narrow : (m + 1) * narrow] for e in each for m in range(4)],
    )
    taps = outer([sum(e[4][...] for e in each)], [same])
    place = 0
    for value in (*made, down, lift, taps):
        held[:, place : place + value.shape[1]] = value
        place += value.shape[1]
    for group in range(wide // (8 * columns)):
        for k in range(columns):
            row = pl.multiple_of(8 * (columns * group + partner(me, k, columns, 1)), 8)
            target = home if k % 2 == 0 else away
            target[k // 2, group] = held[pl.ds(row, 8), :].astype(BF16)


def weight_terms(info, normed, scaled, hidden, up, small, columns):
    count, cells, width = normed.shape
    narrow = small[0][1].shape[2]
    wide = 2 * LANES
    lanes = 2 * width + 2 * narrow + LANES
    groups = width // (8 * columns)
    per = wide // (8 * columns)
    left = pl.BlockSpec((count, cells, wide), lambda i: (0, 0, i))
    right = pl.BlockSpec((count, cells, width), lambda i: (0, 0, 0), pipeline_mode=pl.Buffered(1))
    args, specs = [], []
    for a, b, k in small:
        args += [a, a, b, jnp.repeat(b[1], 4, axis=1), k]
        specs += [
            pl.BlockSpec((1, 8, wide), lambda i: (0, 0, i)),
            pl.BlockSpec((1, 8, width), lambda i: (1, 0, 0)),
            pl.BlockSpec((1, 8, narrow), lambda i: (0, 0, 0)),
            pl.BlockSpec((8, wide), lambda i: (0, i)),
            pl.BlockSpec((16, wide), lambda i: (0, i)),
        ]
    part = jax.ShapeDtypeStruct((columns // 2, groups, 8, lanes), BF16)
    return pl.pallas_call(
        functools.partial(weights_kernel, len(small), columns),
        grid=(width // wide,),
        in_specs=[SMEM, left, left, right, right] + specs,
        out_specs=[pl.BlockSpec((columns // 2, per, 8, lanes), lambda i: (0, i, 0, 0))] * 2,
        out_shape=[part] * 2,
        scratch_shapes=[pltpu.VMEM((wide, lanes), F32)],
        compiler_params=params(),
        cost_estimate=pl.CostEstimate(
            flops=4 * count * cells * width * width, bytes_accessed=8 * count * cells * width, transcendentals=0
        ),
        name="weight_terms",
    )(info, normed, scaled, hidden, up, *args)


def spread_kernel(per, own_ref, pos_ref, *rest):
    arrived, (out, wide) = rest[:CHUNKS], rest[CHUNKS:]
    step = pl.program_id(0)
    slots = arrived[0].shape[1]
    side = out.shape[1] // 2
    width = 2 * side
    for n in range(per):
        group, position = own_ref[step * per + n], pos_ref[step * per + n]
        for h in range(CHUNKS):

            @pl.when(position // slots == h)
            def _(h=h):
                quarter = arrived[h][group, position - h * slots].astype(F32) * 0.25
                wide[n, pl.ds(0, side * side, stride=2), :] = quarter
                wide[n, pl.ds(1, side * side, stride=2), :] = quarter

        for row in range(side):
            line = wide[n, pl.ds(row * width, width), :].astype(BF16)
            out[n, 2 * row] = line
            out[n, 2 * row + 1] = line


def unpack_and_spread(arrived, own, pos, count, grid):
    _, _, cells, channels = arrived[0].shape
    per = 4
    return pl.pallas_call(
        functools.partial(spread_kernel, per),
        grid=(count // per,),
        in_specs=[SMEM, SMEM]
        + [pl.BlockSpec(a.shape, lambda i: (0, 0, 0, 0), pipeline_mode=pl.Buffered(1)) for a in arrived],
        out_specs=pl.BlockSpec((per, grid, grid, channels), lambda i: (i, 0, 0, 0)),
        out_shape=jax.ShapeDtypeStruct((count, grid, grid, channels), BF16),
        scratch_shapes=[pltpu.VMEM((per, grid * grid // 2, channels), F32)],
        compiler_params=pltpu.CompilerParams(vmem_limit_bytes=24 * 1024 * 1024),
        cost_estimate=pl.CostEstimate(
            flops=0, bytes_accessed=10 * count * cells * channels, transcendentals=0
        ),
        name="unpack_and_spread",
    )(own, pos, *arrived)


def before(table):
    groups = table.shape[1]
    index = jnp.arange(groups, dtype=jnp.int32)
    lower = index[None, :] < index[:, None]
    return jnp.sum(jnp.where(lower[None], table[:, None, :], 0), axis=2, dtype=jnp.int32)


def routing(counts, owners, ranks, group_id, local_tiles, capacity):
    groups = counts.shape[0]
    start = before(counts)
    flat_counts, flat_owners, flat_ranks = counts.reshape(-1), owners.reshape(-1), ranks.reshape(-1)
    ahead = (flat_owners[:, None] == flat_owners[None, :]) & (flat_ranks[None, :] < flat_ranks[:, None])
    offset = jnp.sum(jnp.where(ahead, flat_counts[None, :], 0), axis=1, dtype=jnp.int32).reshape(groups, groups)
    sources = jnp.arange(groups, dtype=jnp.int32)
    mine = (sources == group_id)[:, None]

    def row(table):
        return jnp.sum(jnp.where(mine, table, 0), axis=0, dtype=jnp.int32)

    owner_row, start_row, offset_row = row(owners), row(start), row(offset)
    ids = jnp.arange(local_tiles, dtype=jnp.int32)
    member = jnp.sum((start_row[None, :] <= ids[:, None]).astype(jnp.int32), axis=1, dtype=jnp.int32) - 1
    which = member[:, None] == sources[None, :]
    own = jnp.sum(jnp.where(which, owner_row[None, :], 0), axis=1, dtype=jnp.int32)
    slot = jnp.sum(jnp.where(which, (offset_row - start_row)[None, :], 0), axis=1, dtype=jnp.int32) + ids
    arriving = owners == group_id
    recv_count = jnp.sum(jnp.where(arriving, counts, 0), axis=1, dtype=jnp.int32)
    recv_offset = jnp.sum(jnp.where(arriving, offset, 0), axis=1, dtype=jnp.int32)
    positions = jnp.arange(capacity, dtype=jnp.int32)
    inside = (positions[:, None] >= recv_offset[None, :]) & (
        positions[:, None] < (recv_offset + recv_count)[None, :]
    )
    table = jnp.sum(jnp.where(inside, sources[None, :], 0), axis=1, dtype=jnp.int32)
    filled = jnp.sum(recv_count, dtype=jnp.int32).reshape(1)
    return own, slot, table, filled


def local(
    tiles,
    w_in,
    w_out,
    se_down,
    se_up,
    kernel,
    gain,
    token_grads,
    tile_counts,
    sample_owner,
    sample_rank,
):
    groups = lax.axis_size("enc")
    columns = lax.axis_size("abs")
    group_id = lax.axis_index("enc")
    column_id = lax.axis_index("abs")
    local_tiles, grid = tiles.shape[0], tiles.shape[1]
    per, cells, width = token_grads.shape
    capacity = per * columns
    side = grid // 2
    slots = per // CHUNKS
    blocks = width // LANES
    own, slot, table, filled = routing(
        tile_counts, sample_owner, sample_rank, group_id, local_tiles, capacity
    )
    pos = slot % per
    info = jnp.stack([filled[0], column_id.astype(jnp.int32), jnp.int32(per)])
    sends = pool_and_pack(tiles, own, pos, groups, slots)

    taps = jnp.pad(kernel.astype(F32).reshape(9, blocks, LANES).transpose(1, 0, 2), ((0, 0), (0, 7), (0, 0)))
    gains = jnp.broadcast_to(gain.astype(F32).reshape(blocks, 1, LANES), (blocks, 8, LANES))
    weights = [w_in, w_out, w_in.T, w_out.T, se_down, se_up, se_down.T, se_up.T, taps, gains]

    inner = []
    for h in range(CHUNKS):
        send = sends[h]
        if h > 0:
            send, _ = lax.optimization_barrier((send, received))
        received = lax.all_to_all(send, "enc", split_axis=0, concat_axis=0, tiled=True)
        if h == 0:
            received, *weights = lax.optimization_barrier((received, *weights))
        parts = route([received], table, info, h, per, columns, groups, False, h > 0)
        if h > 0:
            inner[-1], parts = lax.optimization_barrier((inner[-1], parts))
        inner.append(exchange(parts))

    carried = []
    arrived, small, narrowed, backs = [], [], [], []
    for h in range(CHUNKS):
        made = run_block(h, side, info, inner[h], token_grads, weights, carried, h == 0)
        carried = list(made[:4])
        small.append(made[-3:])
        narrowed.append(exchange(made[4:-3]))
    narrowed[0], carried = lax.optimization_barrier((narrowed[0], carried))
    for h in range(CHUNKS):
        back = route(narrowed[h], table, info, h, per, columns, groups, True)
        if h == 0:
            back, carried = lax.optimization_barrier((back, carried))
        arrived.append(lax.all_to_all(back, "enc", split_axis=0, concat_axis=0, tiled=True))
    visual, normed, scaled, hidden = carried
    tile_grads = unpack_and_spread(arrived, own, pos, local_tiles, grid)

    home, away = weight_terms(info, normed, scaled, hidden, token_grads, small, columns)
    near = lax.ppermute(away, "abs", partner_pairs(1, columns))
    pair = [(home[k].astype(F32) + near[k].astype(F32)).astype(BF16) for k in range(columns // 2)]
    rows = [pair[0]] + [
        lax.ppermute(pair[k], "abs", partner_pairs(2 * k, columns)) for k in range(1, columns // 2)
    ]
    column = sum(r.astype(F32) for r in rows).astype(BF16)
    spread = lax.all_to_all(column, "enc", split_axis=0, concat_axis=0, tiled=True)
    scale = 1.0 / math.sqrt(groups * local_tiles * cells)
    total = jnp.sum(spread.astype(F32), axis=0) * scale
    narrow = se_down.shape[1]
    ends = [width, 2 * width, 2 * width + narrow, 2 * width + 2 * narrow]
    last = total[:, ends[3] : ends[3] + 10]
    return (
        visual,
        tile_grads,
        total[:, : ends[0]],
        total[:, ends[0] : ends[1]],
        total[:, ends[1] : ends[2]],
        total[:, ends[2] : ends[3]].reshape(2, width),
        last[:, :9].T,
        last[:, 9],
    )


def solution(mesh):
    return jax.shard_map(
        local,
        mesh=mesh,
        in_specs=(
            P("enc", None, None, "abs"),
            P(),
            P(),
            P(),
            P(),
            P(),
            P(),
            P(("enc", "abs"), None, None),
            P(),
            P(),
            P(),
        ),
        out_specs=(
            P(("enc", "abs"), None, None),
            P("enc", None, None, "abs"),
            P(("enc", "abs"), None),
            P(("enc", "abs"), None),
            P(("enc", "abs"), None),
            P(("enc", "abs"), None),
            P(None, ("enc", "abs")),
            P(("enc", "abs")),
        ),
        check_vma=False,
    )
```

```python
import functools
import math

import jax
import jax.numpy as jnp
from jax import lax
from jax.experimental import pallas as pl
from jax.experimental.pallas import tpu as pltpu
from jax.sharding import PartitionSpec as P

F32 = jnp.float32
BF16 = jnp.bfloat16
NORM_EPS = 1e-06
LANES = 128
PAD = 16
CHUNKS = 2
VMEM_BYTES = 60 * 1024 * 1024
ANY = pl.BlockSpec(memory_space=pl.ANY)
SMEM = pl.BlockSpec(memory_space=pltpu.SMEM)
VMEM = pl.BlockSpec(memory_space=pltpu.VMEM)


def params(**more):
    return pltpu.CompilerParams(vmem_limit_bytes=VMEM_BYTES, **more)


def pool_kernel(steps, per, own_ref, pos_ref, tiles_ref, *rest):
    outs, (wide, pooled, sem) = rest[:CHUNKS], rest[CHUNKS:]
    step = pl.program_id(0)
    side = tiles_ref.shape[1] // 2
    width = 2 * side
    slots = outs[0].shape[1]
    for n in range(per):
        for row in range(side):
            pair = tiles_ref[n, 2 * row].astype(F32) + tiles_ref[n, 2 * row + 1].astype(F32)
            wide[pl.ds(row * width, width), :] = pair
        total = wide[pl.ds(0, side * side, stride=2), :] + wide[pl.ds(1, side * side, stride=2), :]
        j = step * per + n
        pooled[j] = (total * 0.25).astype(BF16)
        position = pos_ref[j]
        for h in range(CHUNKS):

            @pl.when(position // slots == h)
            def _(h=h):
                pltpu.make_async_copy(
                    pooled.at[j], outs[h].at[own_ref[j], position - h * slots], sem
                ).start()

    @pl.when(step == steps - 1)
    def _():
        @pl.loop(0, steps * per)
        def _(j):
            pltpu.make_async_copy(pooled.at[0], outs[0].at[0, 0], sem).wait()


def pool_and_pack(tiles, own, pos, groups, slots):
    count, grid, _, channels = tiles.shape
    cells = grid * grid // 4
    per = 8
    steps = count // per
    made = jax.ShapeDtypeStruct((groups, slots, cells, channels), BF16)
    return pl.pallas_call(
        functools.partial(pool_kernel, steps, per),
        grid=(steps,),
        in_specs=[SMEM, SMEM, pl.BlockSpec((per, grid, grid, channels), lambda i: (i, 0, 0, 0))],
        out_specs=[ANY] * CHUNKS,
        out_shape=[made] * CHUNKS,
        scratch_shapes=[
            pltpu.VMEM((grid * grid // 2, channels), F32),
            pltpu.VMEM((count, cells, channels), BF16),
            pltpu.SemaphoreType.DMA,
        ],
        compiler_params=params(),
        cost_estimate=pl.CostEstimate(flops=tiles.size, bytes_accessed=tiles.size * 3, transcendentals=0),
        name="pool_and_pack",
    )(own, pos, tiles)


def partner(me, step, columns, sign):
    ring = columns // 2
    z = lax.rem(me // 2 + sign * (step // 2) + ring, ring)
    return 2 * z + lax.rem(lax.rem(me, 2) + step % 2, 2)


def partner_pairs(step, columns):
    ring = columns // 2
    return [(n, 2 * ((n // 2 + step // 2) % ring) + (n % 2 + step) % 2) for n in range(columns)]


def exchange(parts):
    columns = len(parts)
    if columns == 1:
        return [lax.all_to_all(parts[0], "abs", split_axis=0, concat_axis=0, tiled=True)]
    return [parts[0]] + [lax.ppermute(parts[k], "abs", partner_pairs(k, columns)) for k in range(1, columns)]


def pick(refs, me, step, sign):
    if len(refs) > 1:
        return refs[step]
    return refs[0].at[partner(me, step, refs[0].shape[0], sign)]


def route_kernel(chunk, per, columns, back, table_ref, info_ref, *rest):
    (srcs, outs) = (rest[:-2], rest[-2:-1]) if back else (rest[:1], rest[1:-1])
    sem = rest[-1]
    filled, me = info_ref[0], info_ref[1]
    whole = outs[0] if back else srcs[0]
    slots = whole.shape[1]

    def each(act):
        for k in range(columns):
            first = partner(me, k, columns, -1 if back else 1) * per + chunk * slots
            part = pick(srcs, me, k, -1) if back else pick(outs, me, k, 1)

            @pl.loop(0, slots)
            def _(local, part=part, first=first):
                q = first + local

                @pl.when(q < filled)
                def _():
                    there = whole.at[table_ref[q], local]
                    here = part.at[local]
                    act(pltpu.make_async_copy(*((here, there) if back else (there, here)), sem))

    each(lambda one: one.start())
    each(lambda one: one.wait())


def parts_of(columns, shape, joined):
    if joined:
        return [jax.ShapeDtypeStruct((columns, *shape), BF16)]
    return [jax.ShapeDtypeStruct(shape, BF16)] * columns


def route(sources, table, info, chunk, per, columns, groups, back, joined=False):
    slots, cells, channels = sources[0].shape[-3:]
    parts = parts_of(columns, (slots, cells, channels), joined)
    whole = jax.ShapeDtypeStruct((groups, slots, cells, channels), BF16)
    return pl.pallas_call(
        functools.partial(route_kernel, chunk, per, columns, back),
        in_specs=[SMEM, SMEM] + [VMEM] * len(sources),
        out_specs=ANY if back else [ANY] * len(parts),
        out_shape=whole if back else parts,
        scratch_shapes=[pltpu.SemaphoreType.DMA],
        compiler_params=pltpu.CompilerParams(vmem_limit_bytes=16 * 1024 * 1024),
        cost_estimate=pl.CostEstimate(
            flops=0, bytes_accessed=8 * columns * slots * cells * channels, transcendentals=0
        ),
        name="route_back" if back else "route_in",
    )(table, info, *sources)


def exact_dot(left, weights):
    rows = left.shape[0]
    first = left.astype(BF16).astype(F32)
    rest = left - first
    second = rest.astype(BF16).astype(F32)
    third = rest - second
    stacked = jnp.concatenate([first, second, third, jnp.zeros_like(left)], axis=0).astype(BF16)
    made = jnp.dot(stacked, weights, preferred_element_type=F32)
    return made[:rows] + made[rows : 2 * rows] + made[2 * rows : 3 * rows]


def block_kernel(
    chunk,
    side,
    columns,
    parts_in,
    parts_out,
    info_ref,
    *rest,
):
    x_hbm, rest = rest[:parts_in], rest[parts_in:]
    up_hbm, w_in_hbm, w_out_hbm, w_in_t_hbm, w_out_t_hbm = rest[:5]
    se_down, se_up, se_down_t, se_up_t, taps, gain = rest[5:11]
    outs = rest[-24 - parts_out : -17]
    (vis_hbm, normed_hbm, scaled_hbm, hidden_hbm), back_hbm = outs[:4], outs[4 : 4 + parts_out]
    small_a, small_b, small_k = outs[4 + parts_out :]
    filled, me = info_ref[0], info_ref[1]
    live = filled - me * info_ref[2]
    (
        x,
        up,
        w_in,
        w_out,
        w_in_t,
        w_out_t,
        standard,
        inverse,
        slope_h,
        act,
        mixed,
        slope_s,
        wide,
        tmp,
        masks,
        stage,
        sem,
    ) = rest[-17:]
    (rows_v, squeeze, excite, extra, kacc, gacc, normed, scaled, vis) = stage
    blocks, tiles, cells, lanes = x.shape
    width = blocks * lanes
    flat = tiles * cells
    loads = [
        pltpu.make_async_copy(a, b, sem.at[n])
        for n, (a, b) in enumerate(
            [
                (w_in_hbm, w_in),
                (up_hbm.at[pl.ds(chunk * tiles, tiles)], up),
                (w_out_hbm, w_out),
                (w_out_t_hbm, w_out_t),
                (w_in_t_hbm, w_in_t),
            ]
        )
    ]
    x_loads = [
        pltpu.make_async_copy(pick(x_hbm, me, k, -1), x.at[partner(me, k, columns, -1)], sem.at[10 + k])
        for k in range(columns)
    ]
    for one in x_loads + loads:
        one.start()

    column = lax.rem(lax.broadcasted_iota(jnp.int32, (cells, lanes), 0), side)
    masks[0] = jnp.where(column != 0, 1.0, 0.0).astype(F32)
    masks[1] = jnp.where(column != side - 1, 1.0, 0.0).astype(F32)
    edge = jnp.zeros((PAD, lanes), F32)
    tmp[pl.ds(0, PAD), :] = edge
    tmp[pl.ds(PAD + cells, PAD), :] = edge
    kacc[...] = jnp.zeros_like(kacc)
    gacc[...] = jnp.zeros_like(gacc)
    squeeze[...] = jnp.zeros_like(squeeze)
    extra[...] = jnp.zeros_like(extra)

    @pl.loop(0, blocks * tiles)
    def _(n):
        c, t = n % blocks, n // blocks
        act[c, t, pl.ds(0, PAD), :] = edge
        act[c, t, pl.ds(PAD + cells, PAD), :] = edge

    for one in x_loads:
        one.wait()
    for t in range(tiles):

        @pl.when(chunk * tiles + t >= live)
        def _(t=t):
            for c in range(blocks):
                x[c, t] = jnp.zeros((cells, lanes), BF16)

    @pl.loop(0, tiles)
    def _(t):
        total = x[0, t].astype(F32)
        for c in range(1, blocks):
            total = total + x[c, t].astype(F32)
        average = jnp.sum(total, axis=1, keepdims=True) * (1.0 / width)
        square = jnp.zeros((cells, lanes), F32)
        for c in range(blocks):
            centred = x[c, t].astype(F32) - average
            square = square + centred * centred
        variance = jnp.sum(square, axis=1, keepdims=True) * (1.0 / width)
        inv = lax.rsqrt(variance + NORM_EPS)
        inverse[t] = jnp.broadcast_to(inv, (cells, lanes))
        for c in range(blocks):
            std = (x[c, t].astype(F32) - average) * inv
            standard[c, t] = std
            normed[t, :, c * lanes : (c + 1) * lanes] = (std * gain[c, 0:1, :]).astype(BF16)

    def product(left, right, put):
        wide_n = 256
        value = left[...].reshape(flat, width)
        for n in range(width // wide_n):
            made = jnp.dot(value, right[:, n * wide_n : (n + 1) * wide_n], preferred_element_type=F32)
            for half in range(wide_n // lanes):
                c = n * (wide_n // lanes) + half
                put(c, made[:, half * lanes : (half + 1) * lanes].reshape(tiles, cells, lanes))

    def put_hidden(c, value):
        slope_h[c] = value

    loads[0].wait()
    product(normed, w_in, put_hidden)
    save_normed = pltpu.make_async_copy(normed, normed_hbm.at[pl.ds(chunk * tiles, tiles)], sem.at[6])
    save_normed.start()

    @pl.loop(0, blocks * tiles)
    def _(n):
        c, t = n % blocks, n // blocks
        h = slope_h[c, t]
        sig = jax.nn.sigmoid(h)
        a = h * sig
        slope_h[c, t] = sig * (1.0 + h * (1.0 - sig))
        act[c, t, pl.ds(PAD, cells), :] = a

        def column_sum(b):
            made = None
            for r in range(3):
                term = taps[c, 3 * r + b : 3 * r + b + 1, :] * act[c, t, pl.ds(PAD + side * (r - 1) + b - 1, cells), :]
                made = term if made is None else made + term
            return made

        spatial = column_sum(1) + masks[0] * column_sum(0) + masks[1] * column_sum(2)
        sig = jax.nn.sigmoid(spatial)
        mix = spatial * sig
        mixed[c, t] = mix
        slope_s[c, t] = sig * (1.0 + spatial * (1.0 - sig))
        squeeze[c, pl.ds(t, 1), :] = jnp.sum(mix, axis=0, keepdims=True) * (1.0 / cells)

    def joined(ref):
        return jnp.concatenate([ref[c] for c in range(blocks)], axis=1)

    squeezed = joined(squeeze)
    squeeze_pre = exact_dot(squeezed, se_down[...])
    sig_pre = jax.nn.sigmoid(squeeze_pre)
    squeeze_act = squeeze_pre * sig_pre
    excited = jax.nn.sigmoid(exact_dot(squeeze_act, se_up[...]))
    for c in range(blocks):
        excite[c] = excited[:, c * lanes : (c + 1) * lanes]

    def put_back(c, value):
        wide[c] = value

    loads[1].wait()
    for t in range(tiles):

        @pl.when(chunk * tiles + t >= live)
        def _(t=t):
            up[t] = jnp.zeros(up.shape[1:], BF16)

    loads[3].wait()
    product(up, w_out_t, put_back)

    @pl.loop(0, tiles)
    def _(t):
        for c in range(blocks):
            mix = mixed[c, t]
            scaled[t, :, c * lanes : (c + 1) * lanes] = (mix * excite[c, pl.ds(t, 1), :]).astype(BF16)
            extra[c, pl.ds(t, 1), :] = jnp.sum(wide[c, t] * mix, axis=0, keepdims=True)

    back_pre = joined(extra) * excited * (1.0 - excited)
    back_squeeze_pre = exact_dot(back_pre, se_up_t[...]) * (
        sig_pre * (1.0 + squeeze_pre * (1.0 - sig_pre))
    )
    back_squeeze = exact_dot(back_squeeze_pre, se_down_t[...]) * (1.0 / cells)
    for c in range(blocks):
        extra[c] = back_squeeze[:, c * lanes : (c + 1) * lanes]
    small_a[0] = squeezed
    small_a[1] = back_pre
    small_b[0] = back_squeeze_pre
    small_b[1] = squeeze_act

    def put_visual(c, value):
        vis[:, :, c * lanes : (c + 1) * lanes] = (x[c].astype(F32) + value).astype(BF16)

    loads[2].wait()
    product(scaled, w_out, put_visual)
    save_scaled = pltpu.make_async_copy(scaled, scaled_hbm.at[pl.ds(chunk * tiles, tiles)], sem.at[7])
    save_scaled.start()
    save_vis = pltpu.make_async_copy(vis, vis_hbm.at[pl.ds(chunk * tiles, tiles)], sem.at[8])
    save_vis.start()
    save_normed.wait()

    @pl.loop(0, tiles)
    def _(t):
        for c in range(blocks):
            back = (wide[c, t] * excite[c, pl.ds(t, 1), :] + extra[c, pl.ds(t, 1), :]) * slope_s[c, t]
            tmp[pl.ds(PAD, cells), :] = back
            sides = (back * masks[0], back, back * masks[1])
            for r in range(3):
                for b in range(3):
                    term = sides[b] * act[c, t, pl.ds(PAD + side * (r - 1) + b - 1, cells), :]
                    kacc[c, 3 * r + b] += jnp.sum(term.reshape(cells // 8, 8, lanes), axis=0)

            def column_sum(b, c=c):
                made = None
                for r in range(3):
                    term = taps[c, 3 * r + b : 3 * r + b + 1, :] * tmp[pl.ds(PAD - side * (r - 1) - (b - 1), cells), :]
                    made = term if made is None else made + term
                return made

            back_act = column_sum(1) + masks[1] * column_sum(0) + masks[0] * column_sum(2)
            normed[t, :, c * lanes : (c + 1) * lanes] = (back_act * slope_h[c, t]).astype(BF16)

    loads[4].wait()
    product(normed, w_in_t, put_back)
    save_hidden = pltpu.make_async_copy(normed, hidden_hbm.at[pl.ds(chunk * tiles, tiles)], sem.at[9])
    save_hidden.start()

    @pl.loop(0, tiles)
    def _(t):
        centre = jnp.zeros((cells, lanes), F32)
        along = jnp.zeros((cells, lanes), F32)
        for c in range(blocks):
            along_n = wide[c, t] * standard[c, t]
            gacc[c] += jnp.sum(along_n.reshape(cells // 8, 8, lanes), axis=0)
            centre = centre + wide[c, t] * gain[c, 0:1, :]
            along = along + along_n * gain[c, 0:1, :]
        centre = jnp.sum(centre, axis=1, keepdims=True) * (1.0 / width)
        along = jnp.sum(along, axis=1, keepdims=True) * (1.0 / width)
        inv = inverse[t]
        for c in range(blocks):
            made = up[t, :, c * lanes : (c + 1) * lanes].astype(F32) + inv * (
                wide[c, t] * gain[c, 0:1, :] - centre - standard[c, t] * along
            )
            rows_v[c, t] = made.astype(BF16)

    save_back = [
        pltpu.make_async_copy(rows_v.at[partner(me, k, columns, 1)], pick(back_hbm, me, k, 1), sem.at[10 + columns + k])
        for k in range(columns)
    ]
    for one in save_back:
        one.start()
    small_k[...] = jnp.zeros_like(small_k)
    for c in range(blocks):
        for r in range(9):
            small_k[r : r + 1, c * lanes : (c + 1) * lanes] = jnp.sum(kacc[c, r], axis=0, keepdims=True)
        small_k[9:10, c * lanes : (c + 1) * lanes] = jnp.sum(gacc[c], axis=0, keepdims=True)
    save_scaled.wait()
    save_vis.wait()
    save_hidden.wait()
    for one in save_back:
        one.wait()


def run_block(chunk, side, info, x, up, weights, carried, joined):
    tiles, cells, lanes = x[0].shape[-3:]
    blocks = columns = up.shape[-1] // lanes
    backs = parts_of(columns, (tiles, cells, lanes), joined)
    size = blocks * tiles * cells * lanes
    width = blocks * lanes
    narrow = weights[4].shape[1]
    whole = jax.ShapeDtypeStruct(up.shape, BF16)
    fixed = [info, *x, up, *weights]
    field = pltpu.VMEM((blocks, tiles, cells, lanes), F32)
    packed = pltpu.VMEM((tiles, cells, width), BF16)
    eight = pltpu.VMEM((blocks, 8, lanes), F32)
    square = pltpu.VMEM((width, width), BF16)
    flops = 8 * tiles * cells * width * width
    return pl.pallas_call(
        functools.partial(block_kernel, chunk, side, columns, len(x), len(backs)),
        in_specs=[SMEM] + [ANY] * (len(x) + 5) + [VMEM] * 6 + [ANY] * len(carried),
        out_specs=[ANY] * (4 + len(backs)) + [VMEM] * 3,
        out_shape=[whole] * 4
        + backs
        + [
            jax.ShapeDtypeStruct((2, 8, width), F32),
            jax.ShapeDtypeStruct((2, 8, narrow), F32),
            jax.ShapeDtypeStruct((16, width), F32),
        ],
        input_output_aliases={len(fixed) + n: n for n in range(len(carried))},
        scratch_shapes=[
            pltpu.VMEM((blocks, tiles, cells, lanes), BF16),
            packed,
            square,
            square,
            square,
            square,
            field,
            pltpu.VMEM((tiles, cells, lanes), F32),
            field,
            pltpu.VMEM((blocks, tiles, cells + 2 * PAD, lanes), F32),
            field,
            field,
            field,
            pltpu.VMEM((cells + 2 * PAD, lanes), F32),
            pltpu.VMEM((2, cells, lanes), F32),
            [
                pltpu.VMEM((blocks, tiles, cells, lanes), BF16),
                eight,
                eight,
                eight,
                pltpu.VMEM((blocks, 9, 8, lanes), F32),
                eight,
                packed,
                packed,
                packed,
            ],
            pltpu.SemaphoreType.DMA((10 + 2 * columns,)),
        ],
        compiler_params=params(),
        cost_estimate=pl.CostEstimate(
            flops=flops, bytes_accessed=16 * size + 8 * width * width, transcendentals=2 * size
        ),
        name="block_%d" % chunk,
    )(*fixed, *carried)


def weights_kernel(chunks, columns, info_ref, normed, scaled, hidden, up, *rest):
    smalls, (home, away, held) = rest[: 5 * chunks], rest[5 * chunks :]
    count, cells, wide = normed.shape
    flat = count * cells
    width = hidden.shape[2]
    me = info_ref[1]
    ring = columns // 2
    made = []
    for left, right in ((normed, hidden), (scaled, up)):
        made.append(
            lax.dot_general(
                left[...].reshape(flat, wide),
                right[...].reshape(flat, width),
                (((0,), (0,)), ((), ())),
                preferred_element_type=F32,
            )
        )

    def outer(left, right):
        return lax.dot_general(
            jnp.concatenate(left, axis=0),
            jnp.concatenate(right, axis=0),
            (((0,), (0,)), ((), ())),
            preferred_element_type=F32,
            precision=lax.Precision.HIGHEST,
        )

    quarter = lax.rem(lax.broadcasted_iota(jnp.int32, (8, wide), 1), 4)
    pair = [lax.broadcasted_iota(jnp.int32, (16, LANES), n) for n in range(2)]
    same = jnp.where(pair[0] == pair[1], 1.0, 0.0).astype(F32)
    each = [smalls[5 * h : 5 * h + 5] for h in range(chunks)]
    narrow = each[0][2].shape[2]
    down = outer([e[0][0] for e in each], [e[2][0] for e in each])
    lift = outer(
        [jnp.where(quarter == m, e[3][...], 0.0) for e in each for m in range(4)],
        [e[1][0, :, m * narrow : (m + 1) * narrow] for e in each for m in range(4)],
    )
    taps = outer([sum(e[4][...] for e in each)], [same])
    place = 0
    for value in (*made, down, lift, taps):
        held[:, place : place + value.shape[1]] = value
        place += value.shape[1]
    for group in range(wide // (8 * columns)):
        for k in range(columns):
            row = pl.multiple_of(8 * (columns * group + partner(me, k, columns, 1)), 8)
            target = home if k % 2 == 0 else away
            target[k // 2, group] = held[pl.ds(row, 8), :].astype(BF16)


def weight_terms(info, normed, scaled, hidden, up, small, columns):
    count, cells, width = normed.shape
    narrow = small[0][1].shape[2]
    wide = 2 * LANES
    lanes = 2 * width + 2 * narrow + LANES
    groups = width // (8 * columns)
    per = wide // (8 * columns)
    left = pl.BlockSpec((count, cells, wide), lambda i: (0, 0, i))
    right = pl.BlockSpec((count, cells, width), lambda i: (0, 0, 0), pipeline_mode=pl.Buffered(1))
    args, specs = [], []
    for a, b, k in small:
        args += [a, a, b, jnp.repeat(b[1], 4, axis=1), k]
        specs += [
            pl.BlockSpec((1, 8, wide), lambda i: (0, 0, i)),
            pl.BlockSpec((1, 8, width), lambda i: (1, 0, 0)),
            pl.BlockSpec((1, 8, narrow), lambda i: (0, 0, 0)),
            pl.BlockSpec((8, wide), lambda i: (0, i)),
            pl.BlockSpec((16, wide), lambda i: (0, i)),
        ]
    part = jax.ShapeDtypeStruct((columns // 2, groups, 8, lanes), BF16)
    return pl.pallas_call(
        functools.partial(weights_kernel, len(small), columns),
        grid=(width // wide,),
        in_specs=[SMEM, left, left, right, right] + specs,
        out_specs=[pl.BlockSpec((columns // 2, per, 8, lanes), lambda i: (0, i, 0, 0))] * 2,
        out_shape=[part] * 2,
        scratch_shapes=[pltpu.VMEM((wide, lanes), F32)],
        compiler_params=params(),
        cost_estimate=pl.CostEstimate(
            flops=4 * count * cells * width * width, bytes_accessed=8 * count * cells * width, transcendentals=0
        ),
        name="weight_terms",
    )(info, normed, scaled, hidden, up, *args)


def spread_kernel(per, own_ref, pos_ref, *rest):
    arrived, (out, wide) = rest[:CHUNKS], rest[CHUNKS:]
    step = pl.program_id(0)
    slots = arrived[0].shape[1]
    side = out.shape[1] // 2
    width = 2 * side
    for n in range(per):
        group, position = own_ref[step * per + n], pos_ref[step * per + n]
        for h in range(CHUNKS):

            @pl.when(position // slots == h)
            def _(h=h):
                quarter = arrived[h][group, position - h * slots].astype(F32) * 0.25
                wide[n, pl.ds(0, side * side, stride=2), :] = quarter
                wide[n, pl.ds(1, side * side, stride=2), :] = quarter

        for row in range(side):
            line = wide[n, pl.ds(row * width, width), :].astype(BF16)
            out[n, 2 * row] = line
            out[n, 2 * row + 1] = line


def unpack_and_spread(arrived, own, pos, count, grid):
    _, _, cells, channels = arrived[0].shape
    per = 4
    return pl.pallas_call(
        functools.partial(spread_kernel, per),
        grid=(count // per,),
        in_specs=[SMEM, SMEM]
        + [pl.BlockSpec(a.shape, lambda i: (0, 0, 0, 0), pipeline_mode=pl.Buffered(1)) for a in arrived],
        out_specs=pl.BlockSpec((per, grid, grid, channels), lambda i: (i, 0, 0, 0)),
        out_shape=jax.ShapeDtypeStruct((count, grid, grid, channels), BF16),
        scratch_shapes=[pltpu.VMEM((per, grid * grid // 2, channels), F32)],
        compiler_params=pltpu.CompilerParams(vmem_limit_bytes=24 * 1024 * 1024),
        cost_estimate=pl.CostEstimate(
            flops=0, bytes_accessed=10 * count * cells * channels, transcendentals=0
        ),
        name="unpack_and_spread",
    )(own, pos, *arrived)


def routing(counts, owners, ranks, group_id, local_tiles, capacity):
    groups = counts.shape[0]
    flat_counts, flat_owners, flat_ranks = counts.reshape(-1), owners.reshape(-1), ranks.reshape(-1)
    sources = jnp.arange(groups, dtype=jnp.int32)
    mine = (sources == group_id)[:, None]

    def row(table):
        return jnp.sum(jnp.where(mine, table, 0), axis=0, dtype=jnp.int32)

    owner_row, rank_row, count_row = row(owners), row(ranks), row(counts)
    start_row = jnp.sum(jnp.where(sources[None, :] < sources[:, None], count_row[None, :], 0), axis=1, dtype=jnp.int32)
    ahead = (owner_row[:, None] == flat_owners[None, :]) & (flat_ranks[None, :] < rank_row[:, None])
    offset_row = jnp.sum(jnp.where(ahead, flat_counts[None, :], 0), axis=1, dtype=jnp.int32)
    ids = jnp.arange(local_tiles, dtype=jnp.int32)
    member = jnp.sum((start_row[None, :] <= ids[:, None]).astype(jnp.int32), axis=1, dtype=jnp.int32) - 1
    which = member[:, None] == sources[None, :]
    own = jnp.sum(jnp.where(which, owner_row[None, :], 0), axis=1, dtype=jnp.int32)
    slot = jnp.sum(jnp.where(which, (offset_row - start_row)[None, :], 0), axis=1, dtype=jnp.int32) + ids
    arriving = owners == group_id
    recv_count = jnp.sum(jnp.where(arriving, counts, 0), axis=1, dtype=jnp.int32)
    recv_rank = jnp.sum(jnp.where(arriving, ranks, 0), axis=1, dtype=jnp.int32)
    earlier = recv_rank[None, :] < recv_rank[:, None]
    recv_offset = jnp.sum(jnp.where(earlier, recv_count[None, :], 0), axis=1, dtype=jnp.int32)
    positions = jnp.arange(capacity, dtype=jnp.int32)
    inside = (positions[:, None] >= recv_offset[None, :]) & (
        positions[:, None] < (recv_offset + recv_count)[None, :]
    )
    table = jnp.sum(jnp.where(inside, sources[None, :], 0), axis=1, dtype=jnp.int32)
    filled = jnp.sum(recv_count, dtype=jnp.int32).reshape(1)
    return own, slot, table, filled


def local(
    tiles,
    w_in,
    w_out,
    se_down,
    se_up,
    kernel,
    gain,
    token_grads,
    tile_counts,
    sample_owner,
    sample_rank,
):
    groups = lax.axis_size("enc")
    columns = lax.axis_size("abs")
    group_id = lax.axis_index("enc")
    column_id = lax.axis_index("abs")
    local_tiles, grid = tiles.shape[0], tiles.shape[1]
    per, cells, width = token_grads.shape
    capacity = per * columns
    side = grid // 2
    slots = per // CHUNKS
    blocks = width // LANES
    own, slot, table, filled = routing(
        tile_counts, sample_owner, sample_rank, group_id, local_tiles, capacity
    )
    pos = slot % per
    info = jnp.stack([filled[0], column_id.astype(jnp.int32), jnp.int32(per)])
    sends = pool_and_pack(tiles, own, pos, groups, slots)

    taps = jnp.pad(kernel.astype(F32).reshape(9, blocks, LANES).transpose(1, 0, 2), ((0, 0), (0, 7), (0, 0)))
    gains = jnp.broadcast_to(gain.astype(F32).reshape(blocks, 1, LANES), (blocks, 8, LANES))
    weights = [w_in, w_out, w_in.T, w_out.T, se_down, se_up, se_down.T, se_up.T, taps, gains]

    inner = []
    for h in range(CHUNKS):
        send = sends[h]
        if h > 0:
            send, _ = lax.optimization_barrier((send, received))
        received = lax.all_to_all(send, "enc", split_axis=0, concat_axis=0, tiled=True)
        if h == 0:
            received, *weights = lax.optimization_barrier((received, *weights))
        parts = route([received], table, info, h, per, columns, groups, False, h > 0)
        if h > 0:
            inner[-1], parts = lax.optimization_barrier((inner[-1], parts))
        inner.append(exchange(parts))

    carried = []
    arrived, small, narrowed, backs = [], [], [], []
    for h in range(CHUNKS):
        made = run_block(h, side, info, inner[h], token_grads, weights, carried, h == 0)
        carried = list(made[:4])
        small.append(made[-3:])
        narrowed.append(exchange(made[4:-3]))
    narrowed[0], carried = lax.optimization_barrier((narrowed[0], carried))
    for h in range(CHUNKS):
        back = route(narrowed[h], table, info, h, per, columns, groups, True)
        if h == 0:
            back, carried = lax.optimization_barrier((back, carried))
        arrived.append(lax.all_to_all(back, "enc", split_axis=0, concat_axis=0, tiled=True))
    visual, normed, scaled, hidden = carried
    tile_grads = unpack_and_spread(arrived, own, pos, local_tiles, grid)

    home, away = weight_terms(info, normed, scaled, hidden, token_grads, small, columns)
    near = lax.ppermute(away, "abs", partner_pairs(1, columns))
    pair = [(home[k].astype(F32) + near[k].astype(F32)).astype(BF16) for k in range(columns // 2)]
    rows = [pair[0]] + [
        lax.ppermute(pair[k], "abs", partner_pairs(2 * k, columns)) for k in range(1, columns // 2)
    ]
    column = sum(r.astype(F32) for r in rows).astype(BF16)
    spread = lax.all_to_all(column, "enc", split_axis=0, concat_axis=0, tiled=True)
    scale = 1.0 / math.sqrt(groups * local_tiles * cells)
    total = jnp.sum(spread.astype(F32), axis=0) * scale
    narrow = se_down.shape[1]
    ends = [width, 2 * width, 2 * width + narrow, 2 * width + 2 * narrow]
    last = total[:, ends[3] : ends[3] + 10]
    return (
        visual,
        tile_grads,
        total[:, : ends[0]],
        total[:, ends[0] : ends[1]],
        total[:, ends[1] : ends[2]],
        total[:, ends[2] : ends[3]].reshape(2, width),
        last[:, :9].T,
        last[:, 9],
    )


def solution(mesh):
    return jax.shard_map(
        local,
        mesh=mesh,
        in_specs=(
            P("enc", None, None, "abs"),
            P(),
            P(),
            P(),
            P(),
            P(),
            P(),
            P(("enc", "abs"), None, None),
            P(),
            P(),
            P(),
        ),
        out_specs=(
            P(("enc", "abs"), None, None),
            P("enc", None, None, "abs"),
            P(("enc", "abs"), None),
            P(("enc", "abs"), None),
            P(("enc", "abs"), None),
            P(("enc", "abs"), None),
            P(None, ("enc", "abs")),
            P(("enc", "abs")),
        ),
        check_vma=False,
    )
```

```python
import functools
import math

import jax
import jax.numpy as jnp
from jax import lax
from jax.experimental import pallas as pl
from jax.experimental.pallas import tpu as pltpu
from jax.sharding import PartitionSpec as P

F32 = jnp.float32
BF16 = jnp.bfloat16
NORM_EPS = 1e-06
LANES = 128
PAD = 16
CHUNKS = 2
VMEM_BYTES = 60 * 1024 * 1024
ANY = pl.BlockSpec(memory_space=pl.ANY)
SMEM = pl.BlockSpec(memory_space=pltpu.SMEM)
VMEM = pl.BlockSpec(memory_space=pltpu.VMEM)


def params(**more):
    return pltpu.CompilerParams(vmem_limit_bytes=VMEM_BYTES, **more)


def pool_kernel(steps, per, own_ref, pos_ref, tiles_ref, *rest):
    outs, (wide, pooled, sem) = rest[:CHUNKS], rest[CHUNKS:]
    step = pl.program_id(0)
    side = tiles_ref.shape[1] // 2
    width = 2 * side
    slots = outs[0].shape[1]
    for n in range(per):
        for row in range(side):
            pair = tiles_ref[n, 2 * row].astype(F32) + tiles_ref[n, 2 * row + 1].astype(F32)
            wide[pl.ds(row * width, width), :] = pair
        total = wide[pl.ds(0, side * side, stride=2), :] + wide[pl.ds(1, side * side, stride=2), :]
        j = step * per + n
        pooled[j] = (total * 0.25).astype(BF16)
        position = pos_ref[j]
        for h in range(CHUNKS):

            @pl.when(position // slots == h)
            def _(h=h):
                pltpu.make_async_copy(
                    pooled.at[j], outs[h].at[own_ref[j], position - h * slots], sem
                ).start()

    @pl.when(step == steps - 1)
    def _():
        @pl.loop(0, steps * per)
        def _(j):
            pltpu.make_async_copy(pooled.at[0], outs[0].at[0, 0], sem).wait()


def pool_and_pack(tiles, own, pos, groups, slots):
    count, grid, _, channels = tiles.shape
    cells = grid * grid // 4
    per = 16
    steps = count // per
    made = jax.ShapeDtypeStruct((groups, slots, cells, channels), BF16)
    return pl.pallas_call(
        functools.partial(pool_kernel, steps, per),
        grid=(steps,),
        in_specs=[SMEM, SMEM, pl.BlockSpec((per, grid, grid, channels), lambda i: (i, 0, 0, 0))],
        out_specs=[ANY] * CHUNKS,
        out_shape=[made] * CHUNKS,
        scratch_shapes=[
            pltpu.VMEM((grid * grid // 2, channels), F32),
            pltpu.VMEM((count, cells, channels), BF16),
            pltpu.SemaphoreType.DMA,
        ],
        compiler_params=params(),
        cost_estimate=pl.CostEstimate(flops=tiles.size, bytes_accessed=tiles.size * 3, transcendentals=0),
        name="pool_and_pack",
    )(own, pos, tiles)


def partner(me, step, columns, sign):
    ring = columns // 2
    z = lax.rem(me // 2 + sign * (step // 2) + ring, ring)
    return 2 * z + lax.rem(lax.rem(me, 2) + step % 2, 2)


def partner_pairs(step, columns):
    ring = columns // 2
    return [(n, 2 * ((n // 2 + step // 2) % ring) + (n % 2 + step) % 2) for n in range(columns)]


def exchange(parts):
    columns = len(parts)
    if columns == 1:
        return [lax.all_to_all(parts[0], "abs", split_axis=0, concat_axis=0, tiled=True)]
    return [parts[0]] + [lax.ppermute(parts[k], "abs", partner_pairs(k, columns)) for k in range(1, columns)]


def pick(refs, me, step, sign):
    if len(refs) > 1:
        return refs[step]
    return refs[0].at[partner(me, step, refs[0].shape[0], sign)]


def route_kernel(chunk, per, columns, back, table_ref, info_ref, *rest):
    (srcs, outs) = (rest[:-2], rest[-2:-1]) if back else (rest[:1], rest[1:-1])
    sem = rest[-1]
    filled, me = info_ref[0], info_ref[1]
    whole = outs[0] if back else srcs[0]
    slots = whole.shape[1]

    def each(act):
        for k in range(columns):
            first = partner(me, k, columns, -1 if back else 1) * per + chunk * slots
            part = pick(srcs, me, k, -1) if back else pick(outs, me, k, 1)

            @pl.loop(0, slots)
            def _(local, part=part, first=first):
                q = first + local

                @pl.when(q < filled)
                def _():
                    there = whole.at[table_ref[q], local]
                    here = part.at[local]
                    act(pltpu.make_async_copy(*((here, there) if back else (there, here)), sem))

    each(lambda one: one.start())
    each(lambda one: one.wait())


def parts_of(columns, shape, joined):
    if joined:
        return [jax.ShapeDtypeStruct((columns, *shape), BF16)]
    return [jax.ShapeDtypeStruct(shape, BF16)] * columns


def route(sources, table, info, chunk, per, columns, groups, back, joined=False):
    slots, cells, channels = sources[0].shape[-3:]
    parts = parts_of(columns, (slots, cells, channels), joined)
    whole = jax.ShapeDtypeStruct((groups, slots, cells, channels), BF16)
    return pl.pallas_call(
        functools.partial(route_kernel, chunk, per, columns, back),
        in_specs=[SMEM, SMEM] + [VMEM] * len(sources),
        out_specs=ANY if back else [ANY] * len(parts),
        out_shape=whole if back else parts,
        scratch_shapes=[pltpu.SemaphoreType.DMA],
        compiler_params=pltpu.CompilerParams(vmem_limit_bytes=52 * 1024 * 1024),
        cost_estimate=pl.CostEstimate(
            flops=0, bytes_accessed=8 * columns * slots * cells * channels, transcendentals=0
        ),
        name="route_back" if back else "route_in",
    )(table, info, *sources)


def exact_dot(left, weights):
    rows = left.shape[0]
    first = left.astype(BF16).astype(F32)
    rest = left - first
    second = rest.astype(BF16).astype(F32)
    third = rest - second
    stacked = jnp.concatenate([first, second, third, jnp.zeros_like(left)], axis=0).astype(BF16)
    made = jnp.dot(stacked, weights, preferred_element_type=F32)
    return made[:rows] + made[rows : 2 * rows] + made[2 * rows : 3 * rows]


def block_kernel(
    chunk,
    side,
    columns,
    parts_in,
    parts_out,
    info_ref,
    *rest,
):
    x_hbm, rest = rest[:parts_in], rest[parts_in:]
    up_hbm, w_in_hbm, w_out_hbm, w_in_t_hbm, w_out_t_hbm = rest[:5]
    se_down, se_up, se_down_t, se_up_t, taps, gain = rest[5:11]
    outs = rest[-24 - parts_out : -17]
    (vis_hbm, normed_hbm, scaled_hbm, hidden_hbm), back_hbm = outs[:4], outs[4 : 4 + parts_out]
    small_a, small_b, small_k = outs[4 + parts_out :]
    filled, me = info_ref[0], info_ref[1]
    live = filled - me * info_ref[2]
    (
        x,
        up,
        w_in,
        w_out,
        w_in_t,
        w_out_t,
        standard,
        inverse,
        slope_h,
        act,
        mixed,
        slope_s,
        wide,
        tmp,
        masks,
        stage,
        sem,
    ) = rest[-17:]
    (rows_v, squeeze, excite, extra, kacc, gacc, normed, scaled, vis) = stage
    blocks, tiles, cells, lanes = x.shape
    width = blocks * lanes
    flat = tiles * cells
    loads = [
        pltpu.make_async_copy(a, b, sem.at[n])
        for n, (a, b) in enumerate(
            [
                (w_in_hbm, w_in),
                (up_hbm.at[pl.ds(chunk * tiles, tiles)], up),
                (w_out_hbm, w_out),
                (w_out_t_hbm, w_out_t),
                (w_in_t_hbm, w_in_t),
            ]
        )
    ]
    x_loads = [
        pltpu.make_async_copy(pick(x_hbm, me, k, -1), x.at[partner(me, k, columns, -1)], sem.at[10 + k])
        for k in range(columns)
    ]
    for one in x_loads + loads:
        one.start()

    column = lax.rem(lax.broadcasted_iota(jnp.int32, (cells, lanes), 0), side)
    masks[0] = jnp.where(column != 0, 1.0, 0.0).astype(F32)
    masks[1] = jnp.where(column != side - 1, 1.0, 0.0).astype(F32)
    edge = jnp.zeros((PAD, lanes), F32)
    tmp[pl.ds(0, PAD), :] = edge
    tmp[pl.ds(PAD + cells, PAD), :] = edge
    kacc[...] = jnp.zeros_like(kacc)
    gacc[...] = jnp.zeros_like(gacc)
    squeeze[...] = jnp.zeros_like(squeeze)
    extra[...] = jnp.zeros_like(extra)

    @pl.loop(0, blocks * tiles)
    def _(n):
        c, t = n % blocks, n // blocks
        act[c, t, pl.ds(0, PAD), :] = edge
        act[c, t, pl.ds(PAD + cells, PAD), :] = edge

    for one in x_loads:
        one.wait()
    for t in range(tiles):

        @pl.when(chunk * tiles + t >= live)
        def _(t=t):
            for c in range(blocks):
                x[c, t] = jnp.zeros((cells, lanes), BF16)

    @pl.loop(0, tiles)
    def _(t):
        total = x[0, t].astype(F32)
        for c in range(1, blocks):
            total = total + x[c, t].astype(F32)
        average = jnp.sum(total, axis=1, keepdims=True) * (1.0 / width)
        square = jnp.zeros((cells, lanes), F32)
        for c in range(blocks):
            centred = x[c, t].astype(F32) - average
            square = square + centred * centred
        variance = jnp.sum(square, axis=1, keepdims=True) * (1.0 / width)
        inv = lax.rsqrt(variance + NORM_EPS)
        inverse[t] = jnp.broadcast_to(inv, (cells, lanes))
        for c in range(blocks):
            std = (x[c, t].astype(F32) - average) * inv
            standard[c, t] = std
            normed[t, :, c * lanes : (c + 1) * lanes] = (std * gain[c, 0:1, :]).astype(BF16)

    def product(left, right, put):
        wide_n = 256
        value = left[...].reshape(flat, width)
        for n in range(width // wide_n):
            made = jnp.dot(value, right[:, n * wide_n : (n + 1) * wide_n], preferred_element_type=F32)
            for half in range(wide_n // lanes):
                c = n * (wide_n // lanes) + half
                put(c, made[:, half * lanes : (half + 1) * lanes].reshape(tiles, cells, lanes))

    def put_hidden(c, value):
        slope_h[c] = value

    loads[0].wait()
    product(normed, w_in, put_hidden)
    save_normed = pltpu.make_async_copy(normed, normed_hbm.at[pl.ds(chunk * tiles, tiles)], sem.at[6])
    save_normed.start()

    @pl.loop(0, blocks * tiles)
    def _(n):
        c, t = n % blocks, n // blocks
        h = slope_h[c, t]
        sig = jax.nn.sigmoid(h)
        a = h * sig
        slope_h[c, t] = sig * (1.0 + h * (1.0 - sig))
        act[c, t, pl.ds(PAD, cells), :] = a

        def column_sum(b):
            made = None
            for r in range(3):
                term = taps[c, 3 * r + b : 3 * r + b + 1, :] * act[c, t, pl.ds(PAD + side * (r - 1) + b - 1, cells), :]
                made = term if made is None else made + term
            return made

        spatial = column_sum(1) + masks[0] * column_sum(0) + masks[1] * column_sum(2)
        sig = jax.nn.sigmoid(spatial)
        mix = spatial * sig
        mixed[c, t] = mix
        slope_s[c, t] = sig * (1.0 + spatial * (1.0 - sig))
        squeeze[c, pl.ds(t, 1), :] = jnp.sum(mix, axis=0, keepdims=True) * (1.0 / cells)

    def joined(ref):
        return jnp.concatenate([ref[c] for c in range(blocks)], axis=1)

    squeezed = joined(squeeze)
    squeeze_pre = exact_dot(squeezed, se_down[...])
    sig_pre = jax.nn.sigmoid(squeeze_pre)
    squeeze_act = squeeze_pre * sig_pre
    excited = jax.nn.sigmoid(exact_dot(squeeze_act, se_up[...]))
    for c in range(blocks):
        excite[c] = excited[:, c * lanes : (c + 1) * lanes]

    def put_back(c, value):
        wide[c] = value

    loads[1].wait()
    for t in range(tiles):

        @pl.when(chunk * tiles + t >= live)
        def _(t=t):
            up[t] = jnp.zeros(up.shape[1:], BF16)

    loads[3].wait()
    product(up, w_out_t, put_back)

    @pl.loop(0, tiles)
    def _(t):
        for c in range(blocks):
            mix = mixed[c, t]
            scaled[t, :, c * lanes : (c + 1) * lanes] = (mix * excite[c, pl.ds(t, 1), :]).astype(BF16)
            extra[c, pl.ds(t, 1), :] = jnp.sum(wide[c, t] * mix, axis=0, keepdims=True)

    back_pre = joined(extra) * excited * (1.0 - excited)
    back_squeeze_pre = exact_dot(back_pre, se_up_t[...]) * (
        sig_pre * (1.0 + squeeze_pre * (1.0 - sig_pre))
    )
    back_squeeze = exact_dot(back_squeeze_pre, se_down_t[...]) * (1.0 / cells)
    for c in range(blocks):
        extra[c] = back_squeeze[:, c * lanes : (c + 1) * lanes]
    small_a[0] = squeezed
    small_a[1] = back_pre
    small_b[0] = back_squeeze_pre
    small_b[1] = squeeze_act

    def put_visual(c, value):
        vis[:, :, c * lanes : (c + 1) * lanes] = (x[c].astype(F32) + value).astype(BF16)

    loads[2].wait()
    product(scaled, w_out, put_visual)
    save_scaled = pltpu.make_async_copy(scaled, scaled_hbm.at[pl.ds(chunk * tiles, tiles)], sem.at[7])
    save_scaled.start()
    save_vis = pltpu.make_async_copy(vis, vis_hbm.at[pl.ds(chunk * tiles, tiles)], sem.at[8])
    save_vis.start()
    save_normed.wait()

    @pl.loop(0, tiles)
    def _(t):
        for c in range(blocks):
            back = (wide[c, t] * excite[c, pl.ds(t, 1), :] + extra[c, pl.ds(t, 1), :]) * slope_s[c, t]
            tmp[pl.ds(PAD, cells), :] = back
            sides = (back * masks[0], back, back * masks[1])
            for r in range(3):
                for b in range(3):
                    term = sides[b] * act[c, t, pl.ds(PAD + side * (r - 1) + b - 1, cells), :]
                    kacc[c, 3 * r + b] += jnp.sum(term.reshape(cells // 8, 8, lanes), axis=0)

            def column_sum(b, c=c):
                made = None
                for r in range(3):
                    term = taps[c, 3 * r + b : 3 * r + b + 1, :] * tmp[pl.ds(PAD - side * (r - 1) - (b - 1), cells), :]
                    made = term if made is None else made + term
                return made

            back_act = column_sum(1) + masks[1] * column_sum(0) + masks[0] * column_sum(2)
            normed[t, :, c * lanes : (c + 1) * lanes] = (back_act * slope_h[c, t]).astype(BF16)

    loads[4].wait()
    product(normed, w_in_t, put_back)
    save_hidden = pltpu.make_async_copy(normed, hidden_hbm.at[pl.ds(chunk * tiles, tiles)], sem.at[9])
    save_hidden.start()

    @pl.loop(0, tiles)
    def _(t):
        centre = jnp.zeros((cells, lanes), F32)
        along = jnp.zeros((cells, lanes), F32)
        for c in range(blocks):
            along_n = wide[c, t] * standard[c, t]
            gacc[c] += jnp.sum(along_n.reshape(cells // 8, 8, lanes), axis=0)
            centre = centre + wide[c, t] * gain[c, 0:1, :]
            along = along + along_n * gain[c, 0:1, :]
        centre = jnp.sum(centre, axis=1, keepdims=True) * (1.0 / width)
        along = jnp.sum(along, axis=1, keepdims=True) * (1.0 / width)
        inv = inverse[t]
        for c in range(blocks):
            made = up[t, :, c * lanes : (c + 1) * lanes].astype(F32) + inv * (
                wide[c, t] * gain[c, 0:1, :] - centre - standard[c, t] * along
            )
            rows_v[c, t] = made.astype(BF16)

    save_back = [
        pltpu.make_async_copy(rows_v.at[partner(me, k, columns, 1)], pick(back_hbm, me, k, 1), sem.at[10 + columns + k])
        for k in range(columns)
    ]
    for one in save_back:
        one.start()
    small_k[...] = jnp.zeros_like(small_k)
    for c in range(blocks):
        for r in range(9):
            small_k[r : r + 1, c * lanes : (c + 1) * lanes] = jnp.sum(kacc[c, r], axis=0, keepdims=True)
        small_k[9:10, c * lanes : (c + 1) * lanes] = jnp.sum(gacc[c], axis=0, keepdims=True)
    save_scaled.wait()
    save_vis.wait()
    save_hidden.wait()
    for one in save_back:
        one.wait()


def run_block(chunk, side, info, x, up, weights, carried, joined):
    tiles, cells, lanes = x[0].shape[-3:]
    blocks = columns = up.shape[-1] // lanes
    backs = parts_of(columns, (tiles, cells, lanes), joined)
    size = blocks * tiles * cells * lanes
    width = blocks * lanes
    narrow = weights[4].shape[1]
    whole = jax.ShapeDtypeStruct(up.shape, BF16)
    fixed = [info, *x, up, *weights]
    field = pltpu.VMEM((blocks, tiles, cells, lanes), F32)
    packed = pltpu.VMEM((tiles, cells, width), BF16)
    eight = pltpu.VMEM((blocks, 8, lanes), F32)
    square = pltpu.VMEM((width, width), BF16)
    flops = 8 * tiles * cells * width * width
    return pl.pallas_call(
        functools.partial(block_kernel, chunk, side, columns, len(x), len(backs)),
        in_specs=[SMEM] + [ANY] * (len(x) + 5) + [VMEM] * 6 + [ANY] * len(carried),
        out_specs=[ANY] * (4 + len(backs)) + [VMEM] * 3,
        out_shape=[whole] * 4
        + backs
        + [
            jax.ShapeDtypeStruct((2, 8, width), F32),
            jax.ShapeDtypeStruct((2, 8, narrow), F32),
            jax.ShapeDtypeStruct((16, width), F32),
        ],
        input_output_aliases={len(fixed) + n: n for n in range(len(carried))},
        scratch_shapes=[
            pltpu.VMEM((blocks, tiles, cells, lanes), BF16),
            packed,
            square,
            square,
            square,
            square,
            field,
            pltpu.VMEM((tiles, cells, lanes), F32),
            field,
            pltpu.VMEM((blocks, tiles, cells + 2 * PAD, lanes), F32),
            field,
            field,
            field,
            pltpu.VMEM((cells + 2 * PAD, lanes), F32),
            pltpu.VMEM((2, cells, lanes), F32),
            [
                pltpu.VMEM((blocks, tiles, cells, lanes), BF16),
                eight,
                eight,
                eight,
                pltpu.VMEM((blocks, 9, 8, lanes), F32),
                eight,
                packed,
                packed,
                packed,
            ],
            pltpu.SemaphoreType.DMA((10 + 2 * columns,)),
        ],
        compiler_params=params(),
        cost_estimate=pl.CostEstimate(
            flops=flops, bytes_accessed=16 * size + 8 * width * width, transcendentals=2 * size
        ),
        name="block_%d" % chunk,
    )(*fixed, *carried)


def weights_kernel(chunks, columns, info_ref, normed, scaled, hidden, up, *rest):
    smalls, (home, away, held) = rest[: 5 * chunks], rest[5 * chunks :]
    count, cells, wide = normed.shape
    flat = count * cells
    width = hidden.shape[2]
    me = info_ref[1]
    ring = columns // 2
    made = []
    for left, right in ((normed, hidden), (scaled, up)):
        made.append(
            lax.dot_general(
                left[...].reshape(flat, wide),
                right[...].reshape(flat, width),
                (((0,), (0,)), ((), ())),
                preferred_element_type=F32,
            )
        )

    def outer(left, right):
        return lax.dot_general(
            jnp.concatenate(left, axis=0),
            jnp.concatenate(right, axis=0),
            (((0,), (0,)), ((), ())),
            preferred_element_type=F32,
            precision=lax.Precision.HIGHEST,
        )

    quarter = lax.rem(lax.broadcasted_iota(jnp.int32, (8, wide), 1), 4)
    pair = [lax.broadcasted_iota(jnp.int32, (16, LANES), n) for n in range(2)]
    same = jnp.where(pair[0] == pair[1], 1.0, 0.0).astype(F32)
    each = [smalls[5 * h : 5 * h + 5] for h in range(chunks)]
    narrow = each[0][2].shape[2]
    down = outer([e[0][0] for e in each], [e[2][0] for e in each])
    lift = outer(
        [jnp.where(quarter == m, e[3][...], 0.0) for e in each for m in range(4)],
        [e[1][0, :, m * narrow : (m + 1) * narrow] for e in each for m in range(4)],
    )
    taps = outer([sum(e[4][...] for e in each)], [same])
    place = 0
    for value in (*made, down, lift, taps):
        held[:, place : place + value.shape[1]] = value
        place += value.shape[1]
    for group in range(wide // (8 * columns)):
        for k in range(columns):
            row = pl.multiple_of(8 * (columns * group + partner(me, k, columns, 1)), 8)
            target = home if k % 2 == 0 else away
            target[k // 2, group] = held[pl.ds(row, 8), :].astype(BF16)


def weight_terms(info, normed, scaled, hidden, up, small, columns):
    count, cells, width = normed.shape
    narrow = small[0][1].shape[2]
    wide = 2 * LANES
    lanes = 2 * width + 2 * narrow + LANES
    groups = width // (8 * columns)
    per = wide // (8 * columns)
    left = pl.BlockSpec((count, cells, wide), lambda i: (0, 0, i))
    right = pl.BlockSpec((count, cells, width), lambda i: (0, 0, 0), pipeline_mode=pl.Buffered(1))
    args, specs = [], []
    for a, b, k in small:
        args += [a, a, b, jnp.repeat(b[1], 4, axis=1), k]
        specs += [
            pl.BlockSpec((1, 8, wide), lambda i: (0, 0, i)),
            pl.BlockSpec((1, 8, width), lambda i: (1, 0, 0)),
            pl.BlockSpec((1, 8, narrow), lambda i: (0, 0, 0)),
            pl.BlockSpec((8, wide), lambda i: (0, i)),
            pl.BlockSpec((16, wide), lambda i: (0, i)),
        ]
    part = jax.ShapeDtypeStruct((columns // 2, groups, 8, lanes), BF16)
    return pl.pallas_call(
        functools.partial(weights_kernel, len(small), columns),
        grid=(width // wide,),
        in_specs=[SMEM, left, left, right, right] + specs,
        out_specs=[pl.BlockSpec((columns // 2, per, 8, lanes), lambda i: (0, i, 0, 0))] * 2,
        out_shape=[part] * 2,
        scratch_shapes=[pltpu.VMEM((wide, lanes), F32)],
        compiler_params=params(),
        cost_estimate=pl.CostEstimate(
            flops=4 * count * cells * width * width, bytes_accessed=8 * count * cells * width, transcendentals=0
        ),
        name="weight_terms",
    )(info, normed, scaled, hidden, up, *args)


def spread_kernel(per, own_ref, pos_ref, *rest):
    arrived, (out, wide) = rest[:CHUNKS], rest[CHUNKS:]
    step = pl.program_id(0)
    slots = arrived[0].shape[1]
    side = out.shape[1] // 2
    width = 2 * side
    for n in range(per):
        group, position = own_ref[step * per + n], pos_ref[step * per + n]
        for h in range(CHUNKS):

            @pl.when(position // slots == h)
            def _(h=h):
                quarter = arrived[h][group, position - h * slots].astype(F32) * 0.25
                wide[n, pl.ds(0, side * side, stride=2), :] = quarter
                wide[n, pl.ds(1, side * side, stride=2), :] = quarter

        for row in range(side):
            line = wide[n, pl.ds(row * width, width), :].astype(BF16)
            out[n, 2 * row] = line
            out[n, 2 * row + 1] = line


def unpack_and_spread(arrived, own, pos, count, grid):
    _, _, cells, channels = arrived[0].shape
    per = 4
    return pl.pallas_call(
        functools.partial(spread_kernel, per),
        grid=(count // per,),
        in_specs=[SMEM, SMEM]
        + [pl.BlockSpec(a.shape, lambda i: (0, 0, 0, 0), pipeline_mode=pl.Buffered(1)) for a in arrived],
        out_specs=pl.BlockSpec((per, grid, grid, channels), lambda i: (i, 0, 0, 0)),
        out_shape=jax.ShapeDtypeStruct((count, grid, grid, channels), BF16),
        scratch_shapes=[pltpu.VMEM((per, grid * grid // 2, channels), F32)],
        compiler_params=pltpu.CompilerParams(vmem_limit_bytes=24 * 1024 * 1024),
        cost_estimate=pl.CostEstimate(
            flops=0, bytes_accessed=10 * count * cells * channels, transcendentals=0
        ),
        name="unpack_and_spread",
    )(own, pos, *arrived)


def routing(counts, owners, ranks, group_id, local_tiles, capacity):
    groups = counts.shape[0]
    flat_counts, flat_owners, flat_ranks = counts.reshape(-1), owners.reshape(-1), ranks.reshape(-1)
    sources = jnp.arange(groups, dtype=jnp.int32)
    mine = (sources == group_id)[:, None]

    def row(table):
        return jnp.sum(jnp.where(mine, table, 0), axis=0, dtype=jnp.int32)

    owner_row, rank_row, count_row = row(owners), row(ranks), row(counts)
    start_row = jnp.sum(jnp.where(sources[None, :] < sources[:, None], count_row[None, :], 0), axis=1, dtype=jnp.int32)
    ahead = (owner_row[:, None] == flat_owners[None, :]) & (flat_ranks[None, :] < rank_row[:, None])
    offset_row = jnp.sum(jnp.where(ahead, flat_counts[None, :], 0), axis=1, dtype=jnp.int32)
    ids = jnp.arange(local_tiles, dtype=jnp.int32)
    member = jnp.sum((start_row[None, :] <= ids[:, None]).astype(jnp.int32), axis=1, dtype=jnp.int32) - 1
    which = member[:, None] == sources[None, :]
    own = jnp.sum(jnp.where(which, owner_row[None, :], 0), axis=1, dtype=jnp.int32)
    slot = jnp.sum(jnp.where(which, (offset_row - start_row)[None, :], 0), axis=1, dtype=jnp.int32) + ids
    arriving = owners == group_id
    recv_count = jnp.sum(jnp.where(arriving, counts, 0), axis=1, dtype=jnp.int32)
    recv_rank = jnp.sum(jnp.where(arriving, ranks, 0), axis=1, dtype=jnp.int32)
    earlier = recv_rank[None, :] < recv_rank[:, None]
    recv_offset = jnp.sum(jnp.where(earlier, recv_count[None, :], 0), axis=1, dtype=jnp.int32)
    positions = jnp.arange(capacity, dtype=jnp.int32)
    inside = (positions[:, None] >= recv_offset[None, :]) & (
        positions[:, None] < (recv_offset + recv_count)[None, :]
    )
    table = jnp.sum(jnp.where(inside, sources[None, :], 0), axis=1, dtype=jnp.int32)
    filled = jnp.sum(recv_count, dtype=jnp.int32).reshape(1)
    return own, slot, table, filled


def local(
    tiles,
    w_in,
    w_out,
    se_down,
    se_up,
    kernel,
    gain,
    token_grads,
    tile_counts,
    sample_owner,
    sample_rank,
):
    groups = lax.axis_size("enc")
    columns = lax.axis_size("abs")
    group_id = lax.axis_index("enc")
    column_id = lax.axis_index("abs")
    local_tiles, grid = tiles.shape[0], tiles.shape[1]
    per, cells, width = token_grads.shape
    capacity = per * columns
    side = grid // 2
    slots = per // CHUNKS
    blocks = width // LANES
    own, slot, table, filled = routing(
        tile_counts, sample_owner, sample_rank, group_id, local_tiles, capacity
    )
    pos = slot % per
    info = jnp.stack([filled[0], column_id.astype(jnp.int32), jnp.int32(per)])
    sends = pool_and_pack(tiles, own, pos, groups, slots)

    taps = jnp.pad(kernel.astype(F32).reshape(9, blocks, LANES).transpose(1, 0, 2), ((0, 0), (0, 7), (0, 0)))
    gains = jnp.broadcast_to(gain.astype(F32).reshape(blocks, 1, LANES), (blocks, 8, LANES))
    weights = [w_in, w_out, w_in.T, w_out.T, se_down, se_up, se_down.T, se_up.T, taps, gains]

    inner = []
    for h in range(CHUNKS):
        send = sends[h]
        if h > 0:
            send, _ = lax.optimization_barrier((send, received))
        received = lax.all_to_all(send, "enc", split_axis=0, concat_axis=0, tiled=True)
        if h == 0:
            received, *weights = lax.optimization_barrier((received, *weights))
        parts = route([received], table, info, h, per, columns, groups, False, h > 0)
        if h > 0:
            inner[-1], parts = lax.optimization_barrier((inner[-1], parts))
        inner.append(exchange(parts))

    carried = []
    arrived, small, narrowed, backs = [], [], [], []
    for h in range(CHUNKS):
        made = run_block(h, side, info, inner[h], token_grads, weights, carried, h == 0)
        carried = list(made[:4])
        small.append(made[-3:])
        narrowed.append(exchange(made[4:-3]))
    narrowed[0], carried = lax.optimization_barrier((narrowed[0], carried))
    for h in range(CHUNKS):
        back = route(narrowed[h], table, info, h, per, columns, groups, True)
        if h == 0:
            back, carried = lax.optimization_barrier((back, carried))
        arrived.append(lax.all_to_all(back, "enc", split_axis=0, concat_axis=0, tiled=True))
    visual, normed, scaled, hidden = carried
    tile_grads = unpack_and_spread(arrived, own, pos, local_tiles, grid)

    home, away = weight_terms(info, normed, scaled, hidden, token_grads, small, columns)
    near = lax.ppermute(away, "abs", partner_pairs(1, columns))
    pair = [(home[k].astype(F32) + near[k].astype(F32)).astype(BF16) for k in range(columns // 2)]
    rows = [pair[0]] + [
        lax.ppermute(pair[k], "abs", partner_pairs(2 * k, columns)) for k in range(1, columns // 2)
    ]
    column = sum(r.astype(F32) for r in rows).astype(BF16)
    spread = lax.all_to_all(column, "enc", split_axis=0, concat_axis=0, tiled=True)
    scale = 1.0 / math.sqrt(groups * local_tiles * cells)
    total = jnp.sum(spread.astype(F32), axis=0) * scale
    narrow = se_down.shape[1]
    ends = [width, 2 * width, 2 * width + narrow, 2 * width + 2 * narrow]
    last = total[:, ends[3] : ends[3] + 10]
    return (
        visual,
        tile_grads,
        total[:, : ends[0]],
        total[:, ends[0] : ends[1]],
        total[:, ends[1] : ends[2]],
        total[:, ends[2] : ends[3]].reshape(2, width),
        last[:, :9].T,
        last[:, 9],
    )


def solution(mesh):
    return jax.shard_map(
        local,
        mesh=mesh,
        in_specs=(
            P("enc", None, None, "abs"),
            P(),
            P(),
            P(),
            P(),
            P(),
            P(),
            P(("enc", "abs"), None, None),
            P(),
            P(),
            P(),
        ),
        out_specs=(
            P(("enc", "abs"), None, None),
            P("enc", None, None, "abs"),
            P(("enc", "abs"), None),
            P(("enc", "abs"), None),
            P(("enc", "abs"), None),
            P(("enc", "abs"), None),
            P(None, ("enc", "abs")),
            P(("enc", "abs")),
        ),
        check_vma=False,
    )
```
